32 devices in a mesh: fsdp: 2 (over y), ctx: 4 (over z), tp: 4 (over x, core).
Axes of the slice: x: 2, y: 2, z: 4, core: 2. Of those that a mesh axis runs over, the one named last changes fastest.
Arguments:
- block_input: bfloat16 [4096, 768], P(('fsdp', 'ctx')), may hold values from -6 to 6
- cotangent: bfloat16 [4096, 768], P(('fsdp', 'ctx')), may hold values from -6 to 6
- route_perm: int32 [4096], P('fsdp'), may hold values from 0 to 4095, as said below
- doc_lengths: int32 [2, 4], P('fsdp'), may hold values from 1 to 1024, 2048 in all within a row
- norm_gain: float32 [768], replicated, may hold values from 0.5 to 1.5
- in_proj: float32 [1536, 2, 768], P(('tp', 'fsdp', 'ctx')), may hold values from -0.21875 to 0.21875
- conv_weight: float32 [4, 1536], replicated, may hold values from -3 to 3
- conv_bias: float32 [1536], replicated, may hold values from -3 to 3
- x_proj: float32 [1536, 80], P(('tp', 'fsdp', 'ctx')), may hold values from -0.15625 to 0.15625
- dt_proj: float32 [1536, 48], P(('tp', 'fsdp', 'ctx')), may hold values from -0.875 to 0.875
- dt_bias: float32 [1536], replicated, may hold values from -6.9 to -2.3
- a_log: float32 [16, 1536], replicated, may hold values from -1 to 2.8
- skip_gain: float32 [1536], replicated, may hold values from 0.5 to 1.5
- out_proj: float32 [1536, 768], P(('tp', 'fsdp', 'ctx')), may hold values from -0.15625 to 0.15625
- in_momentum: float32 [1536, 2, 768], P(('tp', 'fsdp', 'ctx')), may hold values from -20 to 20
- x_momentum: float32 [1536, 80], P(('tp', 'fsdp', 'ctx')), may hold values from -20 to 20
- dt_momentum: float32 [1536, 48], P(('tp', 'fsdp', 'ctx')), may hold values from -20 to 20
- out_momentum: float32 [1536, 768], P(('tp', 'fsdp', 'ctx')), may hold values from -20 to 20
- adam_first: float32 [36096], replicated, may hold values from -6 to 6
- adam_second: float32 [36096], replicated, may hold values from 0.1024 to 10.24
- adam_step: int32 [1], replicated, may hold values from 1 to 20
Outputs:
- block_out: bfloat16 [4096, 768], P(('fsdp', 'ctx'))
- input_grad: bfloat16 [4096, 768], P(('fsdp', 'ctx'))
- grad_gain: float32 [768], replicated
- grad_in_proj: float32 [1536, 2, 768], P(('tp', 'fsdp', 'ctx'))
- grad_conv_weight: float32 [4, 1536], replicated
- grad_conv_bias: float32 [1536], replicated
- grad_x_proj: float32 [1536, 80], P(('tp', 'fsdp', 'ctx'))
- grad_dt_proj: float32 [1536, 48], P(('tp', 'fsdp', 'ctx'))
- grad_dt_bias: float32 [1536], replicated
- grad_a_log: float32 [16, 1536], replicated
- grad_skip: float32 [1536], replicated
- grad_out_proj: float32 [1536, 768], P(('tp', 'fsdp', 'ctx'))
- new_gain: float32 [768], replicated
- new_in_proj: float32 [1536, 2, 768], P(('tp', 'fsdp', 'ctx'))
- new_conv_weight: float32 [4, 1536], replicated
- new_conv_bias: float32 [1536], replicated
- new_x_proj: float32 [1536, 80], P(('tp', 'fsdp', 'ctx'))
- new_dt_proj: float32 [1536, 48], P(('tp', 'fsdp', 'ctx'))
- new_dt_bias: float32 [1536], replicated
- new_a_log: float32 [16, 1536], replicated
- new_skip: float32 [1536], replicated
- new_out_proj: float32 [1536, 768], P(('tp', 'fsdp', 'ctx'))
- new_in_momentum: float32 [1536, 2, 768], P(('tp', 'fsdp', 'ctx'))
- new_x_momentum: float32 [1536, 80], P(('tp', 'fsdp', 'ctx'))
- new_dt_momentum: float32 [1536, 48], P(('tp', 'fsdp', 'ctx'))
- new_out_momentum: float32 [1536, 768], P(('tp', 'fsdp', 'ctx'))
- new_adam_first: float32 [36096], replicated
- new_adam_second: float32 [36096], replicated
The draws below stay inside these ranges and needn't reach their ends.
Inputs may be any that keep to these rules, and one draw needn't show every extreme that they name: route_perm is a permutation of 0 .. 4095 that maps the arrival rows of stream r onto positions of stream r; each aligned block of 512 arrival rows sends exactly 128 rows to each aligned block of 512 positions of its stream. `doc_lengths`: each row sums to 2048; its longest document has exactly 1024 positions.
All inputs are finite; a program needn't handle non-finite values.
Results may differ from the reference program's by a relative error of at most 0.006.
The reference program's roundings to bfloat16 on the way count: a program that leaves them out, or rounds other values in their place, can miss the bound.
Values may be sent and summed in bfloat16 or wider, within the bound.
No kernel may reach another device: no remote copies, remote signals or barrier semaphores. Data moves between devices by JAX's collectives and lax.ppermute only.
A program may use at most 256 MiB of HBM per device.

```python
import math
from functools import partial
import jax
import jax.numpy as jnp
import numpy as np
from jax import lax

D = 768
INNER = 1536
NSTATE = 16
RANK = 48
KW = 4
MAXLEN = 1024
TOK_DEV = 512
XW = 80
STREAM = 2048
DOCS = 4
ROWS = 2
TOKENS = 4096
VEC = 36096


def draw_route_perm(key, part):
    blocks = TOKENS // TOK_DEV
    ctx_blocks = STREAM // TOK_DEV
    share_rows = TOK_DEV // ctx_blocks
    first_key, second_key = jax.random.split(jax.random.fold_in(key, 7))

    def block_orders(sub_key):
        scores = jax.random.randint(sub_key, (blocks, TOK_DEV), 0, 32768)
        scores = scores * TOK_DEV + jnp.arange(TOK_DEV, dtype=jnp.int32)[None, :]
        return jnp.argsort(scores, axis=1).astype(jnp.int32)
    source_lists = block_orders(first_key)
    slot_lists = block_orders(second_key)
    rank_in_list = jnp.argsort(source_lists, axis=1).astype(jnp.int32)
    dest_ctx = rank_in_list // share_rows
    within = rank_in_list % share_rows
    block_ids = jnp.arange(blocks, dtype=jnp.int32)[:, None]
    dest_block = block_ids // ctx_blocks * ctx_blocks + dest_ctx
    slot_index = slot_lists[dest_block, block_ids % ctx_blocks * share_rows + within]
    return (dest_block * TOK_DEV + slot_index).reshape(TOKENS).astype(jnp.int32)


def shard_levels(stream_key, shape, cuts, low, largest):
    gain, own = 1.0, jax.random.fold_in(stream_key, 6)
    for axis_at, blocks in cuts:
        heights = jnp.exp(jax.random.uniform(jax.random.fold_in(own, axis_at), (blocks,), jnp.float32, low / len(cuts), largest / len(cuts)))
        gain = gain * jnp.repeat(heights, shape[axis_at] // blocks).reshape([-1 if axis == axis_at else 1 for axis in range(len(shape))])
    return gain


def profile(count, total, most, skew):
    weights = [(1 << 20) // math.isqrt(standing ** skew) + 1 for standing in range(2, count + 1)]
    spare, counts = total - most - (count - 1), [1] * (count - 1)
    while spare > 0:
        free = [i for i in range(count - 1) if counts[i] < most]
        whole, budget = sum([weights[i] for i in free]), spare
        for i in free:
            extra = min(most - counts[i], max(1, budget * weights[i] // whole), spare)
            counts[i] = counts[i] + extra
            spare = spare - extra
    return np.array([most] + counts)


def uneven(stream_key, number_of, total, reach, skew):
    if number_of == 2:
        one = jax.random.randint(stream_key, (), max(1, total - reach), min(reach, total - 1) + 1)
        return jnp.stack([one, total - one])
    sizes = jnp.asarray(profile(number_of, total, reach, skew), jnp.int32)
    pairs = (number_of - 1) // 2
    source_of, sink = sizes[1:1 + 2 * pairs:2], sizes[2:2 + 2 * pairs:2]
    margin = jnp.minimum(source_of - 1, reach - sink)
    shifted = jax.random.randint(jax.random.fold_in(stream_key, 1), (pairs,), 0, 1 << 20) % (margin + 1)
    sizes = sizes.at[1:1 + 2 * pairs:2].set(source_of - shifted).at[2:2 + 2 * pairs:2].set(sink + shifted)
    return sizes[jax.random.permutation(jax.random.fold_in(stream_key, 2), number_of)]


def noise(own_key, shape, scale, reach, cuts=(), kind=jnp.bfloat16):
    entries = scale * jax.random.normal(own_key, shape, jnp.float32)
    if cuts:
        entries = entries * shard_levels(own_key, shape, cuts, -0.22, 0.18)
    return jnp.clip(entries, -reach, reach).astype(kind)


def setup_inputs(seed: int = 0) -> dict:
    keys = jax.random.split(jax.random.key(seed), 22)
    return {
        "block_input": noise(keys[0], (TOKENS, D), 1.0, 6.0, ((0, 8),)),
        "cotangent": noise(keys[1], (TOKENS, D), 1.0, 6.0, ((0, 8),)),
        "route_perm": draw_route_perm(jax.random.fold_in(keys[21], 71), 0),
        "doc_lengths": jax.vmap(lambda own: uneven(own, DOCS, STREAM, MAXLEN, 2))(jax.random.split(keys[3], ROWS)).reshape((ROWS, DOCS)).astype(jnp.int32),
        "norm_gain": jnp.clip(1.0 + 0.1 * jax.random.normal(keys[4], (D,), jnp.float32), 0.5, 1.5),
        "in_proj": noise(keys[5], (INNER, 2, D), D ** -0.5, 0.21875, ((0, 32),), jnp.float32),
        "conv_weight": noise(keys[6], (KW, INNER), KW ** -0.5, 3.0, (), jnp.float32),
        "conv_bias": noise(keys[7], (INNER,), 0.5, 3.0, (), jnp.float32),
        "x_proj": noise(keys[8], (INNER, XW), INNER ** -0.5, 0.15625, ((0, 32),), jnp.float32),
        "dt_proj": noise(keys[9], (INNER, RANK), RANK ** -0.5, 0.875, ((0, 32),), jnp.float32),
        "dt_bias": jnp.clip(jax.random.uniform(keys[10], (INNER,), jnp.float32, -6.9, -2.3), -6.9, -2.3),
        "a_log": jnp.clip(jax.random.uniform(keys[11], (NSTATE, INNER), jnp.float32, -1.0, 2.8), -1.0, 2.8),
        "skip_gain": jnp.clip(jax.random.uniform(keys[12], (INNER,), jnp.float32, 0.5, 1.5), 0.5, 1.5),
        "out_proj": noise(keys[13], (INNER, D), INNER ** -0.5, 0.15625, ((0, 32),), jnp.float32),
        "in_momentum": noise(keys[14], (INNER, 2, D), (0.05 * TOKENS ** 0.5), 20.0, ((0, 32),), jnp.float32),
        "x_momentum": noise(keys[15], (INNER, XW), (0.05 * TOKENS ** 0.5), 20.0, ((0, 32),), jnp.float32),
        "dt_momentum": noise(keys[16], (INNER, RANK), (0.05 * TOKENS ** 0.5), 20.0, ((0, 32),), jnp.float32),
        "out_momentum": noise(keys[17], (INNER, D), (0.05 * TOKENS ** 0.5), 20.0, ((0, 32),), jnp.float32),
        "adam_first": noise(keys[18], (VEC,), (0.01 * TOKENS ** 0.5), 6.0, (), jnp.float32),
        "adam_second": jnp.clip(jnp.exp(jax.random.uniform(keys[19], (VEC,), jnp.float32, math.log(0.1024), math.log(10.24))), 0.1024, 10.24),
        "adam_step": jax.random.randint(keys[20], (1,), 1, 21).astype(jnp.int32),
    }


@jax.custom_vjp
def low(v):
    return lax.optimization_barrier(v.astype(jnp.bfloat16)).astype(jnp.float32)

@jax.custom_vjp
def low_back(v):
    return v

def low_keep(v):
    return (low(v), None)

def low_pass(kept, grad):
    return (grad,)

def back_keep(v):
    return (v, None)

def back_low(kept, grad):
    return (low(grad),)
low.defvjp(low_keep, low_pass)
low_back.defvjp(back_keep, back_low)
HIGH = lax.Precision.HIGHEST
NS_A = 3.4445
NS_B = -4.775
NS_C = 2.0315
MOMENTUM = 0.95
MUON_RATE = 0.1
ADAM_RATE = 0.25
BETA_ONE = 0.9
BETA_TWO = 0.95
ADAM_EPS = 1e-08
DECAY_RATE = 0.01
NORM_EPS = 1e-05

def pair_combine(earlier, latter):
    return (earlier[0] * latter[0], latter[0] * earlier[1] + latter[1])

def doc_masks(doc_lengths):
    offsets = (jnp.cumsum(doc_lengths, axis=1) - doc_lengths).astype(jnp.int32)
    positions = jnp.arange(STREAM, dtype=jnp.int32)
    starts = lax.optimization_barrier(jnp.max(jnp.where(offsets[:, None, :] <= positions[None, :, None], offsets[:, None, :], 0), axis=2)).astype(jnp.int32)
    tap_masks = jnp.stack([positions[None, :] - (KW - 1 - tap_index) >= starts for tap_index in range(KW)], axis=2).astype(jnp.float32)
    keep_mask = (positions[None, :] != starts).astype(jnp.float32)
    return (tap_masks, keep_mask)

def mixer_scan(deltas, b_coef, c_coef, act_float, keep_mask, a_mat):
    block_len = min(128, STREAM)
    block_count = STREAM // block_len

    def scan_block(carry_state, item):
        delta_blk, b_blk, c_blk, act_blk, keep_blk = item
        decays = jnp.exp(delta_blk[:, None, :] * a_mat[None]) * keep_blk[:, None, None]
        drives = delta_blk[:, None, :] * b_blk[:, :, None] * act_blk[:, None, :]
        a_prefix, h_local = lax.associative_scan(pair_combine, (decays, drives), axis=0)
        states = h_local + a_prefix * carry_state[None]
        return (states[-1], lax.optimization_barrier(jnp.sum(c_blk[:, :, None] * states, axis=1)))
    scan_block = jax.checkpoint(scan_block)

    def split_blocks(array):
        return array.reshape((block_count, block_len) + array.shape[1:])

    def one_stream(item):
        delta_row, b_row, c_row, act_row, keep_row = item
        start_state = jnp.zeros((NSTATE, INNER), jnp.float32)
        _, outputs = lax.scan(scan_block, start_state, (split_blocks(delta_row), split_blocks(b_row), split_blocks(c_row), split_blocks(act_row), split_blocks(keep_row)))
        return outputs.reshape(STREAM, INNER)
    return lax.map(one_stream, (deltas, b_coef, c_coef, act_float, keep_mask))

def block_forward(stream_x, norm_gain, in_proj, conv_weight, conv_bias, x_proj, dt_proj, dt_bias, a_log, skip_gain, out_proj, tap_masks, keep_mask):
    inv_rms = lax.rsqrt(lax.optimization_barrier(jnp.mean(stream_x * stream_x, axis=1, keepdims=True)) + NORM_EPS)
    normed = low(stream_x * inv_rms * norm_gain)
    mixed_in = jnp.einsum('td,cqd->tqc', normed, low(in_proj), precision=HIGH)
    mixed_in = low_back(low(mixed_in))
    conv_in = mixed_in[:, 0, :].reshape(ROWS, STREAM, INNER)
    gate_in = mixed_in[:, 1, :]
    padded = jnp.pad(conv_in, ((0, 0), (KW - 1, 0), (0, 0)))
    conv_out = conv_bias + jnp.zeros((ROWS, STREAM, INNER), jnp.float32)
    for tap_index in range(KW):
        conv_out = conv_out + conv_weight[tap_index] * padded[:, tap_index:tap_index + STREAM] * tap_masks[:, :, tap_index:tap_index + 1]
    conv_out = conv_out.reshape(TOKENS, INNER)
    conv_act = low(jax.nn.silu(conv_out))
    proj_full = low_back(jnp.dot(conv_act, low(x_proj), precision=HIGH))
    rank_low = low(proj_full[:, :RANK])
    b_coef = proj_full[:, RANK:RANK + NSTATE]
    c_coef = proj_full[:, RANK + NSTATE:]
    dt_lin = low_back(jnp.dot(rank_low, low(dt_proj).T, precision=HIGH))
    deltas = jax.nn.softplus(dt_lin + dt_bias)
    a_mat = -jnp.exp(a_log)
    scanned = mixer_scan(deltas.reshape(ROWS, STREAM, INNER), b_coef.reshape(ROWS, STREAM, NSTATE), c_coef.reshape(ROWS, STREAM, NSTATE), conv_act.reshape(ROWS, STREAM, INNER), keep_mask, a_mat)
    y_inner = scanned.reshape(TOKENS, INNER) + skip_gain * conv_act
    gate_low = low(y_inner * jax.nn.silu(gate_in))
    return stream_x + jnp.dot(gate_low, low(out_proj), precision=HIGH)

def ns_factor(gram_matrix):
    size_n = gram_matrix.shape[0]
    identity = jnp.eye(size_n, dtype=jnp.float32)
    scale_norm = jnp.sqrt(jnp.trace(gram_matrix)) + 1e-07
    factor = identity / scale_norm
    current = gram_matrix / (scale_norm * scale_norm)
    for step_index in range(5):
        polynomial = NS_B * current + NS_C * jnp.dot(current, current, precision=HIGH)
        factor = jnp.dot(factor, NS_A * identity + polynomial, precision=HIGH)
        if step_index < 4:
            current = jnp.dot(factor.T, jnp.dot(gram_matrix, factor, precision=HIGH), precision=HIGH)
    return factor

def muon_step(weight, gradient, momentum_old):
    momentum_new = MOMENTUM * momentum_old + gradient
    update = gradient + MOMENTUM * momentum_new
    gram_matrix = jnp.dot(update.T, update, precision=HIGH)
    ortho = jnp.dot(update, ns_factor(gram_matrix), precision=HIGH)
    scale_factor = 0.2 * math.sqrt(max(weight.shape[0], weight.shape[1]))
    return (weight - MUON_RATE * scale_factor * ortho, momentum_new)

def adam_update(parameters, gradient, moment_one, moment_two, adam_step):
    count = adam_step[0].astype(jnp.float32)
    first_new = BETA_ONE * moment_one + (1.0 - BETA_ONE) * gradient
    second_new = BETA_TWO * moment_two + (1.0 - BETA_TWO) * gradient * gradient
    first_hat = first_new / (1.0 - jnp.power(jnp.float32(BETA_ONE), count))
    second_hat = second_new / (1.0 - jnp.power(jnp.float32(BETA_TWO), count))
    updated = parameters - ADAM_RATE * (first_hat / (jnp.sqrt(second_hat) + ADAM_EPS) + DECAY_RATE * parameters)
    return (updated, first_new, second_new)

def reference(block_input, cotangent, route_perm, doc_lengths, norm_gain, in_proj, conv_weight, conv_bias, x_proj, dt_proj, dt_bias, a_log, skip_gain, out_proj, in_momentum, x_momentum, dt_momentum, out_momentum, adam_first, adam_second, adam_step):
    order = jnp.argsort(route_perm).astype(jnp.int32)
    stream_x = block_input[order].astype(jnp.float32)
    stream_dy = cotangent[order].astype(jnp.float32)
    tap_masks, keep_mask = doc_masks(doc_lengths)
    forward = partial(block_forward, tap_masks=tap_masks, keep_mask=keep_mask)
    out_stream, pull_back = jax.vjp(forward, stream_x, norm_gain, in_proj, conv_weight, conv_bias, x_proj, dt_proj, dt_bias, a_log, skip_gain, out_proj)
    grads = pull_back(stream_dy)
    block_out = out_stream.astype(jnp.bfloat16)[route_perm]
    input_grad = grads[0].astype(jnp.bfloat16)[route_perm]
    g_gain, g_in, g_kernel, g_cbias, g_x, g_dt, g_dtb, g_alog, g_skip, g_out = grads[1:]
    new_in, mom_in = muon_step(in_proj.reshape(2 * INNER, D), g_in.reshape(2 * INNER, D), in_momentum.reshape(2 * INNER, D))
    new_x, mom_x = muon_step(x_proj, g_x, x_momentum)
    new_dt, mom_dt = muon_step(dt_proj, g_dt, dt_momentum)
    new_out, mom_out = muon_step(out_proj, g_out, out_momentum)
    vec_params = jnp.concatenate([norm_gain, conv_weight.reshape(-1), conv_bias, dt_bias, a_log.reshape(-1), skip_gain])
    vec_grads = jnp.concatenate([g_gain, g_kernel.reshape(-1), g_cbias, g_dtb, g_alog.reshape(-1), g_skip])
    new_vec, first_new, second_new = adam_update(vec_params, vec_grads, adam_first, adam_second, adam_step)
    cut_a = D
    cut_b = cut_a + KW * INNER
    cut_c = cut_b + INNER
    cut_d = cut_c + INNER
    cut_e = cut_d + NSTATE * INNER
    return (block_out, input_grad, g_gain, g_in, g_kernel, g_cbias, g_x, g_dt, g_dtb, g_alog, g_skip, g_out, new_vec[:cut_a], new_in.reshape(INNER, 2, D), new_vec[cut_a:cut_b].reshape(KW, INNER), new_vec[cut_b:cut_c], new_x, new_dt, new_vec[cut_c:cut_d], new_vec[cut_d:cut_e].reshape(NSTATE, INNER), new_vec[cut_e:], new_out, mom_in.reshape(INNER, 2, D), mom_x, mom_dt, mom_out, first_new, second_new)
```

```python
import math

import jax
import jax.numpy as jnp
from jax import lax
from jax.experimental import pallas as pl
from jax.experimental.pallas import tpu as pltpu
from jax.sharding import PartitionSpec as P

F32 = jnp.float32
BF = jnp.bfloat16
LANES = 128
RESET = 1e5
VMEM_LIMIT = 60 * 1024 * 1024


def dot_nn(a, b):
    return lax.dot_general(a, b, (((1,), (0,)), ((), ())), preferred_element_type=F32)


def dot_nt(a, b):
    return lax.dot_general(a, b, (((1,), (1,)), ((), ())), preferred_element_type=F32)


def dot_tn(a, b):
    return lax.dot_general(a, b, (((0,), (0,)), ((), ())), preferred_element_type=F32)


def soft(x):
    return jnp.maximum(x, 0.0) + jnp.log1p(jnp.exp(-jnp.abs(x)))


def slope_of(a, s):
    return s * (1.0 + a * (1.0 - s))


def call(body, outs, n_in, n_smem, scratch=(), flops=10**9):
    specs = [pl.BlockSpec(memory_space=pltpu.SMEM)] * n_smem + [
        pl.BlockSpec(memory_space=pltpu.VMEM)
    ] * (n_in - n_smem)
    return pl.pallas_call(
        body,
        out_shape=[jax.ShapeDtypeStruct(s, d) for s, d in outs],
        in_specs=specs,
        out_specs=[pl.BlockSpec(memory_space=pltpu.VMEM)] * len(outs),
        scratch_shapes=list(scratch),
        compiler_params=pltpu.CompilerParams(vmem_limit_bytes=VMEM_LIMIT),
        name=body.__name__,
    )


def rows_iota(r0, rows):
    return lax.broadcasted_iota(jnp.int32, (rows, LANES), 0) + r0


def tap_mask(sc_ref, docs, p, shift):
    ok = jnp.ones(p.shape, F32)
    for j in range(docs):
        off = sc_ref[1 + j]
        ok = jnp.where((off <= p) & (p < off + shift), 0.0, ok)
    return ok


def wide(mask, width):
    return jnp.concatenate([mask] * (width // LANES), axis=1)


def make_front(T, C, D, docs, XW, R):
    RB = 64

    def front(sc, hb, halo, dy, w, cw, cb, xu_o, z_o, u_o, v_o, pt_o, dg_o, wt_o, xpad):
        w0 = w[:, 0:D]
        w1 = w[:, D : 2 * D]
        wo = w[:, 2 * D + LANES : 3 * D + LANES]
        wt = w[:, 2 * D : 2 * D + LANES].astype(F32).T.astype(BF)
        wt_o[...] = wt
        c0 = pl.multiple_of(sc[0], LANES)
        xpad[0:8, :] = dot_nt(halo[...], w0).astype(BF).astype(F32)
        xu = dot_nt(hb[...], w0).astype(BF)
        xu_o[...] = xu
        xpad[8 : 8 + T, :] = xu.astype(F32)
        z_o[...] = dot_nt(hb[...], w1).astype(BF)
        dg_o[...] = dot_nt(dy[...], wo)
        taps = [cw[k : k + 1, pl.ds(c0, C)] for k in range(4)]
        bias = cb[0:1, pl.ds(c0, C)]

        def block(i, carry):
            r0 = i * RB
            p = rows_iota(r0, RB)
            v = bias + jnp.zeros((RB, C), F32)
            full = xpad[pl.ds(r0, RB + 8), :]
            for k in range(4):
                s = 3 - k
                x = full[8 - s : 8 - s + RB]
                if s:
                    x = x * wide(tap_mask(sc, docs, p, s), C)
                v = v + taps[k] * x
            v_o[pl.ds(r0, RB), :] = v
            u_o[pl.ds(r0, RB), :] = (v / (1.0 + jnp.exp(-v))).astype(BF)
            return carry

        lax.fori_loop(0, T // RB, block, 0)
        pt_o[...] = dot_nt(wt[0:XW], u_o[...])

    outs = [((T, C), BF), ((T, C), BF), ((T, C), BF), ((T, C), F32), ((XW, T), F32), ((T, C), F32), ((LANES, C), BF)]
    return call(front, outs, 7, 1, [pltpu.VMEM((T + 8, C), F32)])


def make_carry(T, C, docs, XW, R, N):
    RB = 64
    LT = C // LANES

    def carry(sc, pa, pb, u, z, dg, wt, dtb, alog, pt_o, da_o, du_o, dyin_o, pre_o, hend_o, gend_o):
        c0 = pl.multiple_of(sc[0], LANES)
        pt = pa[...] + pb[...]
        pt_o[...] = pt
        lin = dot_tn(pt[0:R].astype(BF), wt[XW : XW + R, :])
        pre_o[...] = lin + dtb[0:1, pl.ds(c0, C)]

        def block(i, tot):
            rs = pl.ds(i * RB, RB)
            p = rows_iota(i * RB, RB)
            keep = jnp.ones((RB, LANES), F32)
            for j in range(docs):
                keep = jnp.where(p == sc[1 + j], 0.0, keep)
            x = pre_o[rs, :]
            delta = soft(x)
            d = jnp.where(wide(keep, C) > 0.0, delta, RESET)
            r8 = pl.ds(i * (RB // 8), RB // 8)
            da_o[r8] = d.reshape(RB // 8, 8, C)
            du_o[r8] = (delta * u[rs, :].astype(F32)).reshape(RB // 8, 8, C)
            zf = z[rs, :].astype(F32)
            dyin_o[r8] = (dg[rs, :] * (zf / (1.0 + jnp.exp(-zf)))).reshape(RB // 8, 8, C)
            return tot + jnp.sum(d, axis=0, keepdims=True)

        tot = lax.fori_loop(0, T // RB, block, jnp.zeros((1, C), F32))
        am = [-jnp.exp(alog[:, pl.ds(c0 + l * LANES, LANES)]) for l in range(LT)]

        def rows(ref, i, j):
            full = ref[i, pl.ds(j, N, stride=0), :]
            return [full[:, l * LANES : (l + 1) * LANES] for l in range(LT)]

        nb = T // LANES

        def outer(k, c):
            bt = pt_o[R_ : R_ + N, pl.ds(pl.multiple_of(k * LANES, LANES), LANES)]
            ct = pt_o[R_ + N : R_ + 2 * N, pl.ds(pl.multiple_of((nb - 1 - k) * LANES, LANES), LANES)]

            def inner(i, c):
                h, g, bt, ct = c
                h = list(h)
                g = list(g)
                fi = k * (LANES // 8) + i
                ri = T // 8 - 1 - fi
                for j in range(8):
                    bb = jnp.broadcast_to(bt[:, j : j + 1], (N, LANES))
                    cc = jnp.broadcast_to(ct[:, LANES - 1 - j : LANES - j], (N, LANES))
                    df, uf = rows(da_o, fi, j), rows(du_o, fi, j)
                    db, yb = rows(da_o, ri, 7 - j), rows(dyin_o, ri, 7 - j)
                    for l in range(LT):
                        h[l] = jnp.exp(df[l] * am[l]) * h[l] + uf[l] * bb
                        g[l] = jnp.exp(db[l] * am[l]) * (g[l] + yb[l] * cc)
                return tuple(h), tuple(g), pltpu.roll(bt, LANES - 8, 1), pltpu.roll(ct, 8, 1)

            h, g, _, _ = lax.fori_loop(0, LANES // 8, inner, (c[0], c[1], bt, ct))
            return h, g

        R_ = R
        zero = tuple(jnp.zeros((N, LANES), F32) for _ in range(LT))
        h, g = lax.fori_loop(0, nb, outer, (zero, zero))
        for l in range(LT):
            hend_o[0:N, l * LANES : (l + 1) * LANES] = h[l]
            gend_o[0:N, l * LANES : (l + 1) * LANES] = g[l]
        hend_o[N : N + 8, :] = jnp.broadcast_to(tot, (8, C))
        gend_o[N : N + 8, :] = jnp.broadcast_to(tot, (8, C))

    outs = [((XW, T), F32)] + [((T // 8, 8, C), F32)] * 3 + [((T, C), F32)] + [((N + 8, C), F32)] * 2
    return call(carry, outs, 9, 1)


def make_scan(T, C, D, docs, XW, R, N):
    RB = 64
    LT = C // LANES
    nb = T // LANES

    def scan(sc, pt, da, du, dyin, pre, u, z, dg, dy, w, wt, alog, skip, h1, h2, g1, g2,
             g_o, dz_o, du1_o, dpre_o, dp_o, mix_o, pout_o, pdt_o, vec_o,
             a_s, h_s, y_s, lb_s, dd_s):
        c0 = pl.multiple_of(sc[0], LANES)
        am = [-jnp.exp(alog[:, pl.ds(c0 + l * LANES, LANES)]) for l in range(LT)]
        sl = [slice(l * LANES, (l + 1) * LANES) for l in range(LT)]
        lane = lax.broadcasted_iota(jnp.int32, (N, LANES), 1)

        def rows(ref, i, j):
            full = ref[i, pl.ds(j, N, stride=0), :]
            return [full[:, sl[l]] for l in range(LT)]

        hin, gin = [], []
        for l in range(LT):
            pf = jnp.exp(jnp.broadcast_to(h1[N : N + 1, sl[l]], (N, LANES)) * am[l])
            pb = jnp.exp(jnp.broadcast_to(g1[N : N + 1, sl[l]], (N, LANES)) * am[l])
            hin.append(h1[0:N, sl[l]] + pf * h2[0:N, sl[l]])
            gin.append(g1[0:N, sl[l]] + pb * g2[0:N, sl[l]])
            h_s[0, :, sl[l]] = hin[l]

        def fouter(k, h):
            blk = pl.ds(pl.multiple_of(k * LANES, LANES), LANES)
            bt = pt[R : R + N, blk]
            ct = pt[R + N : R + 2 * N, blk]

            def inner(i, c):
                h, bt, ct = c
                h = list(h)
                fi = k * (LANES // 8) + i
                for j in range(8):
                    t = fi * 8 + j
                    bb = jnp.broadcast_to(bt[:, j : j + 1], (N, LANES))
                    cc = jnp.broadcast_to(ct[:, j : j + 1], (N, LANES))
                    dr, ur = rows(da, fi, j), rows(du, fi, j)
                    for l in range(LT):
                        a = jnp.exp(dr[l] * am[l])
                        a_s[t, :, sl[l]] = a
                        h[l] = a * h[l] + ur[l] * bb
                        h_s[t + 1, :, sl[l]] = h[l]
                        y_s[fi, j : j + 1, sl[l]] = jnp.sum(h[l] * cc, axis=0, keepdims=True)
                return tuple(h), pltpu.roll(bt, LANES - 8, 1), pltpu.roll(ct, LANES - 8, 1)

            return lax.fori_loop(0, LANES // 8, inner, (h, bt, ct))[0]

        lax.fori_loop(0, nb, fouter, tuple(hin))

        def bouter(k, c):
            kb = nb - 1 - k
            blk = pl.ds(pl.multiple_of(kb * LANES, LANES), LANES)
            bt = pt[R : R + N, blk]
            ct = pt[R + N : R + 2 * N, blk]
            zero = jnp.zeros((N, LANES), F32)

            def inner(i, c):
                g, ga, db, dc, bt, ct = c
                g = list(g)
                ga = list(ga)
                l0 = LANES - 1 - i * 8
                fi = kb * (LANES // 8) + LANES // 8 - 1 - i
                for j in range(8):
                    t = kb * LANES + l0 - j
                    jj = 7 - j
                    bb = jnp.broadcast_to(bt[:, LANES - 1 - j : LANES - j], (N, LANES))
                    cc = jnp.broadcast_to(ct[:, LANES - 1 - j : LANES - j], (N, LANES))
                    sb = zero
                    scc = zero
                    dr, ur, yr = rows(da, fi, jj), rows(du, fi, jj), rows(dyin, fi, jj)
                    for l in range(LT):
                        dyr = yr[l]
                        lam = cc * dyr + g[l]
                        g[l] = a_s[t, :, sl[l]] * lam
                        dal = g[l] * h_s[t, :, sl[l]]
                        lb_s[fi, jj : jj + 1, sl[l]] = jnp.sum(lam * bb, axis=0, keepdims=True)
                        dd_s[fi, jj : jj + 1, sl[l]] = jnp.sum(dal * am[l], axis=0, keepdims=True)
                        ga[l] = ga[l] + dal * dr[l]
                        sb = sb + lam * ur[l]
                        scc = scc + dyr * h_s[t + 1, :, sl[l]]
                    here = lane == l0 - j
                    db = jnp.where(here, jnp.sum(sb, axis=1, keepdims=True), db)
                    dc = jnp.where(here, jnp.sum(scc, axis=1, keepdims=True), dc)
                return tuple(g), tuple(ga), db, dc, pltpu.roll(bt, 8, 1), pltpu.roll(ct, 8, 1)

            g, ga, db, dc, _, _ = lax.fori_loop(
                0, LANES // 8, inner, (c[0], c[1], zero, zero, bt, ct)
            )
            dp_o[R : R + N, blk] = db
            dp_o[R + N : R + 2 * N, blk] = dc
            return g, ga

        zeros = tuple(jnp.zeros((N, LANES), F32) for _ in range(LT))
        _, ga = lax.fori_loop(0, nb, bouter, (tuple(gin), zeros))
        for l in range(LT):
            vec_o[8 : 8 + N, sl[l]] = am[l] * ga[l]
        skr = skip[0:1, pl.ds(c0, C)]

        def block(i, tot):
            gdt, gsk = tot
            rs = pl.ds(i * RB, RB)
            r8 = pl.ds(i * (RB // 8), RB // 8)
            uf = u[rs, :].astype(F32)
            zf = z[rs, :].astype(F32)
            s = 1.0 / (1.0 + jnp.exp(-zf))
            yin = y_s[r8].reshape(RB, C) + skr * uf
            g_o[rs, :] = (yin * (zf * s)).astype(BF)
            dz_o[rs, :] = (dg[rs, :] * yin * slope_of(zf, s)).astype(BF)
            lb = lb_s[r8].reshape(RB, C)
            dyr = dyin[r8].reshape(RB, C)
            x = pre[rs, :]
            dpre = (lb * uf + dd_s[r8].reshape(RB, C)) / (1.0 + jnp.exp(-x))
            dpre_o[rs, :] = dpre.astype(BF)
            du1_o[rs, :] = dyr * skr + lb * soft(x)
            return gdt + jnp.sum(dpre, axis=0, keepdims=True), gsk + jnp.sum(dyr * uf, axis=0, keepdims=True)

        z1 = jnp.zeros((1, C), F32)
        gdt, gsk = lax.fori_loop(0, T // RB, block, (z1, z1))
        vec_o[5:6, :] = gdt
        vec_o[6:7, :] = gsk
        vec_o[7:8, :] = z1
        vec_o[0:5, :] = jnp.zeros((5, C), F32)
        dp_o[0:R, :] = dot_nt(wt[XW : XW + R, :], dpre_o[...])
        pdt_o[...] = dot_nn(pt[0:R, :].astype(BF), dpre_o[...])
        mix_o[...] = dot_nn(g_o[...], w[:, 2 * D + LANES : 3 * D + LANES])
        pout_o[...] = dot_tn(g_o[...], dy[...])

    outs = [((T, C), BF), ((T, C), BF), ((T, C), F32), ((T, C), BF), ((XW, T), F32), ((T, D), F32),
            ((C, D), F32), ((R, C), F32), ((8 + N, C), F32)]
    scratch = [pltpu.VMEM((T, N, C), F32), pltpu.VMEM((T + 1, N, C), F32)] + [pltpu.VMEM((T // 8, 8, C), F32)] * 3
    return call(scan, outs, 18, 1, scratch)


def make_back(T, C, D, docs, XW, R):
    RB = 64

    def back(sc, da_, db_, du1, v, u, xu, xhalo, wt, cw, vec, dxu_o, spill_o, pxt_o, vec_o, pad1, pad2, pad3, xpad):
        c0 = pl.multiple_of(sc[0], LANES)
        dpl = (da_[...] + db_[...]).astype(BF)
        pxt_o[...] = dot_nn(dpl, u[...])
        dxu_o[...] = du1[...] + dot_tn(dpl, wt[0:XW, :])
        pads = {1: pad1, 2: pad2, 3: pad3}
        xpad[0:8, :] = xhalo[...]
        xpad[8 : 8 + T, :] = xu[...].astype(F32)
        taps = [cw[k : k + 1, pl.ds(c0, C)] for k in range(4)]
        z8 = jnp.zeros((8, C), F32)
        for s in (1, 2, 3):
            pads[s][0:8, :] = z8
            pads[s][8 + T : 16 + T, :] = z8

        def block(i, tot):
            r0 = i * RB
            rs = pl.ds(r0, RB)
            p = rows_iota(r0, RB)
            vf = v[rs, :]
            sg = 1.0 / (1.0 + jnp.exp(-vf))
            dv = dxu_o[rs, :] * slope_of(vf, sg)
            new = [None] * 5
            full = xpad[pl.ds(r0, RB + 8), :]
            new[4] = tot[4] + jnp.sum(dv, axis=0, keepdims=True)
            for k in range(4):
                s = 3 - k
                x = full[8 - s : 8 - s + RB]
                m = dv
                if s:
                    m = dv * wide(tap_mask(sc, docs, p, s), C)
                    pads[s][pl.ds(8 + r0, RB), :] = taps[k] * m
                else:
                    dxu_o[rs, :] = taps[k] * m
                new[k] = tot[k] + jnp.sum(m * x, axis=0, keepdims=True)
            return tuple(new)

        z1 = jnp.zeros((1, C), F32)
        tot = lax.fori_loop(0, T // RB, block, (z1,) * 5)
        vec_o[...] = vec[...]
        for k in range(5):
            vec_o[k : k + 1, :] = tot[k]

        def gather(i, c):
            r0 = i * RB
            rs = pl.ds(r0, RB)
            acc = dxu_o[rs, :]
            for s in (1, 2, 3):
                acc = acc + pads[s][pl.ds(8 + r0, RB + 8), :][s : s + RB]
            dxu_o[rs, :] = acc
            return c

        lax.fori_loop(0, T // RB, gather, 0)
        acc = z8
        for s in (1, 2, 3):
            acc = acc + pads[s][s : s + 8, :]
        spill_o[...] = acc

    outs = [((T, C), F32), ((8, C), F32), ((XW, C), F32), (None, F32)]

    def build(vrows):
        o = outs[:3] + [((vrows, C), F32)]
        return call(back, o, 11, 1, [pltpu.VMEM((T + 16, C), F32)] * 3 + [pltpu.VMEM((T + 8, C), F32)])

    return build


def make_last(T, C, D, XW, R):
    def last(dxu, spill, dz, hb, w, pxt, pdt, dn_o, p0_o, p1_o, pxdt_o):
        top = dxu[...]
        low = jnp.concatenate([jnp.zeros((T - 8, C), F32), spill[...]], axis=0)
        dx = (top + low).astype(BF)
        dn_o[...] = dot_nn(dx, w[:, 0:D]) + dot_nn(dz[...], w[:, D : 2 * D])
        p0_o[...] = dot_tn(dx, hb[...])
        p1_o[...] = dot_tn(dz[...], hb[...])
        pxdt_o[...] = jnp.concatenate([pxt[...], pdt[...]], axis=0).T

    outs = [((T, D), F32), ((C, D), F32), ((C, D), F32), ((C, LANES), F32)]
    return call(last, outs, 7, 0)


def halves(x):
    hi = x.astype(BF)
    return hi, (x - hi.astype(F32)).astype(BF)


def mul3(ah, al, bh, bl):
    return dot_nn(ah, bh) + (dot_nn(ah, bl) + dot_nn(al, bh))


def make_muon(n, rows, rate, cuts):
    nbk = 256 if n % 256 == 0 else n
    blocks = n // nbk

    def muon(gram, upd, wgt, out, ah, al, qh, ql, th, tl, xs, acc):
        col = lax.broadcasted_iota(jnp.int32, (1, n), 1)
        edges = [0] + list(cuts)
        inv = jnp.zeros((1, n), F32)
        for lo, hi in zip(edges[:-1], edges[1:]):
            tot = jnp.zeros((1, 1), F32)
            for b in range(blocks):
                r = lax.broadcasted_iota(jnp.int32, (nbk, nbk), 0)
                c = lax.broadcasted_iota(jnp.int32, (nbk, nbk), 1)
                inside = (r == c) & (r + b * nbk >= lo) & (r + b * nbk < hi)
                d = gram[b * nbk : (b + 1) * nbk, b * nbk : (b + 1) * nbk]
                d = jnp.sum(jnp.where(inside, d, 0.0), axis=1, keepdims=True)
                tot = tot + jnp.sum(d, axis=0, keepdims=True)
            one = 1.0 / (jnp.sqrt(tot) + 1e-07)
            inv = jnp.where((col >= lo) & (col < hi), one, inv)
        xs[...] = upd[...] * inv

        def at(b):
            return slice(b * nbk, (b + 1) * nbk)

        def put(i, value, hi_ref, lo_ref):
            h, l = halves(value)
            hi_ref[at(i), i * nbk : n] = h
            lo_ref[at(i), i * nbk : n] = l
            for j in range(i + 1, blocks):
                t = value[:, (j - i) * nbk : (j - i + 1) * nbk].T
                h, l = halves(t)
                hi_ref[at(j), at(i)] = h
                lo_ref[at(j), at(i)] = l

        for i in range(blocks):
            g = gram[at(i), i * nbk : n]
            if len(cuts) > 1:
                r = lax.broadcasted_iota(jnp.int32, g.shape, 0) + i * nbk
                c = lax.broadcasted_iota(jnp.int32, g.shape, 1) + i * nbk
                same = jnp.zeros(g.shape, F32)
                rinv = jnp.zeros((nbk, 1), F32)
                for lo, hi in zip(edges[:-1], edges[1:]):
                    both = (r >= lo) & (r < hi) & (c >= lo) & (c < hi)
                    same = jnp.where(both, 1.0, same)
                g = g * same
                one = inv[:, i * nbk : n]
                a = g * one * one
            else:
                one = inv[:, i * nbk : n]
                a = g * (one * one)
            acc[at(i), i * nbk : n] = a
            put(i, a, ah, al)

        def eye_plus(i, a, a2):
            r = lax.broadcasted_iota(jnp.int32, a.shape, 0)
            c = lax.broadcasted_iota(jnp.int32, a.shape, 1)
            return jnp.where(r == c, NS_A, 0.0) + (NS_B * a + NS_C * a2)

        def make_q():
            for i in range(blocks):
                tail = slice(i * nbk, n)
                a2 = mul3(ah[at(i), :], al[at(i), :], ah[:, tail], al[:, tail])
                put(i, eye_plus(i, acc[at(i), tail], a2), qh, ql)

        def apply_q():
            h, l = halves(xs[...])
            xs[...] = mul3(h, l, qh[...], ql[...])

        def step(k, c):
            make_q()
            apply_q()
            for i in range(blocks):
                tail = slice(i * nbk, n)
                put(i, mul3(ah[at(i), :], al[at(i), :], qh[:, tail], ql[:, tail]), th, tl)
            for i in range(blocks):
                tail = slice(i * nbk, n)
                a = mul3(th[at(i), :], tl[at(i), :], qh[:, tail], ql[:, tail])
                acc[at(i), tail] = a
                put(i, a, ah, al)
            return c

        lax.fori_loop(0, 4, step, 0)
        make_q()
        apply_q()
        ends = jnp.zeros((1, n), F32)
        for lo, hi, r in zip(edges[:-1], edges[1:], rate):
            ends = jnp.where((col >= lo) & (col < hi), r, ends)
        out[...] = wgt[...] - ends * xs[...]

    scratch = [pltpu.VMEM((n, n), BF)] * 6 + [pltpu.VMEM((rows, n), F32), pltpu.VMEM((n, n), F32)]
    return call(muon, [((rows, n), F32)], 3, 0, scratch)


HIGH = lax.Precision.HIGHEST
NS_A = 3.4445
NS_B = -4.775
NS_C = 2.0315
MOMENTUM = 0.95
MUON_RATE = 0.1
ADAM_RATE = 0.25
BETA_ONE = 0.9
BETA_TWO = 0.95
ADAM_EPS = 1e-08
DECAY_RATE = 0.01
NORM_EPS = 1e-05


def shifted(value, axis, by):
    devices = lax.axis_size(axis)
    pairs = [(i, i + by) for i in range(devices) if 0 <= i + by < devices]
    return lax.ppermute(value, axis, pairs)


def carried_in(part, axis, combine, identity, reverse):
    count = lax.axis_size(axis)
    place = lax.axis_index(axis)
    ahead = count - 1 - place if reverse else place
    gathered = jax.tree.map(lambda a: lax.all_gather(a, axis), part)
    state = jax.tree.map(lambda a, e: jnp.zeros_like(a) + jnp.asarray(e, a.dtype), part, identity)

    def one(hop, state):
        source = count - 1 - hop if reverse else hop
        return combine(
            state, jax.tree.map(lambda a: lax.dynamic_index_in_dim(a, source, 0, False), gathered)
        )

    return lax.fori_loop(0, ahead, one, state)


def pair_combine(earlier, latter):
    return (earlier[0] * latter[0], latter[0] * earlier[1] + latter[1])


def silu_slope(operand):
    sigmoid_value = jax.nn.sigmoid(operand)
    return sigmoid_value * (1.0 + operand * (1.0 - sigmoid_value))


def tp_swap(value, bit):
    devices = lax.axis_size("tp")
    return lax.ppermute(value, "tp", [(i, i ^ bit) for i in range(devices)])


def widen(local_part, tp_offset, full_width):
    base = jnp.zeros(local_part.shape[:-1] + (full_width,), jnp.float32)
    starts = (0,) * (local_part.ndim - 1) + (tp_offset,)
    return lax.dynamic_update_slice(base, local_part, starts)


def momentum_step(gradient, momentum_old):
    momentum_new = MOMENTUM * momentum_old + gradient
    return (momentum_new, gradient + MOMENTUM * momentum_new)


def adam_update(parameters, gradient, moment_one, moment_two, adam_step):
    count = adam_step[0].astype(jnp.float32)
    first_new = BETA_ONE * moment_one + (1.0 - BETA_ONE) * gradient
    second_new = BETA_TWO * moment_two + (1.0 - BETA_TWO) * gradient * gradient
    first_hat = first_new / (1.0 - jnp.power(jnp.float32(BETA_ONE), count))
    second_hat = second_new / (1.0 - jnp.power(jnp.float32(BETA_TWO), count))
    updated = parameters - ADAM_RATE * (
        first_hat / (jnp.sqrt(second_hat) + ADAM_EPS) + DECAY_RATE * parameters
    )
    return (updated, first_new, second_new)


def on_device(
    block_input,
    cotangent,
    route_perm,
    doc_lengths,
    norm_gain,
    in_proj,
    conv_weight,
    conv_bias,
    x_proj,
    dt_proj,
    dt_bias,
    a_log,
    skip_gain,
    out_proj,
    in_momentum,
    x_momentum,
    dt_momentum,
    out_momentum,
    adam_first,
    adam_second,
    adam_step,
):
    ctx_count = lax.axis_size("ctx")
    fsdp_count = lax.axis_size("fsdp")
    ctx_index = lax.axis_index("ctx")
    tp_index = lax.axis_index("tp")
    tokens = block_input.shape[0]
    model_width = block_input.shape[1]
    stream = tokens * ctx_count
    share_rows = tokens // ctx_count
    kernel = conv_weight.shape[0]
    state_count = a_log.shape[0]
    inner_total = conv_bias.shape[0]
    positions = ctx_index * tokens + jnp.arange(tokens, dtype=jnp.int32)
    perm_row = route_perm % stream
    own_dest = lax.dynamic_slice_in_dim(perm_row, ctx_index * tokens, tokens)
    send_order = jnp.argsort(own_dest)
    send_place = jnp.argsort(send_order)
    source_of = jnp.argsort(perm_row)
    own_source = lax.dynamic_slice_in_dim(source_of, ctx_index * tokens, tokens) // tokens
    recv_order = jnp.argsort(own_source * stream + positions)
    recv_place = jnp.argsort(recv_order)
    sent = (
        block_input[send_order].reshape(ctx_count, share_rows, model_width),
        cotangent[send_order].reshape(ctx_count, share_rows, model_width),
    )
    got_input, got_cotangent = (
        lax.all_to_all(sent[0], "ctx", split_axis=0, concat_axis=0, tiled=True),
        lax.all_to_all(sent[1], "ctx", split_axis=0, concat_axis=0, tiled=True),
    )
    stream_x = got_input.reshape(tokens, model_width)[recv_place]
    stream_dy = got_cotangent.reshape(tokens, model_width)[recv_place]
    lengths_row = doc_lengths[0]
    offsets = jnp.cumsum(lengths_row) - lengths_row
    x_float = stream_x.astype(jnp.float32)
    inv_rms = lax.rsqrt(jnp.mean(x_float * x_float, axis=1, keepdims=True) + NORM_EPS)
    normed = (x_float * inv_rms * norm_gain).astype(jnp.bfloat16)
    rank_width = dt_proj.shape[1]
    proj_width = x_proj.shape[1]
    packed = jnp.concatenate(
        [in_proj.reshape(in_proj.shape[0], -1), x_proj, dt_proj, out_proj], axis=1
    ).astype(jnp.bfloat16)
    wide_all = lax.all_gather(packed, ("fsdp", "ctx"), axis=0, tiled=True)
    channels = wide_all.shape[0]
    docs = lengths_row.shape[0]
    scal = jnp.concatenate(
        [(tp_index * channels)[None], offsets - ctx_index * tokens]
    ).astype(jnp.int32)
    cbias_row = conv_bias.reshape(1, -1)
    dtb_row = dt_bias.reshape(1, -1)
    skip_row = skip_gain.reshape(1, -1)
    halo = shifted(normed[tokens - 8 :], "ctx", 1)
    conv_in, gate_in, conv_act, conv_out, pt_part, d_gated, w_turn = make_front(
        tokens, channels, model_width, docs, proj_width, rank_width
    )(scal, normed, halo, stream_dy, wide_all, conv_weight, cbias_row)
    pt_pair = pt_part + tp_swap(pt_part, 1)
    pt_far = tp_swap(pt_pair, 2)
    pt, dec, drv, d_inner, sig, h_end, g_end = make_carry(
        tokens, channels, docs, proj_width, rank_width, state_count
    )(scal, pt_pair, pt_far, conv_act, gate_in, d_gated, w_turn, dtb_row, a_log)
    h_one = shifted(h_end, "ctx", 1)
    h_two = shifted(h_end, "ctx", 2)
    g_one = shifted(g_end, "ctx", -1)
    g_two = shifted(g_end, "ctx", -2)
    gate_low, d_gate, du_one, d_pre_low, dp_part, mix_part, part_out, part_dt, vec_part = make_scan(
        tokens, channels, model_width, docs, proj_width, rank_width, state_count
    )(
        scal, pt, dec, drv, d_inner, sig, conv_act, gate_in, d_gated, stream_dy, wide_all,
        w_turn, a_log, skip_row, h_one, h_two, g_one, g_two,
    )
    dp_pair = dp_part + tp_swap(dp_part, 1)
    dp_far = tp_swap(dp_pair, 2)
    x_halo = shifted(conv_in[tokens - 8 :].astype(jnp.float32), "ctx", 1)
    d_conv_in, spill, part_xt, vec_chan = make_back(
        tokens, channels, model_width, docs, proj_width, rank_width
    )(8 + state_count)(
        scal, dp_pair, dp_far, du_one, conv_out, conv_act, conv_in, x_halo, w_turn, conv_weight,
        vec_part,
    )
    spill_in = shifted(spill, "ctx", -1)
    d_norm_part, part_in0, part_in1, part_xdt = make_last(
        tokens, channels, model_width, proj_width, rank_width
    )(d_conv_in, spill_in, d_gate, normed, wide_all, part_xt, part_dt)
    g_kernel = vec_chan[:4]
    g_cbias = vec_chan[4]
    g_dtb = vec_chan[5]
    g_skip = vec_chan[6]
    g_alog = vec_chan[8:]
    mix_full, d_normed = lax.psum((mix_part, d_norm_part), "tp")
    out_stream = (x_float + mix_full).astype(jnp.bfloat16)
    scaled = norm_gain * d_normed
    cubed = inv_rms * inv_rms * inv_rms
    d_x = (
        stream_dy.astype(jnp.float32)
        + inv_rms * scaled
        - x_float * cubed * jnp.mean(scaled * x_float, axis=1, keepdims=True)
    )
    g_gain = jnp.sum(d_normed * x_float * inv_rms, axis=0)
    back = (
        out_stream[recv_order].reshape(ctx_count, share_rows, model_width),
        d_x.astype(jnp.bfloat16)[recv_order].reshape(ctx_count, share_rows, model_width),
    )
    out_back, grad_back = (
        lax.all_to_all(back[0], "ctx", split_axis=0, concat_axis=0, tiled=True),
        lax.all_to_all(back[1], "ctx", split_axis=0, concat_axis=0, tiled=True),
    )
    block_out = out_back.reshape(tokens, model_width)[send_place]
    input_grad = grad_back.reshape(tokens, model_width)[send_place]
    row_grads = lax.psum_scatter(
        jnp.concatenate([part_in0, part_in1, part_xdt, part_out], axis=1),
        ("fsdp", "ctx"),
        scatter_dimension=0,
        tiled=True,
    )
    own_rows = row_grads.shape[0]
    cut_in = 2 * model_width
    g_in = row_grads[:, :cut_in].reshape(own_rows, 2, model_width)
    g_xdt = row_grads[:, cut_in : cut_in + proj_width + rank_width]
    g_x = g_xdt[:, :proj_width]
    g_dt = g_xdt[:, proj_width:]
    g_out = row_grads[:, cut_in + proj_width + rank_width :]
    mom_in, upd_in = momentum_step(g_in, in_momentum)
    mom_x, upd_x = momentum_step(g_x, x_momentum)
    mom_dt, upd_dt = momentum_step(g_dt, dt_momentum)
    mom_out, upd_out = momentum_step(g_out, out_momentum)
    upd_xdt = jnp.concatenate([upd_x, upd_dt], axis=1)
    flat_in = upd_in.reshape(own_rows * 2, model_width)
    tp_offset = tp_index * channels
    vec_local = jnp.concatenate(
        [
            jnp.where(tp_index == 0, g_gain, jnp.zeros_like(g_gain)),
            widen(g_kernel, tp_offset, inner_total).reshape(-1),
            widen(g_cbias, tp_offset, inner_total),
            widen(g_dtb, tp_offset, inner_total),
            widen(g_alog, tp_offset, inner_total).reshape(-1),
            widen(g_skip, tp_offset, inner_total),
        ]
    )
    gram_in, gram_xdt, gram_out, vec_grads = lax.psum(
        (
            jnp.dot(flat_in.T, flat_in, precision=HIGH),
            jnp.dot(upd_xdt.T, upd_xdt, precision=HIGH),
            jnp.dot(upd_out.T, upd_out, precision=HIGH),
            vec_local,
        ),
        ("fsdp", "ctx", "tp"),
    )
    scale_in = MUON_RATE * 0.2 * math.sqrt(max(2 * inner_total, model_width))
    scale_x = MUON_RATE * 0.2 * math.sqrt(max(inner_total, proj_width))
    scale_dt = MUON_RATE * 0.2 * math.sqrt(max(inner_total, rank_width))
    scale_out = MUON_RATE * 0.2 * math.sqrt(max(inner_total, model_width))
    new_in = make_muon(model_width, 2 * own_rows, (scale_in,), (model_width,))(
        gram_in, flat_in, in_proj.reshape(2 * own_rows, model_width)
    )[0].reshape(own_rows, 2, model_width)
    new_out = make_muon(model_width, own_rows, (scale_out,), (model_width,))(gram_out, upd_out, out_proj)[0]
    new_xdt = make_muon(
        proj_width + rank_width, own_rows, (scale_x, scale_dt), (proj_width, proj_width + rank_width)
    )(gram_xdt, upd_xdt, jnp.concatenate([x_proj, dt_proj], axis=1))[0]
    new_x = new_xdt[:, :proj_width]
    new_dt = new_xdt[:, proj_width:]
    vec_params = jnp.concatenate(
        [norm_gain, conv_weight.reshape(-1), conv_bias, dt_bias, a_log.reshape(-1), skip_gain]
    )
    new_vec, first_new, second_new = adam_update(
        vec_params, vec_grads, adam_first, adam_second, adam_step
    )
    cut_b = model_width + kernel * inner_total
    cut_c = cut_b + inner_total
    cut_d = cut_c + inner_total
    cut_e = cut_d + state_count * inner_total
    return (
        block_out,
        input_grad,
        vec_grads[:model_width],
        g_in,
        vec_grads[model_width:cut_b].reshape(kernel, inner_total),
        vec_grads[cut_b:cut_c],
        g_x,
        g_dt,
        vec_grads[cut_c:cut_d],
        vec_grads[cut_d:cut_e].reshape(state_count, inner_total),
        vec_grads[cut_e:],
        g_out,
        new_vec[:model_width],
        new_in,
        new_vec[model_width:cut_b].reshape(kernel, inner_total),
        new_vec[cut_b:cut_c],
        new_x,
        new_dt,
        new_vec[cut_c:cut_d],
        new_vec[cut_d:cut_e].reshape(state_count, inner_total),
        new_vec[cut_e:],
        new_out,
        mom_in,
        mom_x,
        mom_dt,
        mom_out,
        first_new,
        second_new,
    )


def solution(mesh):
    return jax.shard_map(
        on_device,
        mesh=mesh,
        in_specs=(
            P(("fsdp", "ctx"), None),
            P(("fsdp", "ctx"), None),
            P("fsdp"),
            P("fsdp", None),
            P(),
            P(("tp", "fsdp", "ctx"), None, None),
            P(),
            P(),
            P(("tp", "fsdp", "ctx"), None),
            P(("tp", "fsdp", "ctx"), None),
            P(),
            P(),
            P(),
            P(("tp", "fsdp", "ctx"), None),
            P(("tp", "fsdp", "ctx"), None, None),
            P(("tp", "fsdp", "ctx"), None),
            P(("tp", "fsdp", "ctx"), None),
            P(("tp", "fsdp", "ctx"), None),
            P(),
            P(),
            P(),
        ),
        out_specs=(
            P(("fsdp", "ctx"), None),
            P(("fsdp", "ctx"), None),
            P(),
            P(("tp", "fsdp", "ctx"), None, None),
            P(),
            P(),
            P(("tp", "fsdp", "ctx"), None),
            P(("tp", "fsdp", "ctx"), None),
            P(),
            P(),
            P(),
            P(("tp", "fsdp", "ctx"), None),
            P(),
            P(("tp", "fsdp", "ctx"), None, None),
            P(),
            P(),
            P(("tp", "fsdp", "ctx"), None),
            P(("tp", "fsdp", "ctx"), None),
            P(),
            P(),
            P(),
            P(("tp", "fsdp", "ctx"), None),
            P(("tp", "fsdp", "ctx"), None, None),
            P(("tp", "fsdp", "ctx"), None),
            P(("tp", "fsdp", "ctx"), None),
            P(("tp", "fsdp", "ctx"), None),
            P(),
            P(),
        ),
        check_vma=False,
    )
```

```python
import math

import jax
import jax.numpy as jnp
from jax import lax
from jax.experimental import pallas as pl
from jax.experimental.pallas import tpu as pltpu
from jax.sharding import PartitionSpec as P

F32 = jnp.float32
BF = jnp.bfloat16
LANES = 128
RESET = 1e5
VMEM_LIMIT = 60 * 1024 * 1024
NS_A = 3.4445
NS_B = -4.775
NS_C = 2.0315
MOMENTUM = 0.95
MUON_RATE = 0.1
ADAM_RATE = 0.25
BETA_ONE = 0.9
BETA_TWO = 0.95
ADAM_EPS = 1e-08
DECAY_RATE = 0.01
NORM_EPS = 1e-05


def dot_nn(a, b):
    return lax.dot_general(a, b, (((1,), (0,)), ((), ())), preferred_element_type=F32)


def dot_nt(a, b):
    return lax.dot_general(a, b, (((1,), (1,)), ((), ())), preferred_element_type=F32)


def dot_tn(a, b):
    return lax.dot_general(a, b, (((0,), (0,)), ((), ())), preferred_element_type=F32)


def soft(x):
    return jnp.maximum(x, 0.0) + jnp.log1p(jnp.exp(-jnp.abs(x)))


def slope_of(a, s):
    return s * (1.0 + a * (1.0 - s))


def call(body, outs, n_in, n_smem, scratch=(), flops=10**9):
    specs = [pl.BlockSpec(memory_space=pltpu.SMEM)] * n_smem + [
        pl.BlockSpec(memory_space=pltpu.VMEM)
    ] * (n_in - n_smem)
    return pl.pallas_call(
        body,
        out_shape=[jax.ShapeDtypeStruct(s, d) for s, d in outs],
        in_specs=specs,
        out_specs=[pl.BlockSpec(memory_space=pltpu.VMEM)] * len(outs),
        scratch_shapes=list(scratch),
        compiler_params=pltpu.CompilerParams(vmem_limit_bytes=VMEM_LIMIT),
        name=body.__name__,
    )


def rows_iota(r0, rows):
    return lax.broadcasted_iota(jnp.int32, (rows, LANES), 0) + r0


def tap_mask(sc_ref, docs, p, shift):
    ok = jnp.ones(p.shape, F32)
    for j in range(docs):
        off = sc_ref[1 + j]
        ok = jnp.where((off <= p) & (p < off + shift), 0.0, ok)
    return ok


def wide(mask, width):
    return jnp.concatenate([mask] * (width // LANES), axis=1)


def make_front(T, C, D, docs, XW, R):
    RB = 64

    def front(sc, hb, halo, dy, wa, wr, cw, cb, xu_o, z_o, u_o, v_o, pt_o, dg_o, wt_o, xpad):
        w0 = wa[...]
        w1 = wr[:, 0:D]
        wo = wr[:, D + LANES : 2 * D + LANES]
        wt = wr[:, D : D + LANES].astype(F32).T.astype(BF)
        wt_o[...] = wt
        c0 = pl.multiple_of(sc[0], LANES)
        xpad[0:8, :] = dot_nt(halo[...], w0).astype(BF).astype(F32)
        xu = dot_nt(hb[...], w0).astype(BF)
        xu_o[...] = xu
        xpad[8 : 8 + T, :] = xu.astype(F32)
        z_o[...] = dot_nt(hb[...], w1).astype(BF)
        dg_o[...] = dot_nt(dy[...], wo)
        taps = [cw[k : k + 1, pl.ds(c0, C)] for k in range(4)]
        bias = cb[0:1, pl.ds(c0, C)]

        def block(i, carry):
            r0 = i * RB
            p = rows_iota(r0, RB)
            v = bias + jnp.zeros((RB, C), F32)
            full = xpad[pl.ds(r0, RB + 8), :]
            for k in range(4):
                s = 3 - k
                x = full[8 - s : 8 - s + RB]
                if s:
                    x = x * wide(tap_mask(sc, docs, p, s), C)
                v = v + taps[k] * x
            v_o[pl.ds(r0, RB), :] = v
            u_o[pl.ds(r0, RB), :] = (v / (1.0 + jnp.exp(-v))).astype(BF)
            return carry

        lax.fori_loop(0, T // RB, block, 0)
        pt_o[...] = dot_nt(wt[0:XW], u_o[...])

    outs = [((T, C), BF), ((T, C), BF), ((T, C), BF), ((T, C), F32), ((XW, T), F32), ((T, C), F32), ((LANES, C), BF)]
    return call(front, outs, 8, 1, [pltpu.VMEM((T + 8, C), F32)])


def make_carry(T, C, docs, XW, R, N):
    RB = 64
    LT = C // LANES

    def carry(sc, pa, pb, u, z, dg, wt, dtb, alog, pt_o, da_o, du_o, dyin_o, pre_o, hend_o, gend_o):
        c0 = pl.multiple_of(sc[0], LANES)
        pt = pa[...] + pb[...]
        pt_o[...] = pt
        lin = dot_tn(pt[0:R].astype(BF), wt[XW : XW + R, :])
        pre_o[...] = lin + dtb[0:1, pl.ds(c0, C)]

        def block(i, tot):
            rs = pl.ds(i * RB, RB)
            p = rows_iota(i * RB, RB)
            keep = jnp.ones((RB, LANES), F32)
            for j in range(docs):
                keep = jnp.where(p == sc[1 + j], 0.0, keep)
            x = pre_o[rs, :]
            delta = soft(x)
            d = jnp.where(wide(keep, C) > 0.0, delta, RESET)
            r8 = pl.ds(i * (RB // 8), RB // 8)
            da_o[r8] = d.reshape(RB // 8, 8, C)
            du_o[r8] = (delta * u[rs, :].astype(F32)).reshape(RB // 8, 8, C)
            zf = z[rs, :].astype(F32)
            dyin_o[r8] = (dg[rs, :] * (zf / (1.0 + jnp.exp(-zf)))).reshape(RB // 8, 8, C)
            return tot + jnp.sum(d, axis=0, keepdims=True)

        tot = lax.fori_loop(0, T // RB, block, jnp.zeros((1, C), F32))
        am = [-jnp.exp(alog[:, pl.ds(c0 + l * LANES, LANES)]) for l in range(LT)]

        def rows(ref, i, j):
            full = ref[i, pl.ds(j, N, stride=0), :]
            return [full[:, l * LANES : (l + 1) * LANES] for l in range(LT)]

        nb = T // LANES

        def outer(k, c):
            bt = pt_o[R_ : R_ + N, pl.ds(pl.multiple_of(k * LANES, LANES), LANES)]
            ct = pt_o[R_ + N : R_ + 2 * N, pl.ds(pl.multiple_of((nb - 1 - k) * LANES, LANES), LANES)]

            def inner(i, c):
                h, g, bt, ct = c
                h = list(h)
                g = list(g)
                fi = k * (LANES // 8) + i
                ri = T // 8 - 1 - fi
                for j in range(8):
                    bb = jnp.broadcast_to(bt[:, j : j + 1], (N, LANES))
                    cc = jnp.broadcast_to(ct[:, LANES - 1 - j : LANES - j], (N, LANES))
                    df, uf = rows(da_o, fi, j), rows(du_o, fi, j)
                    db, yb = rows(da_o, ri, 7 - j), rows(dyin_o, ri, 7 - j)
                    for l in range(LT):
                        h[l] = jnp.exp(df[l] * am[l]) * h[l] + uf[l] * bb
                        g[l] = jnp.exp(db[l] * am[l]) * (g[l] + yb[l] * cc)
                return tuple(h), tuple(g), pltpu.roll(bt, LANES - 8, 1), pltpu.roll(ct, 8, 1)

            h, g, _, _ = lax.fori_loop(0, LANES // 8, inner, (c[0], c[1], bt, ct))
            return h, g

        R_ = R
        zero = tuple(jnp.zeros((N, LANES), F32) for _ in range(LT))
        h, g = lax.fori_loop(0, nb, outer, (zero, zero))
        for l in range(LT):
            hend_o[0:N, l * LANES : (l + 1) * LANES] = h[l]
            gend_o[0:N, l * LANES : (l + 1) * LANES] = g[l]
        hend_o[N : N + 8, :] = jnp.broadcast_to(tot, (8, C))
        gend_o[N : N + 8, :] = jnp.broadcast_to(tot, (8, C))

    outs = [((XW, T), F32)] + [((T // 8, 8, C), F32)] * 3 + [((T, C), F32)] + [((N + 8, C), F32)] * 2
    return call(carry, outs, 9, 1)


def make_scan(T, C, D, docs, XW, R, N):
    RB = 64
    LT = C // LANES
    nb = T // LANES

    def scan(sc, pt, da, du, dyin, pre, u, z, dg, dy, hb, wr, wt, alog, skip, h1, h2, g1, g2,
             g_o, dz_o, du1_o, dpre_o, dp_o, mix_o, pw_o, pdt_o, vec_o,
             a_s, h_s, y_s, lb_s, dd_s):
        c0 = pl.multiple_of(sc[0], LANES)
        am = [-jnp.exp(alog[:, pl.ds(c0 + l * LANES, LANES)]) for l in range(LT)]
        sl = [slice(l * LANES, (l + 1) * LANES) for l in range(LT)]
        lane = lax.broadcasted_iota(jnp.int32, (N, LANES), 1)

        def rows(ref, i, j):
            full = ref[i, pl.ds(j, N, stride=0), :]
            return [full[:, sl[l]] for l in range(LT)]

        hin, gin = [], []
        for l in range(LT):
            pf = jnp.exp(jnp.broadcast_to(h1[N : N + 1, sl[l]], (N, LANES)) * am[l])
            pb = jnp.exp(jnp.broadcast_to(g1[N : N + 1, sl[l]], (N, LANES)) * am[l])
            hin.append(h1[0:N, sl[l]] + pf * h2[0:N, sl[l]])
            gin.append(g1[0:N, sl[l]] + pb * g2[0:N, sl[l]])
            h_s[0, :, sl[l]] = hin[l]

        def fouter(k, h):
            blk = pl.ds(pl.multiple_of(k * LANES, LANES), LANES)
            bt = pt[R : R + N, blk]
            ct = pt[R + N : R + 2 * N, blk]

            def inner(i, c):
                h, bt, ct = c
                h = list(h)
                fi = k * (LANES // 8) + i
                for j in range(8):
                    t = fi * 8 + j
                    bb = jnp.broadcast_to(bt[:, j : j + 1], (N, LANES))
                    cc = jnp.broadcast_to(ct[:, j : j + 1], (N, LANES))
                    dr, ur = rows(da, fi, j), rows(du, fi, j)
                    for l in range(LT):
                        a = jnp.exp(dr[l] * am[l])
                        a_s[t, :, sl[l]] = a
                        h[l] = a * h[l] + ur[l] * bb
                        h_s[t + 1, :, sl[l]] = h[l]
                        y_s[fi, j : j + 1, sl[l]] = jnp.sum(h[l] * cc, axis=0, keepdims=True)
                return tuple(h), pltpu.roll(bt, LANES - 8, 1), pltpu.roll(ct, LANES - 8, 1)

            return lax.fori_loop(0, LANES // 8, inner, (h, bt, ct))[0]

        lax.fori_loop(0, nb, fouter, tuple(hin))

        def bouter(k, c):
            kb = nb - 1 - k
            blk = pl.ds(pl.multiple_of(kb * LANES, LANES), LANES)
            bt = pt[R : R + N, blk]
            ct = pt[R + N : R + 2 * N, blk]
            zero = jnp.zeros((N, LANES), F32)

            def inner(i, c):
                g, ga, db, dc, bt, ct = c
                g = list(g)
                ga = list(ga)
                l0 = LANES - 1 - i * 8
                fi = kb * (LANES // 8) + LANES // 8 - 1 - i
                for j in range(8):
                    t = kb * LANES + l0 - j
                    jj = 7 - j
                    bb = jnp.broadcast_to(bt[:, LANES - 1 - j : LANES - j], (N, LANES))
                    cc = jnp.broadcast_to(ct[:, LANES - 1 - j : LANES - j], (N, LANES))
                    sb = zero
                    scc = zero
                    dr, ur, yr = rows(da, fi, jj), rows(du, fi, jj), rows(dyin, fi, jj)
                    for l in range(LT):
                        dyr = yr[l]
                        lam = cc * dyr + g[l]
                        g[l] = a_s[t, :, sl[l]] * lam
                        dal = g[l] * h_s[t, :, sl[l]]
                        lb_s[fi, jj : jj + 1, sl[l]] = jnp.sum(lam * bb, axis=0, keepdims=True)
                        dd_s[fi, jj : jj + 1, sl[l]] = jnp.sum(dal * am[l], axis=0, keepdims=True)
                        ga[l] = ga[l] + dal * dr[l]
                        sb = sb + lam * ur[l]
                        scc = scc + dyr * h_s[t + 1, :, sl[l]]
                    here = lane == l0 - j
                    db = jnp.where(here, jnp.sum(sb, axis=1, keepdims=True), db)
                    dc = jnp.where(here, jnp.sum(scc, axis=1, keepdims=True), dc)
                return tuple(g), tuple(ga), db, dc, pltpu.roll(bt, 8, 1), pltpu.roll(ct, 8, 1)

            g, ga, db, dc, _, _ = lax.fori_loop(
                0, LANES // 8, inner, (c[0], c[1], zero, zero, bt, ct)
            )
            dp_o[R : R + N, blk] = db
            dp_o[R + N : R + 2 * N, blk] = dc
            return g, ga

        zeros = tuple(jnp.zeros((N, LANES), F32) for _ in range(LT))
        _, ga = lax.fori_loop(0, nb, bouter, (tuple(gin), zeros))
        for l in range(LT):
            vec_o[8 : 8 + N, sl[l]] = am[l] * ga[l]
        skr = skip[0:1, pl.ds(c0, C)]

        def block(i, tot):
            gdt, gsk = tot
            rs = pl.ds(i * RB, RB)
            r8 = pl.ds(i * (RB // 8), RB // 8)
            uf = u[rs, :].astype(F32)
            zf = z[rs, :].astype(F32)
            s = 1.0 / (1.0 + jnp.exp(-zf))
            yin = y_s[r8].reshape(RB, C) + skr * uf
            g_o[rs, :] = (yin * (zf * s)).astype(BF)
            dz_o[rs, :] = (dg[rs, :] * yin * slope_of(zf, s)).astype(BF)
            lb = lb_s[r8].reshape(RB, C)
            dyr = dyin[r8].reshape(RB, C)
            x = pre[rs, :]
            dpre = (lb * uf + dd_s[r8].reshape(RB, C)) / (1.0 + jnp.exp(-x))
            dpre_o[rs, :] = dpre.astype(BF)
            du1_o[rs, :] = dyr * skr + lb * soft(x)
            return gdt + jnp.sum(dpre, axis=0, keepdims=True), gsk + jnp.sum(dyr * uf, axis=0, keepdims=True)

        z1 = jnp.zeros((1, C), F32)
        gdt, gsk = lax.fori_loop(0, T // RB, block, (z1, z1))
        vec_o[5:6, :] = gdt
        vec_o[6:7, :] = gsk
        vec_o[7:8, :] = z1
        vec_o[0:5, :] = jnp.zeros((5, C), F32)
        dp_o[0:R, :] = dot_nt(wt[XW : XW + R, :], dpre_o[...])
        pdt_o[...] = dot_nn(pt[0:R, :].astype(BF), dpre_o[...])
        mix_o[...] = dot_nn(g_o[...], wr[:, D + LANES : 2 * D + LANES]).astype(BF)
        pw_o[:, 0:D] = dot_tn(dz_o[...], hb[...]).astype(BF)
        pw_o[:, D : 2 * D] = dot_tn(g_o[...], dy[...]).astype(BF)

    outs = [((T, C), BF), ((T, C), BF), ((T, C), F32), ((T, C), BF), ((XW, T), F32), ((T, D), BF),
            ((C, 2 * D), BF), ((R, C), F32), ((8 + N, C), F32)]
    scratch = [pltpu.VMEM((T, N, C), F32), pltpu.VMEM((T + 1, N, C), F32)] + [pltpu.VMEM((T // 8, 8, C), F32)] * 3
    return call(scan, outs, 19, 1, scratch)


def make_back(T, C, D, docs, XW, R):
    RB = 64

    def back(sc, da_, db_, du1, v, u, xu, xhalo, wt, cw, vec, pdt, dxu_o, spill_o, pxt_o, vec_o, pad1, pad2, pad3, xpad):
        c0 = pl.multiple_of(sc[0], LANES)
        dpl = (da_[...] + db_[...]).astype(BF)
        pxt_o[...] = jnp.concatenate([dot_nn(dpl, u[...]), pdt[...]], axis=0).T.astype(BF)
        dxu_o[...] = du1[...] + dot_tn(dpl, wt[0:XW, :])
        pads = {1: pad1, 2: pad2, 3: pad3}
        xpad[0:8, :] = xhalo[...]
        xpad[8 : 8 + T, :] = xu[...].astype(F32)
        taps = [cw[k : k + 1, pl.ds(c0, C)] for k in range(4)]
        z8 = jnp.zeros((8, C), F32)
        for s in (1, 2, 3):
            pads[s][0:8, :] = z8
            pads[s][8 + T : 16 + T, :] = z8

        def block(i, tot):
            r0 = i * RB
            rs = pl.ds(r0, RB)
            p = rows_iota(r0, RB)
            vf = v[rs, :]
            sg = 1.0 / (1.0 + jnp.exp(-vf))
            dv = dxu_o[rs, :] * slope_of(vf, sg)
            new = [None] * 5
            full = xpad[pl.ds(r0, RB + 8), :]
            new[4] = tot[4] + jnp.sum(dv, axis=0, keepdims=True)
            for k in range(4):
                s = 3 - k
                x = full[8 - s : 8 - s + RB]
                m = dv
                if s:
                    m = dv * wide(tap_mask(sc, docs, p, s), C)
                    pads[s][pl.ds(8 + r0, RB), :] = taps[k] * m
                else:
                    dxu_o[rs, :] = taps[k] * m
                new[k] = tot[k] + jnp.sum(m * x, axis=0, keepdims=True)
            return tuple(new)

        z1 = jnp.zeros((1, C), F32)
        tot = lax.fori_loop(0, T // RB, block, (z1,) * 5)
        vec_o[...] = vec[...]
        for k in range(5):
            vec_o[k : k + 1, :] = tot[k]

        def gather(i, c):
            r0 = i * RB
            rs = pl.ds(r0, RB)
            acc = dxu_o[rs, :]
            for s in (1, 2, 3):
                acc = acc + pads[s][pl.ds(8 + r0, RB + 8), :][s : s + RB]
            dxu_o[rs, :] = acc
            return c

        lax.fori_loop(0, T // RB, gather, 0)
        acc = z8
        for s in (1, 2, 3):
            acc = acc + pads[s][s : s + 8, :]
        spill_o[...] = acc

    outs = [((T, C), F32), ((8, C), F32), ((C, LANES), BF), (None, F32)]

    def build(vrows):
        o = outs[:3] + [((vrows, C), F32)]
        return call(back, o, 12, 1, [pltpu.VMEM((T + 16, C), F32)] * 3 + [pltpu.VMEM((T + 8, C), F32)])

    return build


def make_last(T, C, D, Q):
    def last(dxu, spill, dz, hb, wa, wr, xdt, mix, x, rt, keep_o, send_o, pw_o, gain_o):
        low = jnp.concatenate([jnp.zeros((T - 8, C), F32), spill[...]], axis=0)
        dx = (dxu[...] + low).astype(BF)
        pw_o[:, 0:D] = dot_tn(dx, hb[...]).astype(BF)
        pw_o[:, D : D + LANES] = xdt[...]
        dn = dot_nn(dx, wa[...]) + dot_nn(dz[...], wr[:, 0:D])
        xf = x[...].astype(F32)
        inv = lax.rsqrt(jnp.mean(xf * xf, axis=1, keepdims=True) + NORM_EPS)
        gain_o[...] = jnp.sum(dn * xf * inv, axis=0, keepdims=True)
        dnl = dn.astype(BF)
        for e in range(T // Q):
            r = rt[:, e * Q : (e + 1) * Q]
            o = send_o if e % 2 else keep_o
            at = slice((e // 2) * Q, (e // 2 + 1) * Q)
            o[at, 0:D] = dot_tn(r, mix[...]).astype(BF)
            o[at, D : 2 * D] = dot_tn(r, dnl).astype(BF)

    half = T // 2
    outs = [((half, 2 * D), BF), ((half, 2 * D), BF), ((C, D + LANES), BF), ((1, D), F32)]
    return call(last, outs, 10, 0)


def flat_slots(k, shift, share, first):
    return (k >> shift) * share + first + (k & ((1 << shift) - 1))


def make_send(T, D, CT, TP):
    Q = T // TP
    share = T // CT
    SR = share // TP
    shift = SR.bit_length() - 1
    assert SR == 1 << shift and Q == CT * SR

    def send(rsc, perm, x, dy, buf_o, fin_o):
        c = rsc[0]
        tp = rsc[1]
        own = perm[0:1, pl.ds(pl.multiple_of(c * T, LANES), T)].astype(F32)
        r = lax.broadcasted_iota(jnp.int32, (T, T), 0)
        q = lax.broadcasted_iota(jnp.int32, (T, T), 1)
        row = jnp.broadcast_to(own, (T, T))
        col = jnp.broadcast_to(jnp.sum(jnp.where(r == q, row, 0.0), axis=1, keepdims=True), (T, T))
        pos_col = jnp.sum(jnp.where(row < col, 1.0, 0.0), axis=1, keepdims=True)
        pos_row = jnp.sum(jnp.where(col < row, 1.0, 0.0), axis=0, keepdims=True)
        k = lax.broadcasted_iota(jnp.int32, (Q, T), 0)
        pick = jnp.where(flat_slots(k, shift, share, SR * tp).astype(F32) == pos_row, 1.0, 0.0).astype(BF)
        buf_o[:, 0:D] = dot_nn(pick, x[...]).astype(BF)
        buf_o[:, D : 2 * D] = dot_nn(pick, dy[...]).astype(BF)
        f = lax.broadcasted_iota(jnp.int32, (T, Q), 1)
        for e in range(TP):
            slot = flat_slots(f, shift, share, SR * (tp ^ e)).astype(F32)
            fin_o[:, e * Q : (e + 1) * Q] = jnp.where(slot == pos_col, 1.0, 0.0).astype(BF)

    return call(send, [((Q, 2 * D), BF), ((T, T), BF)], 4, 1)


def make_recv(T, D, CT, TP):
    Q = T // TP
    share = T // CT
    SR = share // TP
    shift = SR.bit_length() - 1

    def recv(rsc, perm, gain, *rest):
        parts = rest[:TP]
        x_o, dy_o, hb_o, rt_o = rest[TP:]
        c = rsc[0]
        tp = rsc[1]
        place = (lax.broadcasted_iota(jnp.int32, (T, T), 0) + c * T)
        lane = lax.broadcasted_iota(jnp.int32, (T, LANES), 1)
        hot = jnp.zeros((T, LANES), F32)
        for s in range(CT):
            src = jnp.broadcast_to(perm[0:1, s * T : (s + 1) * T], (T, T))
            n = jnp.sum(jnp.where(src == place, 1.0, 0.0), axis=1, keepdims=True)
            hot = jnp.where(lane == s, n, hot)
        r = lax.broadcasted_iota(jnp.int32, (T, T), 0)
        q = lax.broadcasted_iota(jnp.int32, (T, T), 1)
        below = jnp.where(q < r, 1.0, 0.0).astype(BF)
        count = dot_nn(below, hot.astype(BF))
        rank = jnp.sum(hot * count, axis=1, keepdims=True)
        block = jnp.sum(hot * lane.astype(F32), axis=1, keepdims=True)
        want = block * share + rank
        f = lax.broadcasted_iota(jnp.int32, (T, Q), 1)
        xa = jnp.zeros((T, D), F32)
        ya = jnp.zeros((T, D), F32)
        for e in range(TP):
            slot = flat_slots(f, shift, share, SR * (tp ^ e)).astype(F32)
            m = jnp.where(slot == want, 1.0, 0.0).astype(BF)
            rt_o[:, e * Q : (e + 1) * Q] = m
            xa = xa + dot_nn(m, parts[e][:, 0:D])
            ya = ya + dot_nn(m, parts[e][:, D : 2 * D])
        x_o[...] = xa.astype(BF)
        dy_o[...] = ya.astype(BF)
        inv = lax.rsqrt(jnp.mean(xa * xa, axis=1, keepdims=True) + NORM_EPS)
        hb_o[...] = (xa * inv * gain[...]).astype(BF)

    return call(recv, [((T, D), BF)] * 3 + [((T, T), BF)], 3 + TP, 1)


def make_norm_back(Q, D):
    def norm_back(keep, got, far, own, gain, o):
        both = keep[0:Q].astype(F32) + got[0:Q].astype(F32) + far[...].astype(F32)
        xf = own[:, 0:D].astype(F32)
        inv = lax.rsqrt(jnp.mean(xf * xf, axis=1, keepdims=True) + NORM_EPS)
        dn = both[:, D : 2 * D]
        scaled = gain[...] * dn
        mean = jnp.mean(scaled * xf, axis=1, keepdims=True)
        o[:, 0:D] = (xf + both[:, 0:D]).astype(BF)
        o[:, D : 2 * D] = (
            own[:, D : 2 * D].astype(F32) + inv * scaled - xf * (inv * inv * inv) * mean
        ).astype(BF)

    return call(norm_back, [((Q, 2 * D), BF)], 5, 0)


def make_final(T, D, TP):
    Q = T // TP

    def final(fin, *rest):
        out_o, grad_o = rest[TP:]
        a = jnp.zeros((T, D), F32)
        b = jnp.zeros((T, D), F32)
        for e in range(TP):
            m = fin[:, e * Q : (e + 1) * Q]
            a = a + dot_nn(m, rest[e][:, 0:D])
            b = b + dot_nn(m, rest[e][:, D : 2 * D])
        out_o[...] = a.astype(BF)
        grad_o[...] = b.astype(BF)

    return call(final, [((T, D), BF)] * 2, 1 + TP, 0)


def halves(x):
    hi = x.astype(BF)
    return hi, (x - hi.astype(F32)).astype(BF)


def mul3(ah, al, bh, bl):
    return dot_nn(ah, bh) + (dot_nn(ah, bl) + dot_nn(al, bh))


def gram3(parts):
    def rows_of(i, b, n):
        at = slice(i * b, (i + 1) * b)
        tail = slice(i * b, n)
        tot = None
        for h, l in parts:
            one = dot_tn(h[:, at], h[:, tail]) + (dot_tn(h[:, at], l[:, tail]) + dot_tn(l[:, at], h[:, tail]))
            tot = one if tot is None else tot + one
        return tot

    return rows_of


def put_gram(o, parts, n):
    b = n // 3
    rows_of = gram3(parts)
    o[0:b, :] = rows_of(0, b, n)
    o[b : 2 * b, 0 : 2 * b] = rows_of(1, b, n)
    o[b : 2 * b, 2 * b : n] = rows_of(2, b, n)


def momentum_step(gradient, momentum_old):
    momentum_new = MOMENTUM * momentum_old + gradient
    return (momentum_new, gradient + MOMENTUM * momentum_new)


def add_parts(ref, cols):
    tot = ref[0, :, cols].astype(F32)
    for k in range(1, ref.shape[0]):
        tot = tot + ref[k, :, cols].astype(F32)
    return tot


def make_gram_out(G, rows, D):
    def gram_out(got, mom, g1_o, go_o, mo_o, uo_o, gram_o):
        g1_o[...] = add_parts(got, slice(0, D))
        g = add_parts(got, slice(D, 2 * D))
        m, u = momentum_step(g, mom[...])
        go_o[...] = g
        mo_o[...] = m
        uo_o[...] = u
        put_gram(gram_o, [halves(u)], D)

    outs = [((rows, D), F32)] * 4 + [((2 * D // 3, D), F32)]
    return call(gram_out, outs, 2, 0)


def make_gram_in(G, rows, D, XW, R, VR, pack):
    b = D // 3
    top = 2 * b

    def gram_in(got, g1, mom, xm, dm, vec, gi_o, mi_o, ui_o, gx_o, mx_o, gd_o, md_o, ux_o, buf_o):
        parts = []
        for q in range(2):
            g = add_parts(got, slice(0, D)) if q == 0 else g1[...]
            m, u = momentum_step(g, mom[:, q, :])
            gi_o[:, q, :] = g
            mi_o[:, q, :] = m
            ui_o[q * rows : (q + 1) * rows, :] = u
            parts.append(halves(u))
        put_gram(buf_o, parts, D)
        g = add_parts(got, slice(D, D + LANES))
        m, u = momentum_step(g, jnp.concatenate([xm[...], dm[...]], axis=1))
        gx_o[...] = g[:, 0:XW]
        gd_o[...] = g[:, XW : XW + R]
        mx_o[...] = m[:, 0:XW]
        md_o[...] = m[:, XW : XW + R]
        ux_o[...] = u
        h, l = halves(u)
        small = dot_tn(h, h) + (dot_tn(h, l) + dot_tn(l, h))
        buf_o[top : top + VR, :] = vec[...]
        for k in range(D // LANES):
            lo = k * pack
            hi = min(lo + pack, LANES)
            buf_o[top + VR : top + VR + hi - lo, k * LANES : (k + 1) * LANES] = small[lo:hi]
            if hi - lo < pack:
                buf_o[top + VR + hi - lo : top + VR + pack, k * LANES : (k + 1) * LANES] = jnp.zeros(
                    (pack - hi + lo, LANES), F32
                )
        used = top + VR + pack
        full = -(-used // 64) * 64
        if full > used:
            buf_o[used:full, :] = jnp.zeros((full - used, D), F32)

    full = -(-(top + VR + pack) // 64) * 64
    outs = [((rows, 2, D), F32)] * 2 + [((2 * rows, D), F32)]
    outs += [((rows, XW), F32)] * 2 + [((rows, R), F32)] * 2 + [((rows, LANES), F32), ((full, D), F32)]
    return call(gram_in, outs, 6, 0)


class Polar:
    def __init__(self, n, nbk, cuts, refs):
        self.n, self.nbk, self.cuts = n, nbk, list(cuts)
        self.blocks = n // nbk
        self.ah, self.al, self.qh, self.ql, self.th, self.tl, self.xs, self.acc = refs

    @staticmethod
    def scratch(n, rows):
        return [pltpu.VMEM((n, n), BF)] * 6 + [pltpu.VMEM((rows, n), F32), pltpu.VMEM((n, n), F32)]

    def at(self, b):
        return slice(b * self.nbk, (b + 1) * self.nbk)

    def put(self, i, value, hi_ref, lo_ref):
        h, l = halves(value)
        b = self.nbk
        hi_ref[self.at(i), i * b : self.n] = h
        lo_ref[self.at(i), i * b : self.n] = l
        for j in range(i + 1, self.blocks):
            h, l = halves(value[:, (j - i) * b : (j - i + 1) * b].T)
            hi_ref[self.at(j), self.at(i)] = h
            lo_ref[self.at(j), self.at(i)] = l

    def start(self, tails, upd):
        n, b = self.n, self.nbk
        col = lax.broadcasted_iota(jnp.int32, (1, n), 1)
        edges = [0] + self.cuts
        inv = jnp.zeros((1, n), F32)
        r = lax.broadcasted_iota(jnp.int32, (b, b), 0)
        c = lax.broadcasted_iota(jnp.int32, (b, b), 1)
        for lo, hi in zip(edges[:-1], edges[1:]):
            tot = jnp.zeros((1, 1), F32)
            for k in range(self.blocks):
                inside = (r == c) & (r + k * b >= lo) & (r + k * b < hi)
                d = jnp.sum(jnp.where(inside, tails[k][:, 0:b], 0.0), axis=1, keepdims=True)
                tot = tot + jnp.sum(d, axis=0, keepdims=True)
            inv = jnp.where((col >= lo) & (col < hi), 1.0 / (jnp.sqrt(tot) + 1e-07), inv)
        self.xs[...] = upd * inv
        for i in range(self.blocks):
            g = tails[i]
            if len(self.cuts) > 1:
                r = lax.broadcasted_iota(jnp.int32, g.shape, 0) + i * b
                c = lax.broadcasted_iota(jnp.int32, g.shape, 1) + i * b
                same = jnp.zeros(g.shape, F32)
                for lo, hi in zip(edges[:-1], edges[1:]):
                    same = jnp.where((r >= lo) & (r < hi) & (c >= lo) & (c < hi), 1.0, same)
                g = g * same
            one = inv[:, i * b : n]
            a = g * (one * one)
            self.acc[self.at(i), i * b : n] = a
            self.put(i, a, self.ah, self.al)

    def apply(self):
        for i in range(self.blocks):
            tail = slice(i * self.nbk, self.n)
            a2 = mul3(self.ah[self.at(i), :], self.al[self.at(i), :], self.ah[:, tail], self.al[:, tail])
            r = lax.broadcasted_iota(jnp.int32, a2.shape, 0)
            c = lax.broadcasted_iota(jnp.int32, a2.shape, 1)
            q = jnp.where(r == c, NS_A, 0.0) + (NS_B * self.acc[self.at(i), tail] + NS_C * a2)
            self.put(i, q, self.qh, self.ql)
        h, l = halves(self.xs[...])
        self.xs[...] = mul3(h, l, self.qh[...], self.ql[...])

    def advance(self):
        for src, dst in (((self.ah, self.al), (self.th, self.tl)), ((self.th, self.tl), (self.ah, self.al))):
            for i in range(self.blocks):
                tail = slice(i * self.nbk, self.n)
                a = mul3(src[0][self.at(i), :], src[1][self.at(i), :], self.qh[:, tail], self.ql[:, tail])
                if dst[0] is self.ah:
                    self.acc[self.at(i), tail] = a
                self.put(i, a, *dst)


def unpack_gram(buf, n):
    b = n // 3
    return [buf[0:b, :], buf[b : 2 * b, 0 : 2 * b], buf[b : 2 * b, 2 * b : n]]


def make_muon_out(D, rows, rate):
    def muon_out(buf, upd, wgt, o, *refs):
        p = Polar(D, D // 3, (D,), refs)
        p.start(unpack_gram(buf, D), upd[...])

        def step(k, c):
            p.apply()
            p.advance()
            return c

        lax.fori_loop(0, 4, step, 0)
        p.apply()
        o[...] = wgt[...] - rate * p.xs[...]

    return call(muon_out, [((rows, D), F32)], 3, 0, Polar.scratch(D, rows))


def make_muon_in(D, rows, XW, R, VR, pack, rate, rate_x, rate_dt):
    top = 2 * (D // 3)

    def muon_in(buf, upd, wgt, ux, wx, wd, o, ox, od, *refs):
        p = Polar(D, D // 3, (D,), refs[:8])
        s = Polar(LANES, LANES, (XW, XW + R), refs[8:16])
        small = jnp.concatenate(
            [
                buf[top + VR : top + VR + min(pack, LANES - k * pack), k * LANES : (k + 1) * LANES]
                for k in range(-(-LANES // pack))
            ],
            axis=0,
        )
        p.start(unpack_gram(buf, D), upd[...])
        s.start([small], ux[...])

        def step(k, c):
            p.apply()
            s.apply()
            p.advance()
            s.advance()
            return c

        lax.fori_loop(0, 4, step, 0)
        p.apply()
        s.apply()
        for q in range(2):
            o[:, q, :] = wgt[:, q, :] - rate * p.xs[q * rows : (q + 1) * rows, :]
        ox[...] = wx[...] - rate_x * s.xs[:, 0:XW]
        od[...] = wd[...] - rate_dt * s.xs[:, XW : XW + R]

    outs = [((rows, 2, D), F32), ((rows, XW), F32), ((rows, R), F32)]
    return call(muon_in, outs, 6, 0, Polar.scratch(D, 2 * rows) + Polar.scratch(LANES, rows))


def make_pack(rows, D, XW, R):
    def pack(wi, wx, wd, wo, a_o, r_o):
        a_o[...] = wi[:, 0, :].astype(BF)
        r_o[:, 0:D] = wi[:, 1, :].astype(BF)
        r_o[:, D : D + LANES] = jnp.concatenate([wx[...], wd[...]], axis=1).astype(BF)
        r_o[:, D + LANES : 2 * D + LANES] = wo[...].astype(BF)

    return call(pack, [((rows, D), BF), ((rows, 2 * D + LANES), BF)], 4, 0)


def shifted(value, axis, by):
    devices = lax.axis_size(axis)
    pairs = [(i, i + by) for i in range(devices) if 0 <= i + by < devices]
    return lax.ppermute(value, axis, pairs)


def swap(value, axis, bit):
    devices = lax.axis_size(axis)
    return lax.ppermute(value, axis, [(i, i ^ bit) for i in range(devices)])


def side(axis, bit):
    return jnp.where((lax.axis_index(axis) & bit) != 0, 1, 0)


def in_order(mine, theirs, axis, bit):
    low = side(axis, bit) == 0
    return jnp.concatenate([jnp.where(low, mine, theirs), jnp.where(low, theirs, mine)], axis=0)


def half_sum(value, axis, bit):
    half = value.shape[0] // 2
    mine = side(axis, bit) * half
    away = lax.dynamic_slice_in_dim(value, half - mine, half)
    kept = lax.dynamic_slice_in_dim(value, mine, half)
    return kept + swap(away, axis, bit)


def half_join(value, axis, bit):
    return in_order(value, swap(value, axis, bit), axis, bit)


def bits_of(axis):
    count = lax.axis_size(axis)
    return [1 << k for k in range(count.bit_length() - 1)]


def sum_all(value):
    value = half_sum(value, "tp", 1)
    cols = value.shape[1] // 2
    done = []
    for k in range(2):
        part = value[:, k * cols : (k + 1) * cols]
        cut = [("tp", 2), ("fsdp", 1)] if k == 0 else [("ctx", 1), ("ctx", 2)]
        rest = [(a, b) for a in ("tp", "fsdp", "ctx") for b in bits_of(a) if (a, b) not in cut + [("tp", 1)]]
        for axis, bit in cut:
            part = half_sum(part, axis, bit)
        for axis, bit in rest:
            part = part + swap(part, axis, bit)
        for axis, bit in cut[::-1]:
            part = half_join(part, axis, bit)
        done.append(part)
    return half_join(jnp.concatenate(done, axis=1), "tp", 1)


def gather_fsdp(value):
    if lax.axis_size("fsdp") == 2:
        return in_order(value, swap(value, "fsdp", 1), "fsdp", 1)
    return lax.all_gather(value, "fsdp", axis=0, tiled=True)


def adam_update(parameters, gradient, moment_one, moment_two, adam_step):
    count = adam_step[0].astype(jnp.float32)
    first_new = BETA_ONE * moment_one + (1.0 - BETA_ONE) * gradient
    second_new = BETA_TWO * moment_two + (1.0 - BETA_TWO) * gradient * gradient
    first_hat = first_new / (1.0 - jnp.power(jnp.float32(BETA_ONE), count))
    second_hat = second_new / (1.0 - jnp.power(jnp.float32(BETA_TWO), count))
    updated = parameters - ADAM_RATE * (
        first_hat / (jnp.sqrt(second_hat) + ADAM_EPS) + DECAY_RATE * parameters
    )
    return (updated, first_new, second_new)


def on_device(
    block_input,
    cotangent,
    route_perm,
    doc_lengths,
    norm_gain,
    in_proj,
    conv_weight,
    conv_bias,
    x_proj,
    dt_proj,
    dt_bias,
    a_log,
    skip_gain,
    out_proj,
    in_momentum,
    x_momentum,
    dt_momentum,
    out_momentum,
    adam_first,
    adam_second,
    adam_step,
):
    ctx_count = lax.axis_size("ctx")
    fsdp_count = lax.axis_size("fsdp")
    tp_count = lax.axis_size("tp")
    owners = fsdp_count * ctx_count
    ctx_index = lax.axis_index("ctx")
    tp_index = lax.axis_index("tp")
    tokens, width = block_input.shape
    stream = tokens * ctx_count
    quarter = tokens // tp_count
    own_rows = in_proj.shape[0]
    channels = own_rows * owners
    inner = conv_bias.shape[0]
    states = a_log.shape[0]
    rank = dt_proj.shape[1]
    xw = x_proj.shape[1]
    lengths = doc_lengths[0]
    docs = lengths.shape[0]
    offsets = jnp.cumsum(lengths) - lengths
    scal = jnp.concatenate([(tp_index * channels)[None], offsets - ctx_index * tokens]).astype(jnp.int32)
    place = jnp.stack([ctx_index, tp_index]).astype(jnp.int32)
    perm_row = (route_perm % stream).reshape(1, stream)
    gain_row = norm_gain.reshape(1, width)

    w_a, w_r = make_pack(own_rows, width, xw, rank)(in_proj, x_proj, dt_proj, out_proj)
    send, fin = make_send(tokens, width, ctx_count, tp_count)(place, perm_row, block_input, cotangent)
    sent = lax.all_to_all(
        send.reshape(ctx_count, quarter // ctx_count, 2 * width), "ctx", split_axis=0, concat_axis=0, tiled=True
    )
    w_rest = gather_fsdp(lax.all_gather(w_r, "ctx", axis=0, tiled=True))
    w_in = gather_fsdp(lax.all_gather(w_a, "ctx", axis=0, tiled=True))
    own = sent.reshape(quarter, 2 * width)
    far = swap(own, "tp", 2)
    stream_x, stream_dy, normed, route = make_recv(tokens, width, ctx_count, tp_count)(
        place, perm_row, gain_row, own, swap(own, "tp", 1), far, swap(far, "tp", 1)
    )

    halo = shifted(normed[tokens - 8 :], "ctx", 1)
    conv_in, gate_in, conv_act, conv_out, pt_part, d_gated, w_turn = make_front(
        tokens, channels, width, docs, xw, rank
    )(scal, normed, halo, stream_dy, w_in, w_rest, conv_weight, conv_bias.reshape(1, inner))
    x_halo = shifted(conv_in[tokens - 8 :].astype(F32), "ctx", 1)
    pt_pair = pt_part + swap(pt_part, "tp", 1)
    pt, dec, drv, d_inner, pre, h_end, g_end = make_carry(
        tokens, channels, docs, xw, rank, states
    )(scal, pt_pair, swap(pt_pair, "tp", 2), conv_act, gate_in, d_gated, w_turn, dt_bias.reshape(1, inner), a_log)
    gate_low, d_gate, du_one, d_pre_low, dp_part, mix_part, grads_one, part_dt, vec_part = make_scan(
        tokens, channels, width, docs, xw, rank, states
    )(
        scal, pt, dec, drv, d_inner, pre, conv_act, gate_in, d_gated, stream_dy, normed, w_rest, w_turn, a_log,
        skip_gain.reshape(1, inner), shifted(h_end, "ctx", 1), shifted(h_end, "ctx", 2),
        shifted(g_end, "ctx", -1), shifted(g_end, "ctx", -2),
    )

    def to_owners(grads):
        return lax.all_to_all(
            grads.reshape(owners, own_rows, grads.shape[1]), ("fsdp", "ctx"), split_axis=0, concat_axis=0, tiled=True
        )

    got_one = to_owners(grads_one)
    dp_pair = dp_part + swap(dp_part, "tp", 1)
    d_conv_in, spill, part_xdt, vec_chan = make_back(tokens, channels, width, docs, xw, rank)(8 + states)(
        scal, dp_pair, swap(dp_pair, "tp", 2), du_one, conv_out, conv_act, conv_in, x_halo, w_turn, conv_weight,
        vec_part, part_dt,
    )
    keep, away, grads_two, g_gain = make_last(tokens, channels, width, quarter)(
        d_conv_in, shifted(spill, "ctx", -1), d_gate, normed, w_in, w_rest, part_xdt, mix_part, stream_x, route
    )
    got_two = to_owners(grads_two)

    near = swap(away, "tp", 1)
    cross = (keep[quarter:].astype(F32) + near[quarter:].astype(F32)).astype(BF)
    back = make_norm_back(quarter, width)(keep, near, swap(cross, "tp", 2), own, gain_row)[0]
    home = lax.all_to_all(
        back.reshape(ctx_count, quarter // ctx_count, 2 * width), "ctx", split_axis=0, concat_axis=0, tiled=True
    ).reshape(quarter, 2 * width)
    home_far = swap(home, "tp", 2)
    block_out, input_grad = make_final(tokens, width, tp_count)(
        fin, home, swap(home, "tp", 1), home_far, swap(home_far, "tp", 1)
    )

    kinds = 8 + states
    pack = 24
    vec_wide = lax.dynamic_update_slice(jnp.zeros((kinds, inner), F32), vec_chan, (0, tp_index * channels))
    vec_wide = vec_wide + jnp.pad(g_gain, ((7, kinds - 8), (0, inner - width)))
    vec_rows = kinds * inner // width
    g_one, g_out, mom_out, upd_out, gram_out = make_gram_out(owners, own_rows, width)(got_one, out_momentum)
    g_in, mom_in, upd_in, g_x, mom_x, g_dt, mom_dt, upd_xdt, gram_in = make_gram_in(
        owners, own_rows, width, xw, rank, vec_rows, pack
    )(got_two, g_one, in_momentum, x_momentum, dt_momentum, vec_wide.reshape(vec_rows, width))
    all_out = sum_all(gram_out)
    all_in = sum_all(gram_in)
    rate = MUON_RATE * 0.2
    new_out = make_muon_out(width, own_rows, rate * math.sqrt(max(inner, width)))(all_out, upd_out, out_proj)[0]
    new_in, new_x, new_dt = make_muon_in(
        width, own_rows, xw, rank, vec_rows, pack,
        rate * math.sqrt(max(2 * inner, width)), rate * math.sqrt(max(inner, xw)), rate * math.sqrt(max(inner, rank)),
    )(all_in, upd_in, in_proj, upd_xdt, x_proj, dt_proj)

    top = 2 * (width // 3)
    vec_sum = all_in[top : top + vec_rows].reshape(kinds, inner)
    g_alog = vec_sum[8:]
    vec_grads = jnp.concatenate(
        [vec_sum[7, :width], vec_sum[0:4].reshape(-1), vec_sum[4], vec_sum[5], g_alog.reshape(-1), vec_sum[6]]
    )
    vec_params = jnp.concatenate(
        [norm_gain, conv_weight.reshape(-1), conv_bias, dt_bias, a_log.reshape(-1), skip_gain]
    )
    new_vec, first_new, second_new = adam_update(vec_params, vec_grads, adam_first, adam_second, adam_step)
    cut_b = width + 4 * inner
    cut_c = cut_b + inner
    cut_d = cut_c + inner
    cut_e = cut_d + states * inner
    return (
        block_out,
        input_grad,
        vec_sum[7, :width],
        g_in,
        vec_sum[0:4],
        vec_sum[4],
        g_x,
        g_dt,
        vec_sum[5],
        g_alog,
        vec_sum[6],
        g_out,
        new_vec[:width],
        new_in,
        new_vec[width:cut_b].reshape(4, inner),
        new_vec[cut_b:cut_c],
        new_x,
        new_dt,
        new_vec[cut_c:cut_d],
        new_vec[cut_d:cut_e].reshape(states, inner),
        new_vec[cut_e:],
        new_out,
        mom_in,
        mom_x,
        mom_dt,
        mom_out,
        first_new,
        second_new,
    )


def solution(mesh):
    return jax.shard_map(
        on_device,
        mesh=mesh,
        in_specs=(
            P(("fsdp", "ctx"), None),
            P(("fsdp", "ctx"), None),
            P("fsdp"),
            P("fsdp", None),
            P(),
            P(("tp", "fsdp", "ctx"), None, None),
            P(),
            P(),
            P(("tp", "fsdp", "ctx"), None),
            P(("tp", "fsdp", "ctx"), None),
            P(),
            P(),
            P(),
            P(("tp", "fsdp", "ctx"), None),
            P(("tp", "fsdp", "ctx"), None, None),
            P(("tp", "fsdp", "ctx"), None),
            P(("tp", "fsdp", "ctx"), None),
            P(("tp", "fsdp", "ctx"), None),
            P(),
            P(),
            P(),
        ),
        out_specs=(
            P(("fsdp", "ctx"), None),
            P(("fsdp", "ctx"), None),
            P(),
            P(("tp", "fsdp", "ctx"), None, None),
            P(),
            P(),
            P(("tp", "fsdp", "ctx"), None),
            P(("tp", "fsdp", "ctx"), None),
            P(),
            P(),
            P(),
            P(("tp", "fsdp", "ctx"), None),
            P(),
            P(("tp", "fsdp", "ctx"), None, None),
            P(),
            P(),
            P(("tp", "fsdp", "ctx"), None),
            P(("tp", "fsdp", "ctx"), None),
            P(),
            P(),
            P(),
            P(("tp", "fsdp", "ctx"), None),
            P(("tp", "fsdp", "ctx"), None, None),
            P(("tp", "fsdp", "ctx"), None),
            P(("tp", "fsdp", "ctx"), None),
            P(("tp", "fsdp", "ctx"), None),
            P(),
            P(),
        ),
        check_vma=False,
    )
```

```python
import math

import jax
import jax.numpy as jnp
from jax import lax
from jax.experimental import pallas as pl
from jax.experimental.pallas import tpu as pltpu
from jax.sharding import PartitionSpec as P

F32 = jnp.float32
BF = jnp.bfloat16
LANES = 128
RESET = 1e5
LOG2E = 1.4426950408889634
VMEM_LIMIT = 60 * 1024 * 1024
NS_A = 3.4445
NS_B = -4.775
NS_C = 2.0315
MOMENTUM = 0.95
MUON_RATE = 0.1
ADAM_RATE = 0.25
BETA_ONE = 0.9
BETA_TWO = 0.95
ADAM_EPS = 1e-08
DECAY_RATE = 0.01
NORM_EPS = 1e-05


def dot_nn(a, b):
    return lax.dot_general(a, b, (((1,), (0,)), ((), ())), preferred_element_type=F32)


def dot_nt(a, b):
    return lax.dot_general(a, b, (((1,), (1,)), ((), ())), preferred_element_type=F32)


def dot_tn(a, b):
    return lax.dot_general(a, b, (((0,), (0,)), ((), ())), preferred_element_type=F32)


def soft(x):
    return jnp.maximum(x, 0.0) + jnp.log1p(jnp.exp(-jnp.abs(x)))


def slope_of(a, s):
    return s * (1.0 + a * (1.0 - s))


def call(body, outs, n_in, n_smem, scratch=(), flops=10**9):
    specs = [pl.BlockSpec(memory_space=pltpu.SMEM)] * n_smem + [
        pl.BlockSpec(memory_space=pltpu.VMEM)
    ] * (n_in - n_smem)
    return pl.pallas_call(
        body,
        out_shape=[jax.ShapeDtypeStruct(s, d) for s, d in outs],
        in_specs=specs,
        out_specs=[pl.BlockSpec(memory_space=pltpu.VMEM)] * len(outs),
        scratch_shapes=list(scratch),
        compiler_params=pltpu.CompilerParams(vmem_limit_bytes=VMEM_LIMIT),
        name=body.__name__,
    )


def rows_iota(r0, rows):
    return lax.broadcasted_iota(jnp.int32, (rows, LANES), 0) + r0


def tap_mask(sc_ref, docs, p, shift):
    ok = jnp.ones(p.shape, F32)
    for j in range(docs):
        off = sc_ref[1 + j]
        ok = jnp.where((off <= p) & (p < off + shift), 0.0, ok)
    return ok


def wide(mask, width):
    return jnp.concatenate([mask] * (width // LANES), axis=1)


def make_front(T, C, D, docs, XW, R):
    RB = 64

    def front(sc, hb, halo, dy, wa, wr, cw, cb, xu_o, z_o, u_o, v_o, pt_o, dg_o, wt_o, xh_o, xpad):
        w0 = wa[...]
        w1 = wr[:, 0:D]
        wo = wr[:, D + LANES : 2 * D + LANES]
        wt = wr[:, D : D + LANES].astype(F32).T.astype(BF)
        wt_o[...] = wt
        c0 = pl.multiple_of(sc[0], LANES)
        xh = dot_nt(halo[...], w0).astype(BF).astype(F32)
        xpad[0:8, :] = xh
        xh_o[...] = xh
        xu = dot_nt(hb[...], w0).astype(BF)
        xu_o[...] = xu
        xpad[8 : 8 + T, :] = xu.astype(F32)
        z_o[...] = dot_nt(hb[...], w1).astype(BF)
        dg_o[...] = dot_nt(dy[...], wo)
        taps = [cw[k : k + 1, pl.ds(c0, C)] for k in range(4)]
        bias = cb[0:1, pl.ds(c0, C)]

        def block(i, carry):
            r0 = i * RB
            p = rows_iota(r0, RB)
            v = bias + jnp.zeros((RB, C), F32)
            full = xpad[pl.ds(r0, RB + 8), :]
            for k in range(4):
                s = 3 - k
                x = full[8 - s : 8 - s + RB]
                if s:
                    x = x * wide(tap_mask(sc, docs, p, s), C)
                v = v + taps[k] * x
            v_o[pl.ds(r0, RB), :] = v
            u_o[pl.ds(r0, RB), :] = (v / (1.0 + jnp.exp(-v))).astype(BF)
            return carry

        lax.fori_loop(0, T // RB, block, 0)
        pt_o[...] = dot_nt(wt[0:XW], u_o[...])

    outs = [((T, C), BF), ((T, C), BF), ((T, C), BF), ((T, C), F32), ((XW, T), F32), ((T, C), F32), ((LANES, C), BF), ((8, C), F32)]
    return call(front, outs, 8, 1, [pltpu.VMEM((T + 8, C), F32)])


def lane_sums(ref):
    def join(a, b, w):
        m = (lax.broadcasted_iota(jnp.int32, a.shape, 2) & w) == 0
        if w == LANES // 2:
            return jnp.where(m, a, b) + pltpu.roll(jnp.where(m, b, a), w, 2)
        return jnp.where(m, a, b) + jnp.where(m, pltpu.roll(a, LANES - w, 2), pltpu.roll(b, w, 2))

    w = LANES // 2
    while w >= 8:

        def chunk(i, c, w=w):
            ref[pl.ds(i * 8, 8)] = join(ref[pl.ds(i * 8, 8)], ref[pl.ds(i * 8 + w, 8)], w)
            return c

        lax.fori_loop(0, w // 8, chunk, 0)
        w //= 2
    x = ref[0:8]
    while w:
        x = join(x[0:w], x[w : 2 * w], w)
        w //= 2
    return x[0]


def make_carry(T, C, docs, XW, R, N, CT):
    RB = 64
    LT = C // LANES

    def carry(sc, pa, pb, u, z, dg, wt, dtb, alog, pt_o, da_o, du_o, dyin_o, pre_o, ends_o):
        c0 = pl.multiple_of(sc[0], LANES)
        pt = pa[...] + pb[...]
        pt_o[...] = pt
        lin = dot_tn(pt[0:R].astype(BF), wt[XW : XW + R, :])
        pre_o[...] = lin + dtb[0:1, pl.ds(c0, C)]

        def block(i, tot):
            rs = pl.ds(i * RB, RB)
            p = rows_iota(i * RB, RB)
            keep = jnp.ones((RB, LANES), F32)
            for j in range(docs):
                keep = jnp.where(p == sc[1 + j], 0.0, keep)
            x = pre_o[rs, :]
            delta = soft(x)
            d = jnp.where(wide(keep, C) > 0.0, delta, RESET)
            r8 = pl.ds(i * (RB // 8), RB // 8)
            da_o[r8] = d.reshape(RB // 8, 8, C)
            du_o[r8] = (delta * u[rs, :].astype(F32)).reshape(RB // 8, 8, C)
            zf = z[rs, :].astype(F32)
            dyin_o[r8] = (dg[rs, :] * (zf / (1.0 + jnp.exp(-zf)))).reshape(RB // 8, 8, C)
            return tot + jnp.sum(d, axis=0, keepdims=True)

        tot = lax.fori_loop(0, T // RB, block, jnp.zeros((1, C), F32))
        am = [-jnp.exp(alog[:, pl.ds(c0 + l * LANES, LANES)]) for l in range(LT)]
        am2 = [a * LOG2E for a in am]

        def rows(ref, i, j):
            full = ref[i, pl.ds(j, N, stride=0), :]
            return [full[:, l * LANES : (l + 1) * LANES] for l in range(LT)]

        nb = T // LANES

        def outer(k, c):
            bt = pt_o[R_ : R_ + N, pl.ds(pl.multiple_of(k * LANES, LANES), LANES)]
            ct = pt_o[R_ + N : R_ + 2 * N, pl.ds(pl.multiple_of((nb - 1 - k) * LANES, LANES), LANES)]

            def inner(i, c):
                h, g, bt, ct = c
                h = list(h)
                g = list(g)
                fi = k * (LANES // 8) + i
                ri = T // 8 - 1 - fi
                for j in range(8):
                    bb = jnp.broadcast_to(bt[:, j : j + 1], (N, LANES))
                    cc = jnp.broadcast_to(ct[:, LANES - 1 - j : LANES - j], (N, LANES))
                    df, uf = rows(da_o, fi, j), rows(du_o, fi, j)
                    db, yb = rows(da_o, ri, 7 - j), rows(dyin_o, ri, 7 - j)
                    for l in range(LT):
                        h[l] = jnp.exp2(df[l] * am2[l]) * h[l] + uf[l] * bb
                        g[l] = jnp.exp2(db[l] * am2[l]) * (g[l] + yb[l] * cc)
                return tuple(h), tuple(g), pltpu.roll(bt, LANES - 8, 1), pltpu.roll(ct, 8, 1)

            h, g, _, _ = lax.fori_loop(0, LANES // 8, inner, (c[0], c[1], bt, ct))
            return h, g

        R_ = R
        zero = tuple(jnp.zeros((N, LANES), F32) for _ in range(LT))
        h, g = lax.fori_loop(0, nb, outer, (zero, zero))
        here = sc[1 + docs]
        for d in range(CT):
            for l in range(LT):
                ends_o[d, 0:N, l * LANES : (l + 1) * LANES] = jnp.where(d > here, h[l], g[l])
            ends_o[d, N : N + 8, :] = jnp.broadcast_to(tot, (8, C))

    outs = [((XW, T), F32)] + [((T // 8, 8, C), F32)] * 3 + [((T, C), F32)] + [((CT, N + 8, C), F32)]
    return call(carry, outs, 9, 1)


def make_scan(T, C, D, docs, XW, R, N, CT):
    RB = 64
    LT = C // LANES
    nb = T // LANES

    def scan(sc, pt, da, du, dyin, pre, u, z, dg, dy, hb, wr, wt, alog, skip, ends,
             g_o, dz_o, du1_o, dpre_o, dp_o, mix_o, pw_o, pdt_o, vec_o,
             a_s, h_s, y_s, lb_s, dd_s, sb_s, sc_s):
        c0 = pl.multiple_of(sc[0], LANES)
        am = [-jnp.exp(alog[:, pl.ds(c0 + l * LANES, LANES)]) for l in range(LT)]
        am2 = [a * LOG2E for a in am]
        sl = [slice(l * LANES, (l + 1) * LANES) for l in range(LT)]
        top4 = lax.broadcasted_iota(jnp.int32, (8, LANES), 0) < 4

        def rows(ref, i, j):
            full = ref[i, pl.ds(j, N, stride=0), :]
            return [full[:, sl[l]] for l in range(LT)]

        here = sc[1 + docs]
        hin, gin = [], []
        for l in range(LT):
            for way, got in ((-1, hin), (1, gin)):
                one = jnp.clip(here + way, 0, CT - 1)
                two = jnp.clip(here + 2 * way, 0, CT - 1)
                prod = jnp.exp2(jnp.broadcast_to(ends[one, N : N + 1, sl[l]], (N, LANES)) * am2[l])
                far = jnp.where(here + 2 * way == two, ends[two, 0:N, sl[l]], 0.0)
                got.append(jnp.where(here + way == one, ends[one, 0:N, sl[l]] + prod * far, 0.0))
            h_s[0, :, sl[l]] = hin[l]

        def fouter(k, h):
            blk = pl.ds(pl.multiple_of(k * LANES, LANES), LANES)
            bt = pt[R : R + N, blk]
            ct = pt[R + N : R + 2 * N, blk]

            def inner(i, c):
                h, bt, ct = c
                h = list(h)
                fi = k * (LANES // 8) + i
                for j in range(8):
                    t = fi * 8 + j
                    bb = jnp.broadcast_to(bt[:, j : j + 1], (N, LANES))
                    cc = jnp.broadcast_to(ct[:, j : j + 1], (N, LANES))
                    dr, ur = rows(da, fi, j), rows(du, fi, j)
                    for l in range(LT):
                        a = jnp.exp2(dr[l] * am2[l])
                        a_s[t, :, sl[l]] = a
                        h[l] = a * h[l] + ur[l] * bb
                        h_s[t + 1, :, sl[l]] = h[l]
                        y_s[fi, j : j + 1, sl[l]] = jnp.sum(h[l] * cc, axis=0, keepdims=True)
                return tuple(h), pltpu.roll(bt, LANES - 8, 1), pltpu.roll(ct, LANES - 8, 1)

            return lax.fori_loop(0, LANES // 8, inner, (h, bt, ct))[0]

        lax.fori_loop(0, nb, fouter, tuple(hin))

        def bouter(k, c):
            kb = nb - 1 - k
            blk = pl.ds(pl.multiple_of(kb * LANES, LANES), LANES)
            bt = pt[R : R + N, blk]
            ct = pt[R + N : R + 2 * N, blk]
            zero = jnp.zeros((N, LANES), F32)

            def inner(i, c):
                g, ga, bt, ct = c
                g = list(g)
                ga = list(ga)
                l0 = LANES - 1 - i * 8
                fi = kb * (LANES // 8) + LANES // 8 - 1 - i
                for j in range(8):
                    t = kb * LANES + l0 - j
                    jj = 7 - j
                    bb = jnp.broadcast_to(bt[:, LANES - 1 - j : LANES - j], (N, LANES))
                    cc = jnp.broadcast_to(ct[:, LANES - 1 - j : LANES - j], (N, LANES))
                    sb = zero
                    scc = zero
                    dr, ur, yr = rows(da, fi, jj), rows(du, fi, jj), rows(dyin, fi, jj)
                    for l in range(LT):
                        dyr = yr[l]
                        lam = cc * dyr + g[l]
                        g[l] = a_s[t, :, sl[l]] * lam
                        dal = g[l] * h_s[t, :, sl[l]]
                        pb = lam * bb
                        pd = dal * am[l]
                        pb = pb[0:8] + pb[8:16]
                        pd = pd[0:8] + pd[8:16]
                        both = jnp.where(top4, pb, pd) + pltpu.roll(jnp.where(top4, pd, pb), 4, 0)
                        both = both + pltpu.roll(both, 6, 0)
                        both = both + pltpu.roll(both, 7, 0)
                        lb_s[fi, jj : jj + 1, sl[l]] = both[0:1]
                        dd_s[fi, jj : jj + 1, sl[l]] = both[4:5]
                        ga[l] = ga[l] + dal * dr[l]
                        sb = sb + lam * ur[l]
                        scc = scc + dyr * h_s[t + 1, :, sl[l]]
                    sb_s[l0 - j] = sb
                    sc_s[l0 - j] = scc
                return tuple(g), tuple(ga), pltpu.roll(bt, 8, 1), pltpu.roll(ct, 8, 1)

            g, ga, _, _ = lax.fori_loop(0, LANES // 8, inner, (c[0], c[1], bt, ct))
            dp_o[R : R + N, blk] = lane_sums(sb_s)
            dp_o[R + N : R + 2 * N, blk] = lane_sums(sc_s)
            return g, ga

        zeros = tuple(jnp.zeros((N, LANES), F32) for _ in range(LT))
        _, ga = lax.fori_loop(0, nb, bouter, (tuple(gin), zeros))
        for l in range(LT):
            vec_o[8 : 8 + N, sl[l]] = am[l] * ga[l]
        skr = skip[0:1, pl.ds(c0, C)]

        def block(i, tot):
            gdt, gsk = tot
            rs = pl.ds(i * RB, RB)
            r8 = pl.ds(i * (RB // 8), RB // 8)
            uf = u[rs, :].astype(F32)
            zf = z[rs, :].astype(F32)
            s = 1.0 / (1.0 + jnp.exp(-zf))
            yin = y_s[r8].reshape(RB, C) + skr * uf
            g_o[rs, :] = (yin * (zf * s)).astype(BF)
            dz_o[rs, :] = (dg[rs, :] * yin * slope_of(zf, s)).astype(BF)
            lb = lb_s[r8].reshape(RB, C)
            dyr = dyin[r8].reshape(RB, C)
            x = pre[rs, :]
            dpre = (lb * uf + dd_s[r8].reshape(RB, C)) / (1.0 + jnp.exp(-x))
            dpre_o[rs, :] = dpre.astype(BF)
            du1_o[rs, :] = dyr * skr + lb * soft(x)
            return gdt + jnp.sum(dpre, axis=0, keepdims=True), gsk + jnp.sum(dyr * uf, axis=0, keepdims=True)

        z1 = jnp.zeros((1, C), F32)
        gdt, gsk = lax.fori_loop(0, T // RB, block, (z1, z1))
        vec_o[5:6, :] = gdt
        vec_o[6:7, :] = gsk
        vec_o[7:8, :] = z1
        vec_o[0:5, :] = jnp.zeros((5, C), F32)
        dp_o[0:R, :] = dot_nt(wt[XW : XW + R, :], dpre_o[...])
        pdt_o[...] = dot_nn(pt[0:R, :].astype(BF), dpre_o[...])
        mix_o[...] = dot_nn(g_o[...], wr[:, D + LANES : 2 * D + LANES]).astype(BF)
        pw_o[:, 0:D] = dot_tn(dz_o[...], hb[...]).astype(BF)
        pw_o[:, D : 2 * D] = dot_tn(g_o[...], dy[...]).astype(BF)

    outs = [((T, C), BF), ((T, C), BF), ((T, C), F32), ((T, C), BF), ((XW, T), F32), ((T, D), BF),
            ((C, 2 * D), BF), ((R, C), F32), ((8 + N, C), F32)]
    scratch = [pltpu.VMEM((T, N, C), F32), pltpu.VMEM((T + 1, N, C), F32)] + [pltpu.VMEM((T // 8, 8, C), F32)] * 3
    scratch += [pltpu.VMEM((LANES, N, LANES), F32)] * 2
    return call(scan, outs, 16, 1, scratch)


def make_back(T, C, D, docs, XW, R):
    RB = 64

    def back(sc, da_, db_, du1, v, u, xu, xhalo, wt, cw, vec, pdt, hb, halo, dxu_o, spill_o, pxt_o, vec_o, pad1, pad2, pad3, xpad):
        c0 = pl.multiple_of(sc[0], LANES)
        dpl = (da_[...] + db_[...]).astype(BF)
        pxt_o[:, D : D + LANES] = jnp.concatenate([dot_nn(dpl, u[...]), pdt[...]], axis=0).T.astype(BF)
        dxu_o[...] = du1[...] + dot_tn(dpl, wt[0:XW, :])
        pads = {1: pad1, 2: pad2, 3: pad3}
        xpad[0:8, :] = xhalo[...]
        xpad[8 : 8 + T, :] = xu[...].astype(F32)
        taps = [cw[k : k + 1, pl.ds(c0, C)] for k in range(4)]
        z8 = jnp.zeros((8, C), F32)
        for s in (1, 2, 3):
            pads[s][0:8, :] = z8
            pads[s][8 + T : 16 + T, :] = z8

        def block(i, tot):
            r0 = i * RB
            rs = pl.ds(r0, RB)
            p = rows_iota(r0, RB)
            vf = v[rs, :]
            sg = 1.0 / (1.0 + jnp.exp(-vf))
            dv = dxu_o[rs, :] * slope_of(vf, sg)
            new = [None] * 5
            full = xpad[pl.ds(r0, RB + 8), :]
            new[4] = tot[4] + jnp.sum(dv, axis=0, keepdims=True)
            for k in range(4):
                s = 3 - k
                x = full[8 - s : 8 - s + RB]
                m = dv
                if s:
                    m = dv * wide(tap_mask(sc, docs, p, s), C)
                    pads[s][pl.ds(8 + r0, RB), :] = taps[k] * m
                else:
                    dxu_o[rs, :] = taps[k] * m
                new[k] = tot[k] + jnp.sum(m * x, axis=0, keepdims=True)
            return tuple(new)

        z1 = jnp.zeros((1, C), F32)
        tot = lax.fori_loop(0, T // RB, block, (z1,) * 5)
        vec_o[...] = vec[...]
        for k in range(5):
            vec_o[k : k + 1, :] = tot[k]

        def gather(i, c):
            r0 = i * RB
            rs = pl.ds(r0, RB)
            acc = dxu_o[rs, :]
            for s in (1, 2, 3):
                acc = acc + pads[s][pl.ds(8 + r0, RB + 8), :][s : s + RB]
            dxu_o[rs, :] = acc
            return c

        lax.fori_loop(0, T // RB, gather, 0)
        acc = z8
        for s in (1, 2, 3):
            acc = acc + pads[s][s : s + 8, :]
        spill_o[...] = acc
        own = dot_tn(dxu_o[...].astype(BF), hb[...])
        pxt_o[:, 0:D] = (own + dot_tn(acc.astype(BF), halo[...])).astype(BF)

    outs = [((T, C), F32), ((8, C), F32), ((C, D + LANES), BF), (None, F32)]

    def build(vrows):
        o = outs[:3] + [((vrows, C), F32)]
        return call(back, o, 14, 1, [pltpu.VMEM((T + 16, C), F32)] * 3 + [pltpu.VMEM((T + 8, C), F32)])

    return build


def make_last(T, C, D, Q):
    def last(dxu, spill, dz, wa, wr, mix, x, rt, keep_o, send_o, gain_o):
        low = jnp.concatenate([jnp.zeros((T - 8, C), F32), spill[...]], axis=0)
        dx = (dxu[...] + low).astype(BF)
        dn = dot_nn(dx, wa[...]) + dot_nn(dz[...], wr[:, 0:D])
        xf = x[...].astype(F32)
        inv = lax.rsqrt(jnp.mean(xf * xf, axis=1, keepdims=True) + NORM_EPS)
        gain_o[...] = jnp.sum(dn * xf * inv, axis=0, keepdims=True)
        dnl = dn.astype(BF)
        for e in range(T // Q):
            r = rt[:, e * Q : (e + 1) * Q]
            o = send_o if e % 2 else keep_o
            at = slice((e // 2) * Q, (e // 2 + 1) * Q)
            o[at, 0:D] = dot_tn(r, mix[...]).astype(BF)
            o[at, D : 2 * D] = dot_tn(r, dnl).astype(BF)

    half = T // 2
    outs = [((half, 2 * D), BF), ((half, 2 * D), BF), ((1, D), F32)]
    return call(last, outs, 8, 0)


def flat_slots(k, shift, share, first):
    return (k >> shift) * share + first + (k & ((1 << shift) - 1))


def make_send(T, D, CT, TP):
    Q = T // TP
    share = T // CT
    SR = share // TP
    shift = SR.bit_length() - 1
    assert SR == 1 << shift and Q == CT * SR

    def send(rsc, perm, x, dy, buf_o, fin_o):
        c = rsc[0]
        tp = rsc[1]
        own = perm[0:1, pl.ds(pl.multiple_of(c * T, LANES), T)].astype(F32)
        r = lax.broadcasted_iota(jnp.int32, (T, T), 0)
        q = lax.broadcasted_iota(jnp.int32, (T, T), 1)
        row = jnp.broadcast_to(own, (T, T))
        col = jnp.broadcast_to(jnp.sum(jnp.where(r == q, row, 0.0), axis=1, keepdims=True), (T, T))
        pos_col = jnp.sum(jnp.where(row < col, 1.0, 0.0), axis=1, keepdims=True)
        pos_row = jnp.sum(jnp.where(col < row, 1.0, 0.0), axis=0, keepdims=True)
        k = lax.broadcasted_iota(jnp.int32, (Q, T), 0)
        pick = jnp.where(flat_slots(k, shift, share, SR * tp).astype(F32) == pos_row, 1.0, 0.0).astype(BF)
        buf_o[:, 0:D] = dot_nn(pick, x[...]).astype(BF)
        buf_o[:, D : 2 * D] = dot_nn(pick, dy[...]).astype(BF)
        f = lax.broadcasted_iota(jnp.int32, (T, Q), 1)
        for e in range(TP):
            slot = flat_slots(f, shift, share, SR * (tp ^ e)).astype(F32)
            fin_o[:, e * Q : (e + 1) * Q] = jnp.where(slot == pos_col, 1.0, 0.0).astype(BF)

    return call(send, [((Q, 2 * D), BF), ((T, T), BF)], 4, 1)


def make_recv(T, D, CT, TP):
    Q = T // TP
    share = T // CT
    SR = share // TP
    shift = SR.bit_length() - 1

    def recv(rsc, perm, gain, *rest):
        parts = rest[:TP]
        x_o, dy_o, hb_o, rt_o = rest[TP:]
        c = rsc[0]
        tp = rsc[1]
        place = (lax.broadcasted_iota(jnp.int32, (T, T), 0) + c * T)
        lane = lax.broadcasted_iota(jnp.int32, (T, LANES), 1)
        hot = jnp.zeros((T, LANES), F32)
        for s in range(CT):
            src = jnp.broadcast_to(perm[0:1, s * T : (s + 1) * T], (T, T))
            n = jnp.sum(jnp.where(src == place, 1.0, 0.0), axis=1, keepdims=True)
            hot = jnp.where(lane == s, n, hot)
        r = lax.broadcasted_iota(jnp.int32, (T, T), 0)
        q = lax.broadcasted_iota(jnp.int32, (T, T), 1)
        below = jnp.where(q < r, 1.0, 0.0).astype(BF)
        count = dot_nn(below, hot.astype(BF))
        rank = jnp.sum(hot * count, axis=1, keepdims=True)
        block = jnp.sum(hot * lane.astype(F32), axis=1, keepdims=True)
        want = block * share + rank
        f = lax.broadcasted_iota(jnp.int32, (T, Q), 1)
        xa = jnp.zeros((T, D), F32)
        ya = jnp.zeros((T, D), F32)
        for e in range(TP):
            slot = flat_slots(f, shift, share, SR * (tp ^ e)).astype(F32)
            m = jnp.where(slot == want, 1.0, 0.0).astype(BF)
            rt_o[:, e * Q : (e + 1) * Q] = m
            xa = xa + dot_nn(m, parts[e][:, 0:D])
            ya = ya + dot_nn(m, parts[e][:, D : 2 * D])
        x_o[...] = xa.astype(BF)
        dy_o[...] = ya.astype(BF)
        inv = lax.rsqrt(jnp.mean(xa * xa, axis=1, keepdims=True) + NORM_EPS)
        hb_o[...] = (xa * inv * gain[...]).astype(BF)

    return call(recv, [((T, D), BF)] * 3 + [((T, T), BF)], 3 + TP, 1)


def make_norm_back(Q, D):
    def norm_back(keep, got, far, own, gain, o):
        both = keep[0:Q].astype(F32) + got[0:Q].astype(F32) + far[...].astype(F32)
        xf = own[:, 0:D].astype(F32)
        inv = lax.rsqrt(jnp.mean(xf * xf, axis=1, keepdims=True) + NORM_EPS)
        dn = both[:, D : 2 * D]
        scaled = gain[...] * dn
        mean = jnp.mean(scaled * xf, axis=1, keepdims=True)
        o[:, 0:D] = (xf + both[:, 0:D]).astype(BF)
        o[:, D : 2 * D] = (
            own[:, D : 2 * D].astype(F32) + inv * scaled - xf * (inv * inv * inv) * mean
        ).astype(BF)

    return call(norm_back, [((Q, 2 * D), BF)], 5, 0)


def make_final(T, D, TP):
    Q = T // TP

    def final(fin, *rest):
        out_o, grad_o = rest[TP:]
        a = jnp.zeros((T, D), F32)
        b = jnp.zeros((T, D), F32)
        for e in range(TP):
            m = fin[:, e * Q : (e + 1) * Q]
            a = a + dot_nn(m, rest[e][:, 0:D])
            b = b + dot_nn(m, rest[e][:, D : 2 * D])
        out_o[...] = a.astype(BF)
        grad_o[...] = b.astype(BF)

    return call(final, [((T, D), BF)] * 2, 1 + TP, 0)


def halves(x):
    hi = x.astype(BF)
    return hi, (x - hi.astype(F32)).astype(BF)


def mul3(ah, al, bh, bl):
    return dot_nn(ah, bh) + (dot_nn(ah, bl) + dot_nn(al, bh))


def gram3(parts):
    def rows_of(i, b, n):
        at = slice(i * b, (i + 1) * b)
        tail = slice(i * b, n)
        tot = None
        for h, l in parts:
            one = dot_tn(h[:, at], h[:, tail]) + (dot_tn(h[:, at], l[:, tail]) + dot_tn(l[:, at], h[:, tail]))
            tot = one if tot is None else tot + one
        return tot

    return rows_of


def put_gram(o, parts, n):
    b = n // 3
    rows_of = gram3(parts)
    o[0:b, :] = rows_of(0, b, n)
    o[b : 2 * b, 0 : 2 * b] = rows_of(1, b, n)
    o[b : 2 * b, 2 * b : n] = rows_of(2, b, n)


def momentum_step(gradient, momentum_old):
    momentum_new = MOMENTUM * momentum_old + gradient
    return (momentum_new, gradient + MOMENTUM * momentum_new)


def add_parts(ref, cols):
    tot = ref[0, :, cols].astype(F32)
    for k in range(1, ref.shape[0]):
        tot = tot + ref[k, :, cols].astype(F32)
    return tot


def make_gram_out(G, rows, D):
    def gram_out(got, mom, g1_o, go_o, mo_o, uo_o, gram_o):
        g1_o[...] = add_parts(got, slice(0, D))
        g = add_parts(got, slice(D, 2 * D))
        m, u = momentum_step(g, mom[...])
        go_o[...] = g
        mo_o[...] = m
        uo_o[...] = u
        put_gram(gram_o, [halves(u)], D)

    outs = [((rows, D), F32)] * 4 + [((2 * D // 3, D), F32)]
    return call(gram_out, outs, 2, 0)


def make_gram_in(G, rows, D, XW, R, VR, pack, full):
    b = D // 3
    top = 2 * b

    def gram_in(place, got, g1, mom, xm, dm, vec, go, uo, gi_o, mi_o, gx_o, mx_o, gd_o, md_o, mine_o, away_o, um_o, ua_o, tmp):
        even = (place[1] & 1) == 0
        parts = []
        us = []
        for q in range(2):
            g = add_parts(got, slice(0, D)) if q == 0 else g1[...]
            m, u = momentum_step(g, mom[:, q, :])
            gi_o[:, q, :] = g
            mi_o[:, q, :] = m
            us.append(u)
            parts.append(halves(u))
        put_gram(tmp, parts, D)
        g = add_parts(got, slice(D, D + LANES))
        m, u = momentum_step(g, jnp.concatenate([xm[...], dm[...]], axis=1))
        gx_o[...] = g[:, 0:XW]
        gd_o[...] = g[:, XW : XW + R]
        mx_o[...] = m[:, 0:XW]
        md_o[...] = m[:, XW : XW + R]
        h, l = halves(u)
        small = dot_tn(h, h) + (dot_tn(h, l) + dot_tn(l, h))

        def put_in(buf, ub):
            buf[0:top, :] = tmp[...]
            buf[top : top + VR, :] = vec[...]
            if full > top + VR:
                buf[top + VR : full, :] = jnp.zeros((full - top - VR, D), F32)
            ub[0:rows, :] = us[0]
            ub[rows : 2 * rows, :] = us[1]

        def put_out(buf, ub):
            buf[0:top, :] = go[...]
            buf[top:full, :] = jnp.zeros((full - top, D), F32)
            for k in range(-(-LANES // pack)):
                lo = k * pack
                hi = min(lo + pack, LANES)
                buf[top : top + hi - lo, k * LANES : (k + 1) * LANES] = small[lo:hi]
            ub[0:rows, :] = uo[...]
            ub[rows : 2 * rows, :] = jnp.zeros((rows, D), F32)
            ub[rows : 2 * rows, 0:LANES] = u

        @pl.when(even)
        def _():
            put_in(mine_o, um_o)
            put_out(away_o, ua_o)

        @pl.when(jnp.logical_not(even))
        def _():
            put_out(mine_o, um_o)
            put_in(away_o, ua_o)

    outs = [((rows, 2, D), F32)] * 2
    outs += [((rows, XW), F32)] * 2 + [((rows, R), F32)] * 2 + [((full, D), F32)] * 2 + [((2 * rows, D), F32)] * 2
    return call(gram_in, outs, 9, 1, [pltpu.VMEM((top, D), F32)])


class Polar:
    def __init__(self, n, nbk, cuts, refs):
        self.n, self.nbk, self.cuts = n, nbk, list(cuts)
        self.blocks = n // nbk
        self.ah, self.al, self.qh, self.ql, self.th, self.tl, self.xs, self.acc = refs

    @staticmethod
    def scratch(n, rows):
        return [pltpu.VMEM((n, n), BF)] * 6 + [pltpu.VMEM((rows, n), F32), pltpu.VMEM((n, n), F32)]

    def at(self, b):
        return slice(b * self.nbk, (b + 1) * self.nbk)

    def put(self, i, value, hi_ref, lo_ref):
        h, l = halves(value)
        b = self.nbk
        hi_ref[self.at(i), i * b : self.n] = h
        lo_ref[self.at(i), i * b : self.n] = l
        for j in range(i + 1, self.blocks):
            h, l = halves(value[:, (j - i) * b : (j - i + 1) * b].T)
            hi_ref[self.at(j), self.at(i)] = h
            lo_ref[self.at(j), self.at(i)] = l

    def start(self, tails, upd):
        n, b = self.n, self.nbk
        col = lax.broadcasted_iota(jnp.int32, (1, n), 1)
        edges = [0] + self.cuts
        inv = jnp.zeros((1, n), F32)
        r = lax.broadcasted_iota(jnp.int32, (b, b), 0)
        c = lax.broadcasted_iota(jnp.int32, (b, b), 1)
        for lo, hi in zip(edges[:-1], edges[1:]):
            tot = jnp.zeros((1, 1), F32)
            for k in range(self.blocks):
                inside = (r == c) & (r + k * b >= lo) & (r + k * b < hi)
                d = jnp.sum(jnp.where(inside, tails[k][:, 0:b], 0.0), axis=1, keepdims=True)
                tot = tot + jnp.sum(d, axis=0, keepdims=True)
            inv = jnp.where((col >= lo) & (col < hi), 1.0 / (jnp.sqrt(tot) + 1e-07), inv)
        self.xs[...] = upd * inv
        for i in range(self.blocks):
            g = tails[i]
            if len(self.cuts) > 1:
                r = lax.broadcasted_iota(jnp.int32, g.shape, 0) + i * b
                c = lax.broadcasted_iota(jnp.int32, g.shape, 1) + i * b
                same = jnp.zeros(g.shape, F32)
                for lo, hi in zip(edges[:-1], edges[1:]):
                    same = jnp.where((r >= lo) & (r < hi) & (c >= lo) & (c < hi), 1.0, same)
                g = g * same
            one = inv[:, i * b : n]
            a = g * (one * one)
            self.acc[self.at(i), i * b : n] = a
            self.put(i, a, self.ah, self.al)

    def apply(self):
        for i in range(self.blocks):
            tail = slice(i * self.nbk, self.n)
            a2 = mul3(self.ah[self.at(i), :], self.al[self.at(i), :], self.ah[:, tail], self.al[:, tail])
            r = lax.broadcasted_iota(jnp.int32, a2.shape, 0)
            c = lax.broadcasted_iota(jnp.int32, a2.shape, 1)
            q = jnp.where(r == c, NS_A, 0.0) + (NS_B * self.acc[self.at(i), tail] + NS_C * a2)
            self.put(i, q, self.qh, self.ql)
        h, l = halves(self.xs[...])
        self.xs[...] = mul3(h, l, self.qh[...], self.ql[...])

    def advance(self):
        for src, dst in (((self.ah, self.al), (self.th, self.tl)), ((self.th, self.tl), (self.ah, self.al))):
            for i in range(self.blocks):
                tail = slice(i * self.nbk, self.n)
                a = mul3(src[0][self.at(i), :], src[1][self.at(i), :], self.qh[:, tail], self.ql[:, tail])
                if dst[0] is self.ah:
                    self.acc[self.at(i), tail] = a
                self.put(i, a, *dst)


def unpack_gram(buf, n):
    b = n // 3
    return [buf[0:b, :], buf[b : 2 * b, 0 : 2 * b], buf[b : 2 * b, 2 * b : n]]


def make_muon(D, rows, XW, R, pack, full):
    top = 2 * (D // 3)

    def muon(buf, um, ua, xm_o, xa_o, *refs):
        p = Polar(D, D // 3, (D,), refs[:8])
        s = Polar(LANES, LANES, (XW, XW + R), refs[8:16])
        small = jnp.concatenate(
            [
                buf[top : top + min(pack, LANES - k * pack), k * LANES : (k + 1) * LANES]
                for k in range(-(-LANES // pack))
            ],
            axis=0,
        )
        p.start(unpack_gram(buf, D), jnp.concatenate([um[...], ua[...]], axis=0))
        s.start([small], jnp.concatenate([um[rows:, 0:LANES], ua[rows:, 0:LANES]], axis=0))

        def step(k, c):
            p.apply()
            s.apply()
            p.advance()
            s.advance()
            return c

        lax.fori_loop(0, 4, step, 0)
        p.apply()
        s.apply()
        xm_o[...] = p.xs[0 : 2 * rows, :]
        xa_o[0:rows, :] = p.xs[2 * rows : 3 * rows, :]
        xa_o[rows : 2 * rows, :] = p.xs[3 * rows : 4 * rows, :]
        return s

    def body(place, buf, um, ua, xm_o, xa_o, *refs):
        s = muon(buf, um, ua, xm_o, xa_o, *refs)

        @pl.when((place[1] & 1) == 1)
        def _():
            xm_o[rows : 2 * rows, 0:LANES] = s.xs[0:rows, :]
            xa_o[rows : 2 * rows, 0:LANES] = s.xs[rows : 2 * rows, :]

    body.__name__ = "muon"
    scratch = Polar.scratch(D, 4 * rows) + Polar.scratch(LANES, 2 * rows)
    return call(body, [((2 * rows, D), F32)] * 2, 4, 1, scratch)


def make_finish(rows, D, XW, R, rates):
    def finish(place, xm, xr, wi, wx, wd, wo, oi, ox, od, oo):
        even = (place[1] & 1) == 0
        for q in range(2):
            at = slice(q * rows, (q + 1) * rows)
            oi[:, q, :] = wi[:, q, :] - rates[0] * jnp.where(even, xm[at], xr[at])
        oo[...] = wo[...] - rates[3] * jnp.where(even, xr[0:rows], xm[0:rows])
        s = jnp.where(even, xr[rows:, 0:LANES], xm[rows:, 0:LANES])
        ox[...] = wx[...] - rates[1] * s[:, 0:XW]
        od[...] = wd[...] - rates[2] * s[:, XW : XW + R]

    outs = [((rows, 2, D), F32), ((rows, XW), F32), ((rows, R), F32), ((rows, D), F32)]
    return call(finish, outs, 7, 1)


def make_pack(rows, D, XW, R):
    def pack(wi, wx, wd, wo, a_o, r_o):
        a_o[...] = wi[:, 0, :].astype(BF)
        r_o[:, 0:D] = wi[:, 1, :].astype(BF)
        r_o[:, D : D + LANES] = jnp.concatenate([wx[...], wd[...]], axis=1).astype(BF)
        r_o[:, D + LANES : 2 * D + LANES] = wo[...].astype(BF)

    return call(pack, [((rows, D), BF), ((rows, 2 * D + LANES), BF)], 4, 0)


def shifted(value, axis, by):
    devices = lax.axis_size(axis)
    pairs = [(i, i + by) for i in range(devices) if 0 <= i + by < devices]
    return lax.ppermute(value, axis, pairs)


def swap(value, axis, bit):
    devices = lax.axis_size(axis)
    return lax.ppermute(value, axis, [(i, i ^ bit) for i in range(devices)])


def side(axis, bit):
    return jnp.where((lax.axis_index(axis) & bit) != 0, 1, 0)


def in_order(mine, theirs, axis, bit):
    low = side(axis, bit) == 0
    return jnp.concatenate([jnp.where(low, mine, theirs), jnp.where(low, theirs, mine)], axis=0)


def half_sum(value, axis, bit):
    half = value.shape[0] // 2
    mine = side(axis, bit) * half
    away = lax.dynamic_slice_in_dim(value, half - mine, half)
    kept = lax.dynamic_slice_in_dim(value, mine, half)
    return kept + swap(away, axis, bit)


def half_join(value, axis, bit):
    return in_order(value, swap(value, axis, bit), axis, bit)


def bits_of(axis):
    count = lax.axis_size(axis)
    return [1 << k for k in range(count.bit_length() - 1)]


def sum_rest(value):
    cols = value.shape[1] // 2
    done = []
    for k in range(2):
        part = value[:, k * cols : (k + 1) * cols]
        cut = [("tp", 2), ("fsdp", 1), ("ctx", 1)] if k == 0 else [("fsdp", 1), ("tp", 2), ("ctx", 1)]
        rest = [(a, b) for a in ("tp", "fsdp", "ctx") for b in bits_of(a) if (a, b) not in cut + [("tp", 1)]]
        for axis, bit in cut:
            part = half_sum(part, axis, bit)
        for axis, bit in rest:
            part = part + swap(part, axis, bit)
        for axis, bit in cut[::-1]:
            part = half_join(part, axis, bit)
        done.append(part)
    return jnp.concatenate(done, axis=1)


def gather_fsdp(value):
    if lax.axis_size("fsdp") == 2:
        return in_order(value, swap(value, "fsdp", 1), "fsdp", 1)
    return lax.all_gather(value, "fsdp", axis=0, tiled=True)


def adam_update(parameters, gradient, moment_one, moment_two, adam_step):
    count = adam_step[0].astype(jnp.float32)
    first_new = BETA_ONE * moment_one + (1.0 - BETA_ONE) * gradient
    second_new = BETA_TWO * moment_two + (1.0 - BETA_TWO) * gradient * gradient
    first_hat = first_new / (1.0 - jnp.power(jnp.float32(BETA_ONE), count))
    second_hat = second_new / (1.0 - jnp.power(jnp.float32(BETA_TWO), count))
    updated = parameters - ADAM_RATE * (
        first_hat / (jnp.sqrt(second_hat) + ADAM_EPS) + DECAY_RATE * parameters
    )
    return (updated, first_new, second_new)


def on_device(
    block_input,
    cotangent,
    route_perm,
    doc_lengths,
    norm_gain,
    in_proj,
    conv_weight,
    conv_bias,
    x_proj,
    dt_proj,
    dt_bias,
    a_log,
    skip_gain,
    out_proj,
    in_momentum,
    x_momentum,
    dt_momentum,
    out_momentum,
    adam_first,
    adam_second,
    adam_step,
):
    ctx_count = lax.axis_size("ctx")
    fsdp_count = lax.axis_size("fsdp")
    tp_count = lax.axis_size("tp")
    owners = fsdp_count * ctx_count
    ctx_index = lax.axis_index("ctx")
    tp_index = lax.axis_index("tp")
    tokens, width = block_input.shape
    stream = tokens * ctx_count
    quarter = tokens // tp_count
    own_rows = in_proj.shape[0]
    channels = own_rows * owners
    inner = conv_bias.shape[0]
    states = a_log.shape[0]
    rank = dt_proj.shape[1]
    xw = x_proj.shape[1]
    lengths = doc_lengths[0]
    docs = lengths.shape[0]
    offsets = jnp.cumsum(lengths) - lengths
    scal = jnp.concatenate([(tp_index * channels)[None], offsets - ctx_index * tokens, ctx_index[None]]).astype(
        jnp.int32
    )
    place = jnp.stack([ctx_index, tp_index]).astype(jnp.int32)
    perm_row = (route_perm % stream).reshape(1, stream)
    gain_row = norm_gain.reshape(1, width)

    w_a, w_r = make_pack(own_rows, width, xw, rank)(in_proj, x_proj, dt_proj, out_proj)
    send, fin = make_send(tokens, width, ctx_count, tp_count)(place, perm_row, block_input, cotangent)
    sent = lax.all_to_all(
        send.reshape(ctx_count, quarter // ctx_count, 2 * width), "ctx", split_axis=0, concat_axis=0, tiled=True
    )
    w_rest = gather_fsdp(lax.all_gather(w_r, "ctx", axis=0, tiled=True))
    w_in = gather_fsdp(lax.all_gather(w_a, "ctx", axis=0, tiled=True))
    own = sent.reshape(quarter, 2 * width)
    far = swap(own, "tp", 2)
    stream_x, stream_dy, normed, route = make_recv(tokens, width, ctx_count, tp_count)(
        place, perm_row, gain_row, own, swap(own, "tp", 1), far, swap(far, "tp", 1)
    )

    halo = shifted(normed[tokens - 8 :], "ctx", 1)
    conv_in, gate_in, conv_act, conv_out, pt_part, d_gated, w_turn, x_halo = make_front(
        tokens, channels, width, docs, xw, rank
    )(scal, normed, halo, stream_dy, w_in, w_rest, conv_weight, conv_bias.reshape(1, inner))
    pt_pair = pt_part + swap(pt_part, "tp", 1)
    pt, dec, drv, d_inner, pre, ends = make_carry(
        tokens, channels, docs, xw, rank, states, ctx_count
    )(scal, pt_pair, swap(pt_pair, "tp", 2), conv_act, gate_in, d_gated, w_turn, dt_bias.reshape(1, inner), a_log)
    ends = lax.all_to_all(ends, "ctx", split_axis=0, concat_axis=0, tiled=True)
    gate_low, d_gate, du_one, d_pre_low, dp_part, mix_part, grads_one, part_dt, vec_part = make_scan(
        tokens, channels, width, docs, xw, rank, states, ctx_count
    )(
        scal, pt, dec, drv, d_inner, pre, conv_act, gate_in, d_gated, stream_dy, normed, w_rest, w_turn, a_log,
        skip_gain.reshape(1, inner), ends,
    )

    def to_owners(grads):
        return lax.all_to_all(
            grads.reshape(owners, own_rows, grads.shape[1]), ("fsdp", "ctx"), split_axis=0, concat_axis=0, tiled=True
        )

    got_one = to_owners(grads_one)
    dp_pair = dp_part + swap(dp_part, "tp", 1)
    d_conv_in, spill, grads_two, vec_chan = make_back(tokens, channels, width, docs, xw, rank)(8 + states)(
        scal, dp_pair, swap(dp_pair, "tp", 2), du_one, conv_out, conv_act, conv_in, x_halo, w_turn, conv_weight,
        vec_part, part_dt, normed, halo,
    )
    got_two = to_owners(grads_two)
    keep, away, g_gain = make_last(tokens, channels, width, quarter)(
        d_conv_in, shifted(spill, "ctx", -1), d_gate, w_in, w_rest, mix_part, stream_x, route
    )

    near = swap(away, "tp", 1)
    cross = (keep[quarter:].astype(F32) + near[quarter:].astype(F32)).astype(BF)
    back = make_norm_back(quarter, width)(keep, near, swap(cross, "tp", 2), own, gain_row)[0]
    home = lax.all_to_all(
        back.reshape(ctx_count, quarter // ctx_count, 2 * width), "ctx", split_axis=0, concat_axis=0, tiled=True
    ).reshape(quarter, 2 * width)
    home_far = swap(home, "tp", 2)
    block_out, input_grad = make_final(tokens, width, tp_count)(
        fin, home, swap(home, "tp", 1), home_far, swap(home_far, "tp", 1)
    )

    kinds = 8 + states
    pack = 24
    vec_wide = lax.dynamic_update_slice(jnp.zeros((kinds, inner), F32), vec_chan, (0, tp_index * channels))
    vec_wide = vec_wide + jnp.pad(g_gain, ((7, kinds - 8), (0, inner - width)))
    vec_rows = kinds * inner // width
    g_one, g_out, mom_out, upd_out, gram_out = make_gram_out(owners, own_rows, width)(got_one, out_momentum)
    top = 2 * (width // 3)
    full = -(-(top + max(vec_rows, pack)) // 64) * 64
    g_in, mom_in, g_x, mom_x, g_dt, mom_dt, gram_mine, gram_away, upd_mine, upd_away = make_gram_in(
        owners, own_rows, width, xw, rank, vec_rows, pack, full
    )(place, got_two, g_one, in_momentum, x_momentum, dt_momentum, vec_wide.reshape(vec_rows, width), gram_out, upd_out)
    gram = sum_rest(gram_mine + swap(gram_away, "tp", 1))
    x_mine, x_away = make_muon(width, own_rows, xw, rank, pack, full)(place, gram, upd_mine, swap(upd_away, "tp", 1))
    rates = [MUON_RATE * 0.2 * math.sqrt(max(a, b)) for a, b in ((2 * inner, width), (inner, xw), (inner, rank), (inner, width))]
    new_in, new_x, new_dt, new_out = make_finish(own_rows, width, xw, rank, rates)(
        place, x_mine, swap(x_away, "tp", 1), in_proj, x_proj, dt_proj, out_proj
    )
    vec_own = gram[top : top + vec_rows]
    vec_sum = jnp.where((tp_index & 1) == 0, vec_own, swap(vec_own, "tp", 1)).reshape(kinds, inner)
    g_alog = vec_sum[8:]
    vec_grads = jnp.concatenate(
        [vec_sum[7, :width], vec_sum[0:4].reshape(-1), vec_sum[4], vec_sum[5], g_alog.reshape(-1), vec_sum[6]]
    )
    vec_params = jnp.concatenate(
        [norm_gain, conv_weight.reshape(-1), conv_bias, dt_bias, a_log.reshape(-1), skip_gain]
    )
    new_vec, first_new, second_new = adam_update(vec_params, vec_grads, adam_first, adam_second, adam_step)
    cut_b = width + 4 * inner
    cut_c = cut_b + inner
    cut_d = cut_c + inner
    cut_e = cut_d + states * inner
    return (
        block_out,
        input_grad,
        vec_sum[7, :width],
        g_in,
        vec_sum[0:4],
        vec_sum[4],
        g_x,
        g_dt,
        vec_sum[5],
        g_alog,
        vec_sum[6],
        g_out,
        new_vec[:width],
        new_in,
        new_vec[width:cut_b].reshape(4, inner),
        new_vec[cut_b:cut_c],
        new_x,
        new_dt,
        new_vec[cut_c:cut_d],
        new_vec[cut_d:cut_e].reshape(states, inner),
        new_vec[cut_e:],
        new_out,
        mom_in,
        mom_x,
        mom_dt,
        mom_out,
        first_new,
        second_new,
    )


def solution(mesh):
    return jax.shard_map(
        on_device,
        mesh=mesh,
        in_specs=(
            P(("fsdp", "ctx"), None),
            P(("fsdp", "ctx"), None),
            P("fsdp"),
            P("fsdp", None),
            P(),
            P(("tp", "fsdp", "ctx"), None, None),
            P(),
            P(),
            P(("tp", "fsdp", "ctx"), None),
            P(("tp", "fsdp", "ctx"), None),
            P(),
            P(),
            P(),
            P(("tp", "fsdp", "ctx"), None),
            P(("tp", "fsdp", "ctx"), None, None),
            P(("tp", "fsdp", "ctx"), None),
            P(("tp", "fsdp", "ctx"), None),
            P(("tp", "fsdp", "ctx"), None),
            P(),
            P(),
            P(),
        ),
        out_specs=(
            P(("fsdp", "ctx"), None),
            P(("fsdp", "ctx"), None),
            P(),
            P(("tp", "fsdp", "ctx"), None, None),
            P(),
            P(),
            P(("tp", "fsdp", "ctx"), None),
            P(("tp", "fsdp", "ctx"), None),
            P(),
            P(),
            P(),
            P(("tp", "fsdp", "ctx"), None),
            P(),
            P(("tp", "fsdp", "ctx"), None, None),
            P(),
            P(),
            P(("tp", "fsdp", "ctx"), None),
            P(("tp", "fsdp", "ctx"), None),
            P(),
            P(),
            P(),
            P(("tp", "fsdp", "ctx"), None),
            P(("tp", "fsdp", "ctx"), None, None),
            P(("tp", "fsdp", "ctx"), None),
            P(("tp", "fsdp", "ctx"), None),
            P(("tp", "fsdp", "ctx"), None),
            P(),
            P(),
        ),
        check_vma=False,
    )
```

```python
import math

import jax
import jax.numpy as jnp
from jax import lax
from jax.experimental import pallas as pl
from jax.experimental.pallas import tpu as pltpu
from jax.sharding import PartitionSpec as P

F32 = jnp.float32
BF = jnp.bfloat16
LANES = 128
RESET = 1e5
LOG2E = 1.4426950408889634
VMEM_LIMIT = 60 * 1024 * 1024
NS_A = 3.4445
NS_B = -4.775
NS_C = 2.0315
MOMENTUM = 0.95
MUON_RATE = 0.1
ADAM_RATE = 0.25
BETA_ONE = 0.9
BETA_TWO = 0.95
ADAM_EPS = 1e-08
DECAY_RATE = 0.01
NORM_EPS = 1e-05


def dot_nn(a, b):
    return lax.dot_general(a, b, (((1,), (0,)), ((), ())), preferred_element_type=F32)


def dot_nt(a, b):
    return lax.dot_general(a, b, (((1,), (1,)), ((), ())), preferred_element_type=F32)


def dot_tn(a, b):
    return lax.dot_general(a, b, (((0,), (0,)), ((), ())), preferred_element_type=F32)


def soft(x):
    return jnp.maximum(x, 0.0) + jnp.log1p(jnp.exp(-jnp.abs(x)))


def slope_of(a, s):
    return s * (1.0 + a * (1.0 - s))


def call(body, outs, n_in, n_smem, scratch=(), flops=10**9):
    specs = [pl.BlockSpec(memory_space=pltpu.SMEM)] * n_smem + [
        pl.BlockSpec(memory_space=pltpu.VMEM)
    ] * (n_in - n_smem)
    return pl.pallas_call(
        body,
        out_shape=[jax.ShapeDtypeStruct(s, d) for s, d in outs],
        in_specs=specs,
        out_specs=[pl.BlockSpec(memory_space=pltpu.VMEM)] * len(outs),
        scratch_shapes=list(scratch),
        compiler_params=pltpu.CompilerParams(vmem_limit_bytes=VMEM_LIMIT),
        name=body.__name__,
    )


def rows_iota(r0, rows):
    return lax.broadcasted_iota(jnp.int32, (rows, LANES), 0) + r0


def tap_mask(sc_ref, docs, p, shift):
    ok = jnp.ones(p.shape, F32)
    for j in range(docs):
        off = sc_ref[1 + j]
        ok = jnp.where((off <= p) & (p < off + shift), 0.0, ok)
    return ok


def wide(mask, width):
    return jnp.concatenate([mask] * (width // LANES), axis=1)


def make_front(T, C, D, docs, XW, R, CT, FS, swapped):
    RB = 64

    def front(sc, hb, halo, dy, a0, a1, r0, r1, cw, cb, wa, wr, xu_o, z_o, u_o, v_o, pt_o, dg_o, wt_o, xh_o, xpad):
        own = C // (CT * FS)
        if swapped:
            z, f = sc[1 + docs], sc[2 + docs]
            for pieces, out in (((a0, a1), wa), ((r0, r1), wr)):
                for e in range(CT * FS):
                    fe, ze = (e % FS, e // FS) if out is wa else (e // CT, e % CT)
                    at = pl.multiple_of(((f ^ fe) * CT + (z ^ ze)) * own, own)
                    k = e * own
                    half = C // 2
                    piece = pieces[k // half]
                    out[pl.ds(at, own), :] = piece[k % half : k % half + own, :]
        else:
            wa[0 : C // 2, :] = a0[...]
            wa[C // 2 : C, :] = a1[...]
            wr[0 : C // 2, :] = r0[...]
            wr[C // 2 : C, :] = r1[...]
        w0 = wa[...]
        w1 = wr[:, 0:D]
        wo = wr[:, D + LANES : 2 * D + LANES]
        wt = wr[:, D : D + LANES].astype(F32).T.astype(BF)
        wt_o[...] = wt
        c0 = pl.multiple_of(sc[0], LANES)
        xh = dot_nt(halo[...], w0).astype(BF).astype(F32)
        xpad[0:8, :] = xh
        xh_o[...] = xh
        xu = dot_nt(hb[...], w0).astype(BF)
        xu_o[...] = xu
        xpad[8 : 8 + T, :] = xu.astype(F32)
        z_o[...] = dot_nt(hb[...], w1).astype(BF)
        dg_o[...] = dot_nt(dy[...], wo)
        taps = [cw[k : k + 1, pl.ds(c0, C)] for k in range(4)]
        bias = cb[0:1, pl.ds(c0, C)]

        def block(i, carry):
            r0 = i * RB
            p = rows_iota(r0, RB)
            v = bias + jnp.zeros((RB, C), F32)
            full = xpad[pl.ds(r0, RB + 8), :]
            for k in range(4):
                s = 3 - k
                x = full[8 - s : 8 - s + RB]
                if s:
                    x = x * wide(tap_mask(sc, docs, p, s), C)
                v = v + taps[k] * x
            v_o[pl.ds(r0, RB), :] = v
            u_o[pl.ds(r0, RB), :] = (v / (1.0 + jnp.exp(-v))).astype(BF)
            return carry

        lax.fori_loop(0, T // RB, block, 0)
        pt_o[...] = dot_nt(wt[0:XW], u_o[...])

    outs = [((C, D), BF), ((C, 2 * D + LANES), BF)]
    outs += [((T, C), BF)] * 3 + [((T, C), F32), ((XW, T), F32), ((T, C), F32), ((LANES, C), BF), ((8, C), F32)]
    return call(front, outs, 10, 1, [pltpu.VMEM((T + 8, C), F32)])


def lane_sums(ref):
    def join(a, b, w):
        m = (lax.broadcasted_iota(jnp.int32, a.shape, 2) & w) == 0
        if w == LANES // 2:
            return jnp.where(m, a, b) + pltpu.roll(jnp.where(m, b, a), w, 2)
        return jnp.where(m, a, b) + jnp.where(m, pltpu.roll(a, LANES - w, 2), pltpu.roll(b, w, 2))

    w = LANES // 2
    while w >= 8:

        def chunk(i, c, w=w):
            ref[pl.ds(i * 8, 8)] = join(ref[pl.ds(i * 8, 8)], ref[pl.ds(i * 8 + w, 8)], w)
            return c

        lax.fori_loop(0, w // 8, chunk, 0)
        w //= 2
    x = ref[0:8]
    while w:
        x = join(x[0:w], x[w : 2 * w], w)
        w //= 2
    return x[0]


def make_carry(T, C, docs, XW, R, N, CT):
    RB = 64
    LT = C // LANES

    def carry(sc, pa, pb, u, z, dg, wt, dtb, alog, pt_o, da_o, du_o, dyin_o, pre_o, ends_o):
        c0 = pl.multiple_of(sc[0], LANES)
        pt = pa[...] + pb[...]
        pt_o[...] = pt
        lin = dot_tn(pt[0:R].astype(BF), wt[XW : XW + R, :])
        pre_o[...] = lin + dtb[0:1, pl.ds(c0, C)]

        def block(i, tot):
            rs = pl.ds(i * RB, RB)
            p = rows_iota(i * RB, RB)
            keep = jnp.ones((RB, LANES), F32)
            for j in range(docs):
                keep = jnp.where(p == sc[1 + j], 0.0, keep)
            x = pre_o[rs, :]
            delta = soft(x)
            d = jnp.where(wide(keep, C) > 0.0, delta, RESET)
            r8 = pl.ds(i * (RB // 8), RB // 8)
            da_o[r8] = d.reshape(RB // 8, 8, C)
            du_o[r8] = (delta * u[rs, :].astype(F32)).reshape(RB // 8, 8, C)
            zf = z[rs, :].astype(F32)
            dyin_o[r8] = (dg[rs, :] * (zf / (1.0 + jnp.exp(-zf)))).reshape(RB // 8, 8, C)
            return tot + jnp.sum(d, axis=0, keepdims=True)

        tot = lax.fori_loop(0, T // RB, block, jnp.zeros((1, C), F32))
        am = [-jnp.exp(alog[:, pl.ds(c0 + l * LANES, LANES)]) for l in range(LT)]
        am2 = [a * LOG2E for a in am]

        def rows(ref, i, j):
            full = ref[i, pl.ds(j, N, stride=0), :]
            return [full[:, l * LANES : (l + 1) * LANES] for l in range(LT)]

        nb = T // LANES

        def outer(k, c):
            bt = pt_o[R_ : R_ + N, pl.ds(pl.multiple_of(k * LANES, LANES), LANES)]
            ct = pt_o[R_ + N : R_ + 2 * N, pl.ds(pl.multiple_of((nb - 1 - k) * LANES, LANES), LANES)]

            def inner(i, c):
                h, g, bt, ct = c
                h = list(h)
                g = list(g)
                fi = k * (LANES // 8) + i
                ri = T // 8 - 1 - fi
                for j in range(8):
                    bb = jnp.broadcast_to(bt[:, j : j + 1], (N, LANES))
                    cc = jnp.broadcast_to(ct[:, LANES - 1 - j : LANES - j], (N, LANES))
                    df, uf = rows(da_o, fi, j), rows(du_o, fi, j)
                    db, yb = rows(da_o, ri, 7 - j), rows(dyin_o, ri, 7 - j)
                    for l in range(LT):
                        h[l] = jnp.exp2(df[l] * am2[l]) * h[l] + uf[l] * bb
                        g[l] = jnp.exp2(db[l] * am2[l]) * (g[l] + yb[l] * cc)
                return tuple(h), tuple(g), pltpu.roll(bt, LANES - 8, 1), pltpu.roll(ct, 8, 1)

            h, g, _, _ = lax.fori_loop(0, LANES // 8, inner, (c[0], c[1], bt, ct))
            return h, g

        R_ = R
        zero = tuple(jnp.zeros((N, LANES), F32) for _ in range(LT))
        h, g = lax.fori_loop(0, nb, outer, (zero, zero))
        here = sc[1 + docs]
        for d in range(CT):
            for l in range(LT):
                ends_o[d, 0:N, l * LANES : (l + 1) * LANES] = jnp.where((here ^ d) > here, h[l], g[l])
            ends_o[d, N : N + 8, :] = jnp.broadcast_to(tot, (8, C))

    outs = [((XW, T), F32)] + [((T // 8, 8, C), F32)] * 3 + [((T, C), F32)] + [((CT, N + 8, C), F32)]
    return call(carry, outs, 9, 1)


def make_scan(T, C, D, docs, XW, R, N, CT):
    RB = 64
    LT = C // LANES
    nb = T // LANES

    def scan(sc, pt, da, du, dyin, pre, u, z, dg, dy, hb, wr, wt, alog, skip, *rest):
        ends = rest[: CT - 1]
        (
            g_o, dz_o, du1_o, dpre_o, dp_o, mix_o, pw_o, pdt_o, vec_o,
            a_s, h_s, y_s, lb_s, dd_s, sb_s, sc_s,
        ) = rest[CT - 1 :]
        c0 = pl.multiple_of(sc[0], LANES)
        am = [-jnp.exp(alog[:, pl.ds(c0 + l * LANES, LANES)]) for l in range(LT)]
        am2 = [a * LOG2E for a in am]
        sl = [slice(l * LANES, (l + 1) * LANES) for l in range(LT)]
        top4 = lax.broadcasted_iota(jnp.int32, (8, LANES), 0) < 4

        def rows(ref, i, j):
            full = ref[i, pl.ds(j, N, stride=0), :]
            return [full[:, sl[l]] for l in range(LT)]

        here = sc[1 + docs]
        hin, gin = [], []
        for l in range(LT):
            for way, got in ((-1, hin), (1, gin)):
                near = jnp.zeros((N, LANES), F32)
                tot = jnp.zeros((1, LANES), F32)
                far = near
                for d in range(1, CT):
                    e = ends[d - 1]
                    near = jnp.where((here ^ d) == here + way, e[0:N, sl[l]], near)
                    tot = jnp.where((here ^ d) == here + way, e[N : N + 1, sl[l]], tot)
                    far = jnp.where((here ^ d) == here + 2 * way, e[0:N, sl[l]], far)
                got.append(near + jnp.exp2(jnp.broadcast_to(tot, (N, LANES)) * am2[l]) * far)
            h_s[0, :, sl[l]] = hin[l]

        def fouter(k, h):
            blk = pl.ds(pl.multiple_of(k * LANES, LANES), LANES)
            bt = pt[R : R + N, blk]
            ct = pt[R + N : R + 2 * N, blk]

            def inner(i, c):
                h, bt, ct = c
                h = list(h)
                fi = k * (LANES // 8) + i
                for j in range(8):
                    t = fi * 8 + j
                    bb = jnp.broadcast_to(bt[:, j : j + 1], (N, LANES))
                    cc = jnp.broadcast_to(ct[:, j : j + 1], (N, LANES))
                    dr, ur = rows(da, fi, j), rows(du, fi, j)
                    for l in range(LT):
                        a = jnp.exp2(dr[l] * am2[l])
                        a_s[t, :, sl[l]] = a
                        h[l] = a * h[l] + ur[l] * bb
                        h_s[t + 1, :, sl[l]] = h[l]
                        y_s[fi, j : j + 1, sl[l]] = jnp.sum(h[l] * cc, axis=0, keepdims=True)
                return tuple(h), pltpu.roll(bt, LANES - 8, 1), pltpu.roll(ct, LANES - 8, 1)

            return lax.fori_loop(0, LANES // 8, inner, (h, bt, ct))[0]

        lax.fori_loop(0, nb, fouter, tuple(hin))

        def bouter(k, c):
            kb = nb - 1 - k
            blk = pl.ds(pl.multiple_of(kb * LANES, LANES), LANES)
            bt = pt[R : R + N, blk]
            ct = pt[R + N : R + 2 * N, blk]
            zero = jnp.zeros((N, LANES), F32)

            def inner(i, c):
                g, ga, bt, ct = c
                g = list(g)
                ga = list(ga)
                l0 = LANES - 1 - i * 8
                fi = kb * (LANES // 8) + LANES // 8 - 1 - i
                for j in range(8):
                    t = kb * LANES + l0 - j
                    jj = 7 - j
                    bb = jnp.broadcast_to(bt[:, LANES - 1 - j : LANES - j], (N, LANES))
                    cc = jnp.broadcast_to(ct[:, LANES - 1 - j : LANES - j], (N, LANES))
                    sb = zero
                    scc = zero
                    dr, ur, yr = rows(da, fi, jj), rows(du, fi, jj), rows(dyin, fi, jj)
                    for l in range(LT):
                        dyr = yr[l]
                        lam = cc * dyr + g[l]
                        g[l] = a_s[t, :, sl[l]] * lam
                        dal = g[l] * h_s[t, :, sl[l]]
                        pb = lam * bb
                        pd = dal * am[l]
                        pb = pb[0:8] + pb[8:16]
                        pd = pd[0:8] + pd[8:16]
                        both = jnp.where(top4, pb, pd) + pltpu.roll(jnp.where(top4, pd, pb), 4, 0)
                        both = both + pltpu.roll(both, 6, 0)
                        both = both + pltpu.roll(both, 7, 0)
                        lb_s[fi, jj : jj + 1, sl[l]] = both[0:1]
                        dd_s[fi, jj : jj + 1, sl[l]] = both[4:5]
                        ga[l] = ga[l] + dal * dr[l]
                        sb = sb + lam * ur[l]
                        scc = scc + dyr * h_s[t + 1, :, sl[l]]
                    sb_s[l0 - j] = sb
                    sc_s[l0 - j] = scc
                return tuple(g), tuple(ga), pltpu.roll(bt, 8, 1), pltpu.roll(ct, 8, 1)

            g, ga, _, _ = lax.fori_loop(0, LANES // 8, inner, (c[0], c[1], bt, ct))
            dp_o[R : R + N, blk] = lane_sums(sb_s)
            dp_o[R + N : R + 2 * N, blk] = lane_sums(sc_s)
            return g, ga

        zeros = tuple(jnp.zeros((N, LANES), F32) for _ in range(LT))
        _, ga = lax.fori_loop(0, nb, bouter, (tuple(gin), zeros))
        for l in range(LT):
            vec_o[8 : 8 + N, sl[l]] = am[l] * ga[l]
        skr = skip[0:1, pl.ds(c0, C)]

        def block(i, tot):
            gdt, gsk = tot
            rs = pl.ds(i * RB, RB)
            r8 = pl.ds(i * (RB // 8), RB // 8)
            uf = u[rs, :].astype(F32)
            zf = z[rs, :].astype(F32)
            s = 1.0 / (1.0 + jnp.exp(-zf))
            yin = y_s[r8].reshape(RB, C) + skr * uf
            g_o[rs, :] = (yin * (zf * s)).astype(BF)
            dz_o[rs, :] = (dg[rs, :] * yin * slope_of(zf, s)).astype(BF)
            lb = lb_s[r8].reshape(RB, C)
            dyr = dyin[r8].reshape(RB, C)
            x = pre[rs, :]
            dpre = (lb * uf + dd_s[r8].reshape(RB, C)) / (1.0 + jnp.exp(-x))
            dpre_o[rs, :] = dpre.astype(BF)
            du1_o[rs, :] = dyr * skr + lb * soft(x)
            return gdt + jnp.sum(dpre, axis=0, keepdims=True), gsk + jnp.sum(dyr * uf, axis=0, keepdims=True)

        z1 = jnp.zeros((1, C), F32)
        gdt, gsk = lax.fori_loop(0, T // RB, block, (z1, z1))
        vec_o[5:6, :] = gdt
        vec_o[6:7, :] = gsk
        vec_o[7:8, :] = z1
        vec_o[0:5, :] = jnp.zeros((5, C), F32)
        dp_o[0:R, :] = dot_nt(wt[XW : XW + R, :], dpre_o[...])
        pdt_o[...] = dot_nn(pt[0:R, :].astype(BF), dpre_o[...])
        mix_o[...] = dot_nn(g_o[...], wr[:, D + LANES : 2 * D + LANES]).astype(BF)
        pw_o[:, 0:D] = dot_tn(dz_o[...], hb[...]).astype(BF)
        pw_o[:, D : 2 * D] = dot_tn(g_o[...], dy[...]).astype(BF)

    outs = [((T, C), BF), ((T, C), BF), ((T, C), F32), ((T, C), BF), ((XW, T), F32), ((T, D), BF),
            ((C, 2 * D), BF), ((R, C), F32), ((8 + N, C), F32)]
    scratch = [pltpu.VMEM((T, N, C), F32), pltpu.VMEM((T + 1, N, C), F32)] + [pltpu.VMEM((T // 8, 8, C), F32)] * 3
    scratch += [pltpu.VMEM((LANES, N, LANES), F32)] * 2
    return call(scan, outs, 14 + CT, 1, scratch)


def make_back(T, C, D, docs, XW, R):
    RB = 64

    def back(sc, da_, db_, du1, v, u, xu, xhalo, wt, cw, vec, pdt, hb, halo, dxu_o, spill_o, pxt_o, vec_o, pad1, pad2, pad3, xpad):
        c0 = pl.multiple_of(sc[0], LANES)
        dpl = (da_[...] + db_[...]).astype(BF)
        pxt_o[:, D : D + LANES] = jnp.concatenate([dot_nn(dpl, u[...]), pdt[...]], axis=0).T.astype(BF)
        dxu_o[...] = du1[...] + dot_tn(dpl, wt[0:XW, :])
        pads = {1: pad1, 2: pad2, 3: pad3}
        xpad[0:8, :] = xhalo[...]
        xpad[8 : 8 + T, :] = xu[...].astype(F32)
        taps = [cw[k : k + 1, pl.ds(c0, C)] for k in range(4)]
        z8 = jnp.zeros((8, C), F32)
        for s in (1, 2, 3):
            pads[s][0:8, :] = z8
            pads[s][8 + T : 16 + T, :] = z8

        def block(i, tot):
            r0 = i * RB
            rs = pl.ds(r0, RB)
            p = rows_iota(r0, RB)
            vf = v[rs, :]
            sg = 1.0 / (1.0 + jnp.exp(-vf))
            dv = dxu_o[rs, :] * slope_of(vf, sg)
            new = [None] * 5
            full = xpad[pl.ds(r0, RB + 8), :]
            new[4] = tot[4] + jnp.sum(dv, axis=0, keepdims=True)
            for k in range(4):
                s = 3 - k
                x = full[8 - s : 8 - s + RB]
                m = dv
                if s:
                    m = dv * wide(tap_mask(sc, docs, p, s), C)
                    pads[s][pl.ds(8 + r0, RB), :] = taps[k] * m
                else:
                    dxu_o[rs, :] = taps[k] * m
                new[k] = tot[k] + jnp.sum(m * x, axis=0, keepdims=True)
            return tuple(new)

        z1 = jnp.zeros((1, C), F32)
        tot = lax.fori_loop(0, T // RB, block, (z1,) * 5)
        vec_o[...] = vec[...]
        for k in range(5):
            vec_o[k : k + 1, :] = tot[k]

        def gather(i, c):
            r0 = i * RB
            rs = pl.ds(r0, RB)
            acc = dxu_o[rs, :]
            for s in (1, 2, 3):
                acc = acc + pads[s][pl.ds(8 + r0, RB + 8), :][s : s + RB]
            dxu_o[rs, :] = acc
            return c

        lax.fori_loop(0, T // RB, gather, 0)
        acc = z8
        for s in (1, 2, 3):
            acc = acc + pads[s][s : s + 8, :]
        spill_o[...] = acc
        own = dot_tn(dxu_o[...].astype(BF), hb[...])
        pxt_o[:, 0:D] = (own + dot_tn(acc.astype(BF), halo[...])).astype(BF)

    outs = [((T, C), F32), ((8, C), F32), ((C, D + LANES), BF), (None, F32)]

    def build(vrows):
        o = outs[:3] + [((vrows, C), F32)]
        return call(back, o, 14, 1, [pltpu.VMEM((T + 16, C), F32)] * 3 + [pltpu.VMEM((T + 8, C), F32)])

    return build


def make_last(T, C, D, Q):
    def last(dxu, spill, dz, wa, wr, mix, x, rt, keep_o, send_o, gain_o):
        low = jnp.concatenate([jnp.zeros((T - 8, C), F32), spill[...]], axis=0)
        dx = (dxu[...] + low).astype(BF)
        dn = dot_nn(dx, wa[...]) + dot_nn(dz[...], wr[:, 0:D])
        xf = x[...].astype(F32)
        inv = lax.rsqrt(jnp.mean(xf * xf, axis=1, keepdims=True) + NORM_EPS)
        gain_o[...] = jnp.sum(dn * xf * inv, axis=0, keepdims=True)
        dnl = dn.astype(BF)
        for e in range(T // Q):
            r = rt[:, e * Q : (e + 1) * Q]
            o = send_o if e % 2 else keep_o
            at = slice((e // 2) * Q, (e // 2 + 1) * Q)
            o[at, 0:D] = dot_tn(r, mix[...]).astype(BF)
            o[at, D : 2 * D] = dot_tn(r, dnl).astype(BF)

    half = T // 2
    outs = [((half, 2 * D), BF), ((half, 2 * D), BF), ((1, D), F32)]
    return call(last, outs, 8, 0)


def flat_slots(k, shift, share, first, here):
    return ((k >> shift) ^ here) * share + first + (k & ((1 << shift) - 1))


def chunk_shape(T, CT, TP):
    share = T // CT
    SR = share // TP
    shift = SR.bit_length() - 1
    assert SR == 1 << shift and T // TP == CT * SR
    return T // TP, share, SR, shift


def make_send(T, D, CT, TP):
    Q, share, SR, shift = chunk_shape(T, CT, TP)

    def send(rsc, perm, x, dy, buf_o, pos_o):
        c = rsc[0]
        tp = rsc[1]
        own = perm[0:1, pl.ds(pl.multiple_of(c * T, LANES), T)].astype(F32)
        r = lax.broadcasted_iota(jnp.int32, (T, T), 0)
        q = lax.broadcasted_iota(jnp.int32, (T, T), 1)
        row = jnp.broadcast_to(own, (T, T))
        col = jnp.broadcast_to(jnp.sum(jnp.where(r == q, row, 0.0), axis=1, keepdims=True), (T, T))
        pos_row = jnp.sum(jnp.where(col < row, 1.0, 0.0), axis=0, keepdims=True)
        k = lax.broadcasted_iota(jnp.int32, (Q, T), 0)
        slot = flat_slots(k, shift, share, SR * tp, c).astype(F32)
        pick = jnp.where(slot == pos_row, 1.0, 0.0).astype(BF)
        buf_o[:, 0:D] = dot_nn(pick, x[...]).astype(BF)
        buf_o[:, D : 2 * D] = dot_nn(pick, dy[...]).astype(BF)
        pos_o[...] = pos_row

    return call(send, [((Q, 2 * D), BF), ((1, T), F32)], 4, 1)


def make_plan(T, CT, TP):
    Q, share, SR, shift = chunk_shape(T, CT, TP)

    def plan(rsc, perm, pos, rt_o, fin_o):
        c = rsc[0]
        tp = rsc[1]
        r = lax.broadcasted_iota(jnp.int32, (T, T), 0)
        q = lax.broadcasted_iota(jnp.int32, (T, T), 1)
        place = r + c * T
        lane = lax.broadcasted_iota(jnp.int32, (T, LANES), 1)
        hot = jnp.zeros((T, LANES), F32)
        for s in range(CT):
            src = jnp.broadcast_to(perm[0:1, s * T : (s + 1) * T], (T, T))
            n = jnp.sum(jnp.where(src == place, 1.0, 0.0), axis=1, keepdims=True)
            hot = jnp.where(lane == s, n, hot)
        below = jnp.where(q < r, 1.0, 0.0).astype(BF)
        count = dot_nn(below, hot.astype(BF))
        rank = jnp.sum(hot * count, axis=1, keepdims=True)
        block = jnp.sum(hot * lane.astype(F32), axis=1, keepdims=True)
        want = block * share + rank
        back = jnp.sum(jnp.where(r == q, jnp.broadcast_to(pos[...], (T, T)), 0.0), axis=1, keepdims=True)
        f = lax.broadcasted_iota(jnp.int32, (T, Q), 1)
        for e in range(TP):
            slot = flat_slots(f, shift, share, SR * (tp ^ e), c).astype(F32)
            rt_o[:, e * Q : (e + 1) * Q] = jnp.where(slot == want, 1.0, 0.0).astype(BF)
            fin_o[:, e * Q : (e + 1) * Q] = jnp.where(slot == back, 1.0, 0.0).astype(BF)

    return call(plan, [((T, T), BF)] * 2, 3, 1)


def make_recv(T, D, TP):
    Q = T // TP

    def recv(rt, gain, *rest):
        parts = rest[:TP]
        x_o, dy_o, hb_o = rest[TP:]
        xa = jnp.zeros((T, D), F32)
        ya = jnp.zeros((T, D), F32)
        for e in range(TP):
            m = rt[:, e * Q : (e + 1) * Q]
            xa = xa + dot_nn(m, parts[e][:, 0:D])
            ya = ya + dot_nn(m, parts[e][:, D : 2 * D])
        x_o[...] = xa.astype(BF)
        dy_o[...] = ya.astype(BF)
        inv = lax.rsqrt(jnp.mean(xa * xa, axis=1, keepdims=True) + NORM_EPS)
        hb_o[...] = (xa * inv * gain[...]).astype(BF)

    return call(recv, [((T, D), BF)] * 3, 2 + TP, 0)


def make_norm_back(Q, D):
    def norm_back(keep, got, far, own, gain, o):
        both = keep[0:Q].astype(F32) + got[0:Q].astype(F32) + far[...].astype(F32)
        xf = own[:, 0:D].astype(F32)
        inv = lax.rsqrt(jnp.mean(xf * xf, axis=1, keepdims=True) + NORM_EPS)
        dn = both[:, D : 2 * D]
        scaled = gain[...] * dn
        mean = jnp.mean(scaled * xf, axis=1, keepdims=True)
        o[:, 0:D] = (xf + both[:, 0:D]).astype(BF)
        o[:, D : 2 * D] = (
            own[:, D : 2 * D].astype(F32) + inv * scaled - xf * (inv * inv * inv) * mean
        ).astype(BF)

    return call(norm_back, [((Q, 2 * D), BF)], 5, 0)


def make_final(T, D, TP):
    Q = T // TP

    def final(fin, *rest):
        out_o, grad_o = rest[TP:]
        a = jnp.zeros((T, D), F32)
        b = jnp.zeros((T, D), F32)
        for e in range(TP):
            m = fin[:, e * Q : (e + 1) * Q]
            a = a + dot_nn(m, rest[e][:, 0:D])
            b = b + dot_nn(m, rest[e][:, D : 2 * D])
        out_o[...] = a.astype(BF)
        grad_o[...] = b.astype(BF)

    return call(final, [((T, D), BF)] * 2, 1 + TP, 0)


def halves(x):
    hi = x.astype(BF)
    return hi, (x - hi.astype(F32)).astype(BF)


def mul3(ah, al, bh, bl):
    return dot_nn(ah, bh) + (dot_nn(ah, bl) + dot_nn(al, bh))


def gram3(parts):
    def rows_of(i, b, n):
        at = slice(i * b, (i + 1) * b)
        tail = slice(i * b, n)
        tot = None
        for h, l in parts:
            one = dot_tn(h[:, at], h[:, tail]) + (dot_tn(h[:, at], l[:, tail]) + dot_tn(l[:, at], h[:, tail]))
            tot = one if tot is None else tot + one
        return tot

    return rows_of


def put_gram(o, parts, n):
    b = n // 3
    rows_of = gram3(parts)
    o[0:b, :] = rows_of(0, b, n)
    o[b : 2 * b, 0 : 2 * b] = rows_of(1, b, n)
    o[b : 2 * b, 2 * b : n] = rows_of(2, b, n)


def momentum_step(gradient, momentum_old):
    momentum_new = MOMENTUM * momentum_old + gradient
    return (momentum_new, gradient + MOMENTUM * momentum_new)


def make_gram_out(rows, D):
    def gram_out(got, mom, g1_o, go_o, mo_o, uo_o, gram_o):
        g1_o[...] = got[:, 0:D]
        g = got[:, D : 2 * D]
        m, u = momentum_step(g, mom[...])
        go_o[...] = g
        mo_o[...] = m
        uo_o[...] = u
        put_gram(gram_o, [halves(u)], D)

    outs = [((rows, D), F32)] * 4 + [((2 * D // 3, D), F32)]
    return call(gram_out, outs, 2, 0)


def make_gram_in(rows, D, XW, R, VR, pack, full):
    b = D // 3
    top = 2 * b

    def gram_in(place, got, g1, mom, xm, dm, vec, go, uo, gi_o, mi_o, gx_o, mx_o, gd_o, md_o, mine_o, away_o, um_o, ua_o, tmp):
        even = (place[1] & 1) == 0
        parts = []
        us = []
        for q in range(2):
            g = got[:, 0:D] if q == 0 else g1[...]
            m, u = momentum_step(g, mom[:, q, :])
            gi_o[:, q, :] = g
            mi_o[:, q, :] = m
            us.append(u)
            parts.append(halves(u))
        put_gram(tmp, parts, D)
        g = got[:, D : D + LANES]
        m, u = momentum_step(g, jnp.concatenate([xm[...], dm[...]], axis=1))
        gx_o[...] = g[:, 0:XW]
        gd_o[...] = g[:, XW : XW + R]
        mx_o[...] = m[:, 0:XW]
        md_o[...] = m[:, XW : XW + R]
        h, l = halves(u)
        small = dot_tn(h, h) + (dot_tn(h, l) + dot_tn(l, h))

        def put_in(buf, ub):
            buf[0:top, :] = tmp[...]
            buf[top : top + VR, :] = vec[...]
            if full > top + VR:
                buf[top + VR : full, :] = jnp.zeros((full - top - VR, D), F32)
            ub[0:rows, :] = us[0]
            ub[rows : 2 * rows, :] = us[1]

        def put_out(buf, ub):
            buf[0:top, :] = go[...]
            buf[top:full, :] = jnp.zeros((full - top, D), F32)
            for k in range(-(-LANES // pack)):
                lo = k * pack
                hi = min(lo + pack, LANES)
                buf[top : top + hi - lo, k * LANES : (k + 1) * LANES] = small[lo:hi]
            ub[0:rows, :] = uo[...]
            ub[rows : 2 * rows, :] = jnp.zeros((rows, D), F32)
            ub[rows : 2 * rows, 0:LANES] = u

        @pl.when(even)
        def _():
            put_in(mine_o, um_o)
            put_out(away_o, ua_o)

        @pl.when(jnp.logical_not(even))
        def _():
            put_out(mine_o, um_o)
            put_in(away_o, ua_o)

    outs = [((rows, 2, D), F32)] * 2
    outs += [((rows, XW), F32)] * 2 + [((rows, R), F32)] * 2 + [((full, D), F32)] * 2 + [((2 * rows, D), F32)] * 2
    return call(gram_in, outs, 9, 1, [pltpu.VMEM((top, D), F32)])


class Polar:
    def __init__(self, n, nbk, cuts, refs):
        self.n, self.nbk, self.cuts = n, nbk, list(cuts)
        self.blocks = n // nbk
        self.ah, self.al, self.qh, self.ql, self.th, self.tl, self.xs, self.acc = refs

    @staticmethod
    def scratch(n, rows):
        return [pltpu.VMEM((n, n), BF)] * 6 + [pltpu.VMEM((rows, n), F32), pltpu.VMEM((n, n), F32)]

    def at(self, b):
        return slice(b * self.nbk, (b + 1) * self.nbk)

    def put(self, i, value, hi_ref, lo_ref):
        h, l = halves(value)
        b = self.nbk
        hi_ref[self.at(i), i * b : self.n] = h
        lo_ref[self.at(i), i * b : self.n] = l
        for j in range(i + 1, self.blocks):
            h, l = halves(value[:, (j - i) * b : (j - i + 1) * b].T)
            hi_ref[self.at(j), self.at(i)] = h
            lo_ref[self.at(j), self.at(i)] = l

    def start(self, tails, upd):
        n, b = self.n, self.nbk
        col = lax.broadcasted_iota(jnp.int32, (1, n), 1)
        edges = [0] + self.cuts
        inv = jnp.zeros((1, n), F32)
        r = lax.broadcasted_iota(jnp.int32, (b, b), 0)
        c = lax.broadcasted_iota(jnp.int32, (b, b), 1)
        for lo, hi in zip(edges[:-1], edges[1:]):
            tot = jnp.zeros((1, 1), F32)
            for k in range(self.blocks):
                inside = (r == c) & (r + k * b >= lo) & (r + k * b < hi)
                d = jnp.sum(jnp.where(inside, tails[k][:, 0:b], 0.0), axis=1, keepdims=True)
                tot = tot + jnp.sum(d, axis=0, keepdims=True)
            inv = jnp.where((col >= lo) & (col < hi), 1.0 / (jnp.sqrt(tot) + 1e-07), inv)
        self.xs[...] = upd * inv
        for i in range(self.blocks):
            g = tails[i]
            if len(self.cuts) > 1:
                r = lax.broadcasted_iota(jnp.int32, g.shape, 0) + i * b
                c = lax.broadcasted_iota(jnp.int32, g.shape, 1) + i * b
                same = jnp.zeros(g.shape, F32)
                for lo, hi in zip(edges[:-1], edges[1:]):
                    same = jnp.where((r >= lo) & (r < hi) & (c >= lo) & (c < hi), 1.0, same)
                g = g * same
            one = inv[:, i * b : n]
            a = g * (one * one)
            self.acc[self.at(i), i * b : n] = a
            self.put(i, a, self.ah, self.al)

    def apply(self):
        for i in range(self.blocks):
            tail = slice(i * self.nbk, self.n)
            a2 = mul3(self.ah[self.at(i), :], self.al[self.at(i), :], self.ah[:, tail], self.al[:, tail])
            r = lax.broadcasted_iota(jnp.int32, a2.shape, 0)
            c = lax.broadcasted_iota(jnp.int32, a2.shape, 1)
            q = jnp.where(r == c, NS_A, 0.0) + (NS_B * self.acc[self.at(i), tail] + NS_C * a2)
            self.put(i, q, self.qh, self.ql)
        h, l = halves(self.xs[...])
        self.xs[...] = mul3(h, l, self.qh[...], self.ql[...])

    def advance(self):
        for src, dst in (((self.ah, self.al), (self.th, self.tl)), ((self.th, self.tl), (self.ah, self.al))):
            for i in range(self.blocks):
                tail = slice(i * self.nbk, self.n)
                a = mul3(src[0][self.at(i), :], src[1][self.at(i), :], self.qh[:, tail], self.ql[:, tail])
                if dst[0] is self.ah:
                    self.acc[self.at(i), tail] = a
                self.put(i, a, *dst)


def unpack_gram(buf, n):
    b = n // 3
    return [buf[0:b, :], buf[b : 2 * b, 0 : 2 * b], buf[b : 2 * b, 2 * b : n]]


def make_muon(D, rows, XW, R, pack, full):
    top = 2 * (D // 3)

    def muon(buf, um, ua, xm_o, xa_o, *refs):
        p = Polar(D, D // 3, (D,), refs[:8])
        s = Polar(LANES, LANES, (XW, XW + R), refs[8:16])
        small = jnp.concatenate(
            [
                buf[top : top + min(pack, LANES - k * pack), k * LANES : (k + 1) * LANES]
                for k in range(-(-LANES // pack))
            ],
            axis=0,
        )
        p.start(unpack_gram(buf, D), jnp.concatenate([um[...], ua[...]], axis=0))
        s.start([small], jnp.concatenate([um[rows:, 0:LANES], ua[rows:, 0:LANES]], axis=0))

        def step(k, c):
            p.apply()
            s.apply()
            p.advance()
            s.advance()
            return c

        lax.fori_loop(0, 4, step, 0)
        p.apply()
        s.apply()
        xm_o[...] = p.xs[0 : 2 * rows, :]
        xa_o[0:rows, :] = p.xs[2 * rows : 3 * rows, :]
        xa_o[rows : 2 * rows, :] = p.xs[3 * rows : 4 * rows, :]
        return s

    def body(place, buf, um, ua, xm_o, xa_o, *refs):
        s = muon(buf, um, ua, xm_o, xa_o, *refs)

        @pl.when((place[1] & 1) == 1)
        def _():
            xm_o[rows : 2 * rows, 0:LANES] = s.xs[0:rows, :]
            xa_o[rows : 2 * rows, 0:LANES] = s.xs[rows : 2 * rows, :]

    body.__name__ = "muon"
    scratch = Polar.scratch(D, 4 * rows) + Polar.scratch(LANES, 2 * rows)
    return call(body, [((2 * rows, D), F32)] * 2, 4, 1, scratch)


def make_finish(rows, D, XW, R, rates):
    def finish(place, xm, xr, wi, wx, wd, wo, oi, ox, od, oo):
        even = (place[1] & 1) == 0
        for q in range(2):
            at = slice(q * rows, (q + 1) * rows)
            oi[:, q, :] = wi[:, q, :] - rates[0] * jnp.where(even, xm[at], xr[at])
        oo[...] = wo[...] - rates[3] * jnp.where(even, xr[0:rows], xm[0:rows])
        s = jnp.where(even, xr[rows:, 0:LANES], xm[rows:, 0:LANES])
        ox[...] = wx[...] - rates[1] * s[:, 0:XW]
        od[...] = wd[...] - rates[2] * s[:, XW : XW + R]

    outs = [((rows, 2, D), F32), ((rows, XW), F32), ((rows, R), F32), ((rows, D), F32)]
    return call(finish, outs, 7, 1)


def make_pack(rows, D, XW, R):
    def pack(wi, wx, wd, wo, a_o, r_o):
        a_o[...] = wi[:, 0, :].astype(BF)
        r_o[:, 0:D] = wi[:, 1, :].astype(BF)
        r_o[:, D : D + LANES] = jnp.concatenate([wx[...], wd[...]], axis=1).astype(BF)
        r_o[:, D + LANES : 2 * D + LANES] = wo[...].astype(BF)

    return call(pack, [((rows, D), BF), ((rows, 2 * D + LANES), BF)], 4, 0)


def shifted(value, axis, by):
    devices = lax.axis_size(axis)
    pairs = [(i, i + by) for i in range(devices) if 0 <= i + by < devices]
    return lax.ppermute(value, axis, pairs)


def swap(value, axis, bit):
    devices = lax.axis_size(axis)
    return lax.ppermute(value, axis, [(i, i ^ bit) for i in range(devices)])


def side(axis, bit):
    return jnp.where((lax.axis_index(axis) & bit) != 0, 1, 0)


def in_order(mine, theirs, axis, bit):
    low = side(axis, bit) == 0
    return jnp.concatenate([jnp.where(low, mine, theirs), jnp.where(low, theirs, mine)], axis=0)


def half_sum(value, axis, bit):
    half = value.shape[0] // 2
    mine = side(axis, bit) * half
    away = lax.dynamic_slice_in_dim(value, half - mine, half)
    kept = lax.dynamic_slice_in_dim(value, mine, half)
    return kept + swap(away, axis, bit)


def half_join(value, axis, bit):
    return in_order(value, swap(value, axis, bit), axis, bit)


def bits_of(axis):
    count = lax.axis_size(axis)
    return [1 << k for k in range(count.bit_length() - 1)]


def sum_rest(value):
    cols = value.shape[1] // 2
    done = []
    for k in range(2):
        part = value[:, k * cols : (k + 1) * cols]
        cut = [("tp", 2), ("fsdp", 1), ("ctx", 1)] if k == 0 else [("fsdp", 1), ("tp", 2), ("ctx", 1)]
        rest = [(a, b) for a in ("tp", "fsdp", "ctx") for b in bits_of(a) if (a, b) not in cut + [("tp", 1)]]
        for axis, bit in cut:
            part = half_sum(part, axis, bit)
        for axis, bit in rest:
            part = part + swap(part, axis, bit)
        for axis, bit in cut[::-1]:
            part = half_join(part, axis, bit)
        done.append(part)
    return jnp.concatenate(done, axis=1)


def to_owners(grads, rows):
    steps = [("fsdp", b) for b in bits_of("fsdp")[::-1]] + [("ctx", b) for b in bits_of("ctx")]
    value = grads
    for axis, bit in steps:
        if axis == "fsdp":
            value = value.reshape(1, 2, value.shape[0] // 2, value.shape[1])
        else:
            value = value.reshape(value.shape[0] // (2 * rows), 2, rows, value.shape[1])
        mine = side(axis, bit)
        away = lax.dynamic_slice_in_dim(value, 1 - mine, 1, 1).astype(BF)
        kept = lax.dynamic_slice_in_dim(value, mine, 1, 1)
        value = kept.astype(F32) + swap(away, axis, bit).astype(F32)
        value = value.reshape(-1, value.shape[3])
    return value


def over_ctx(value):
    count = lax.axis_size("ctx")
    rows = value.shape[0] // count
    parts = [value[d * rows : (d + 1) * rows] for d in range(count)]
    return jnp.concatenate([parts[0]] + [swap(parts[d], "ctx", d) for d in range(1, count)], axis=0)


def doubled(value, axes):
    steps = [(a, b) for a in axes for b in bits_of(a)]
    for axis, bit in steps[:-1]:
        value = jnp.concatenate([value, swap(value, axis, bit)], axis=0)
    return value, swap(value, *steps[-1])


def adam_update(parameters, gradient, moment_one, moment_two, adam_step):
    count = adam_step[0].astype(jnp.float32)
    first_new = BETA_ONE * moment_one + (1.0 - BETA_ONE) * gradient
    second_new = BETA_TWO * moment_two + (1.0 - BETA_TWO) * gradient * gradient
    first_hat = first_new / (1.0 - jnp.power(jnp.float32(BETA_ONE), count))
    second_hat = second_new / (1.0 - jnp.power(jnp.float32(BETA_TWO), count))
    updated = parameters - ADAM_RATE * (
        first_hat / (jnp.sqrt(second_hat) + ADAM_EPS) + DECAY_RATE * parameters
    )
    return (updated, first_new, second_new)


def on_device(
    block_input,
    cotangent,
    route_perm,
    doc_lengths,
    norm_gain,
    in_proj,
    conv_weight,
    conv_bias,
    x_proj,
    dt_proj,
    dt_bias,
    a_log,
    skip_gain,
    out_proj,
    in_momentum,
    x_momentum,
    dt_momentum,
    out_momentum,
    adam_first,
    adam_second,
    adam_step,
):
    ctx_count = lax.axis_size("ctx")
    fsdp_count = lax.axis_size("fsdp")
    tp_count = lax.axis_size("tp")
    owners = fsdp_count * ctx_count
    ctx_index = lax.axis_index("ctx")
    tp_index = lax.axis_index("tp")
    tokens, width = block_input.shape
    stream = tokens * ctx_count
    quarter = tokens // tp_count
    own_rows = in_proj.shape[0]
    channels = own_rows * owners
    inner = conv_bias.shape[0]
    states = a_log.shape[0]
    rank = dt_proj.shape[1]
    xw = x_proj.shape[1]
    lengths = doc_lengths[0]
    docs = lengths.shape[0]
    offsets = jnp.cumsum(lengths) - lengths
    scal = jnp.concatenate(
        [(tp_index * channels)[None], offsets - ctx_index * tokens, ctx_index[None], lax.axis_index("fsdp")[None]]
    ).astype(jnp.int32)
    place = jnp.stack([ctx_index, tp_index]).astype(jnp.int32)
    perm_row = (route_perm % stream).reshape(1, stream)
    gain_row = norm_gain.reshape(1, width)

    w_a, w_r = make_pack(own_rows, width, xw, rank)(in_proj, x_proj, dt_proj, out_proj)
    send, send_pos = make_send(tokens, width, ctx_count, tp_count)(place, perm_row, block_input, cotangent)
    own = over_ctx(send)
    swapped = own_rows % 16 == 0
    if swapped:
        parts_in = doubled(w_a, ("fsdp", "ctx"))
        parts_rest = doubled(w_r, ("ctx", "fsdp"))
    else:
        half = channels // 2
        full_in, full_rest = [lax.all_gather(w, ("fsdp", "ctx"), axis=0, tiled=True) for w in (w_a, w_r)]
        parts_in = (full_in[:half], full_in[half:])
        parts_rest = (full_rest[:half], full_rest[half:])
    route, fin = make_plan(tokens, ctx_count, tp_count)(place, perm_row, send_pos)
    far = swap(own, "tp", 2)
    stream_x, stream_dy, normed = make_recv(tokens, width, tp_count)(
        route, gain_row, own, swap(own, "tp", 1), far, swap(far, "tp", 1)
    )

    halo = shifted(normed[tokens - 8 :], "ctx", 1)
    w_in, w_rest, conv_in, gate_in, conv_act, conv_out, pt_part, d_gated, w_turn, x_halo = make_front(
        tokens, channels, width, docs, xw, rank, ctx_count, fsdp_count, swapped
    )(scal, normed, halo, stream_dy, *parts_in, *parts_rest, conv_weight, conv_bias.reshape(1, inner))
    pt_pair = pt_part + swap(pt_part, "tp", 1)
    pt, dec, drv, d_inner, pre, ends = make_carry(
        tokens, channels, docs, xw, rank, states, ctx_count
    )(scal, pt_pair, swap(pt_pair, "tp", 2), conv_act, gate_in, d_gated, w_turn, dt_bias.reshape(1, inner), a_log)
    ends = [swap(ends[d], "ctx", d) for d in range(1, ctx_count)]
    gate_low, d_gate, du_one, d_pre_low, dp_part, mix_part, grads_one, part_dt, vec_part = make_scan(
        tokens, channels, width, docs, xw, rank, states, ctx_count
    )(
        scal, pt, dec, drv, d_inner, pre, conv_act, gate_in, d_gated, stream_dy, normed, w_rest, w_turn, a_log,
        skip_gain.reshape(1, inner), *ends,
    )

    got_one = to_owners(grads_one, own_rows)
    dp_pair = dp_part + swap(dp_part, "tp", 1)
    d_conv_in, spill, grads_two, vec_chan = make_back(tokens, channels, width, docs, xw, rank)(8 + states)(
        scal, dp_pair, swap(dp_pair, "tp", 2), du_one, conv_out, conv_act, conv_in, x_halo, w_turn, conv_weight,
        vec_part, part_dt, normed, halo,
    )
    got_two = to_owners(grads_two, own_rows)
    keep, away, g_gain = make_last(tokens, channels, width, quarter)(
        d_conv_in, shifted(spill, "ctx", -1), d_gate, w_in, w_rest, mix_part, stream_x, route
    )

    near = swap(away, "tp", 1)
    cross = (keep[quarter:].astype(F32) + near[quarter:].astype(F32)).astype(BF)
    back = make_norm_back(quarter, width)(keep, near, swap(cross, "tp", 2), own, gain_row)[0]
    home = over_ctx(back)
    home_far = swap(home, "tp", 2)
    block_out, input_grad = make_final(tokens, width, tp_count)(
        fin, home, swap(home, "tp", 1), home_far, swap(home_far, "tp", 1)
    )

    kinds = 8 + states
    pack = 24
    vec_wide = lax.dynamic_update_slice(jnp.zeros((kinds, inner), F32), vec_chan, (0, tp_index * channels))
    vec_wide = vec_wide + jnp.pad(g_gain, ((7, kinds - 8), (0, inner - width)))
    vec_rows = kinds * inner // width
    g_one, g_out, mom_out, upd_out, gram_out = make_gram_out(own_rows, width)(got_one, out_momentum)
    top = 2 * (width // 3)
    full = -(-(top + max(vec_rows, pack)) // 64) * 64
    g_in, mom_in, g_x, mom_x, g_dt, mom_dt, gram_mine, gram_away, upd_mine, upd_away = make_gram_in(
        own_rows, width, xw, rank, vec_rows, pack, full
    )(place, got_two, g_one, in_momentum, x_momentum, dt_momentum, vec_wide.reshape(vec_rows, width), gram_out, upd_out)
    gram = sum_rest(gram_mine + swap(gram_away, "tp", 1))
    x_mine, x_away = make_muon(width, own_rows, xw, rank, pack, full)(place, gram, upd_mine, swap(upd_away, "tp", 1))
    rates = [MUON_RATE * 0.2 * math.sqrt(max(a, b)) for a, b in ((2 * inner, width), (inner, xw), (inner, rank), (inner, width))]
    new_in, new_x, new_dt, new_out = make_finish(own_rows, width, xw, rank, rates)(
        place, x_mine, swap(x_away, "tp", 1), in_proj, x_proj, dt_proj, out_proj
    )
    vec_own = gram[top : top + vec_rows]
    vec_sum = jnp.where((tp_index & 1) == 0, vec_own, swap(vec_own, "tp", 1)).reshape(kinds, inner)
    g_alog = vec_sum[8:]
    vec_grads = jnp.concatenate(
        [vec_sum[7, :width], vec_sum[0:4].reshape(-1), vec_sum[4], vec_sum[5], g_alog.reshape(-1), vec_sum[6]]
    )
    vec_params = jnp.concatenate(
        [norm_gain, conv_weight.reshape(-1), conv_bias, dt_bias, a_log.reshape(-1), skip_gain]
    )
    new_vec, first_new, second_new = adam_update(vec_params, vec_grads, adam_first, adam_second, adam_step)
    cut_b = width + 4 * inner
    cut_c = cut_b + inner
    cut_d = cut_c + inner
    cut_e = cut_d + states * inner
    return (
        block_out,
        input_grad,
        vec_sum[7, :width],
        g_in,
        vec_sum[0:4],
        vec_sum[4],
        g_x,
        g_dt,
        vec_sum[5],
        g_alog,
        vec_sum[6],
        g_out,
        new_vec[:width],
        new_in,
        new_vec[width:cut_b].reshape(4, inner),
        new_vec[cut_b:cut_c],
        new_x,
        new_dt,
        new_vec[cut_c:cut_d],
        new_vec[cut_d:cut_e].reshape(states, inner),
        new_vec[cut_e:],
        new_out,
        mom_in,
        mom_x,
        mom_dt,
        mom_out,
        first_new,
        second_new,
    )


def solution(mesh):
    return jax.shard_map(
        on_device,
        mesh=mesh,
        in_specs=(
            P(("fsdp", "ctx"), None),
            P(("fsdp", "ctx"), None),
            P("fsdp"),
            P("fsdp", None),
            P(),
            P(("tp", "fsdp", "ctx"), None, None),
            P(),
            P(),
            P(("tp", "fsdp", "ctx"), None),
            P(("tp", "fsdp", "ctx"), None),
            P(),
            P(),
            P(),
            P(("tp", "fsdp", "ctx"), None),
            P(("tp", "fsdp", "ctx"), None, None),
            P(("tp", "fsdp", "ctx"), None),
            P(("tp", "fsdp", "ctx"), None),
            P(("tp", "fsdp", "ctx"), None),
            P(),
            P(),
            P(),
        ),
        out_specs=(
            P(("fsdp", "ctx"), None),
            P(("fsdp", "ctx"), None),
            P(),
            P(("tp", "fsdp", "ctx"), None, None),
            P(),
            P(),
            P(("tp", "fsdp", "ctx"), None),
            P(("tp", "fsdp", "ctx"), None),
            P(),
            P(),
            P(),
            P(("tp", "fsdp", "ctx"), None),
            P(),
            P(("tp", "fsdp", "ctx"), None, None),
            P(),
            P(),
            P(("tp", "fsdp", "ctx"), None),
            P(("tp", "fsdp", "ctx"), None),
            P(),
            P(),
            P(),
            P(("tp", "fsdp", "ctx"), None),
            P(("tp", "fsdp", "ctx"), None, None),
            P(("tp", "fsdp", "ctx"), None),
            P(("tp", "fsdp", "ctx"), None),
            P(("tp", "fsdp", "ctx"), None),
            P(),
            P(),
        ),
        check_vma=False,
    )
```

```python
import math

import jax
import jax.numpy as jnp
from jax import lax
from jax.experimental import pallas as pl
from jax.experimental.pallas import tpu as pltpu
from jax.sharding import PartitionSpec as P

F32 = jnp.float32
BF = jnp.bfloat16
LANES = 128
RESET = 1e5
LOG2E = 1.4426950408889634
VMEM_LIMIT = 60 * 1024 * 1024
NS_A = 3.4445
NS_B = -4.775
NS_C = 2.0315
MOMENTUM = 0.95
MUON_RATE = 0.1
ADAM_RATE = 0.25
BETA_ONE = 0.9
BETA_TWO = 0.95
ADAM_EPS = 1e-08
DECAY_RATE = 0.01
NORM_EPS = 1e-05


def dot_nn(a, b):
    return lax.dot_general(a, b, (((1,), (0,)), ((), ())), preferred_element_type=F32)


def dot_nt(a, b):
    return lax.dot_general(a, b, (((1,), (1,)), ((), ())), preferred_element_type=F32)


def dot_tn(a, b):
    return lax.dot_general(a, b, (((0,), (0,)), ((), ())), preferred_element_type=F32)


def soft(x):
    return jnp.maximum(x, 0.0) + jnp.log1p(jnp.exp(-jnp.abs(x)))


def slope_of(a, s):
    return s * (1.0 + a * (1.0 - s))


def call(body, outs, n_in, n_smem, scratch=(), flops=10**9):
    specs = [pl.BlockSpec(memory_space=pltpu.SMEM)] * n_smem + [
        pl.BlockSpec(memory_space=pltpu.VMEM)
    ] * (n_in - n_smem)
    return pl.pallas_call(
        body,
        out_shape=[jax.ShapeDtypeStruct(s, d) for s, d in outs],
        in_specs=specs,
        out_specs=[pl.BlockSpec(memory_space=pltpu.VMEM)] * len(outs),
        scratch_shapes=list(scratch),
        compiler_params=pltpu.CompilerParams(vmem_limit_bytes=VMEM_LIMIT),
        name=body.__name__,
    )


def rows_iota(r0, rows):
    return lax.broadcasted_iota(jnp.int32, (rows, LANES), 0) + r0


def tap_mask(sc_ref, docs, p, shift):
    ok = jnp.ones(p.shape, F32)
    for j in range(docs):
        off = sc_ref[1 + j]
        ok = jnp.where((off <= p) & (p < off + shift), 0.0, ok)
    return ok


def wide(mask, width):
    return jnp.concatenate([mask] * (width // LANES), axis=1)


def make_front(T, C, D, docs, XW, R, CT, FS, swapped):
    RB = 64

    def front(sc, hb, halo, dy, a0, a1, r0, r1, cw, cb, wa, wr, xu_o, z_o, u_o, v_o, pt_o, dg_o, wt_o, xh_o, xpad):
        own = C // (CT * FS)
        if swapped:
            z, f = sc[1 + docs], sc[2 + docs]
            for pieces, out in (((a0, a1), wa), ((r0, r1), wr)):
                for e in range(CT * FS):
                    fe, ze = (e % FS, e // FS) if out is wa else (e // CT, e % CT)
                    at = pl.multiple_of(((f ^ fe) * CT + (z ^ ze)) * own, own)
                    k = e * own
                    half = C // 2
                    piece = pieces[k // half]
                    out[pl.ds(at, own), :] = piece[k % half : k % half + own, :]
        else:
            wa[0 : C // 2, :] = a0[...]
            wa[C // 2 : C, :] = a1[...]
            wr[0 : C // 2, :] = r0[...]
            wr[C // 2 : C, :] = r1[...]
        w0 = wa[...]
        w1 = wr[:, 0:D]
        wo = wr[:, D + LANES : 2 * D + LANES]
        wt = wr[:, D : D + LANES].astype(F32).T.astype(BF)
        wt_o[...] = wt
        c0 = pl.multiple_of(sc[0], LANES)
        xh = dot_nt(halo[...], w0).astype(BF).astype(F32)
        xpad[0:8, :] = xh
        xh_o[...] = xh
        xu = dot_nt(hb[...], w0).astype(BF)
        xu_o[...] = xu
        xpad[8 : 8 + T, :] = xu.astype(F32)
        z_o[...] = dot_nt(hb[...], w1).astype(BF)
        dg_o[...] = dot_nt(dy[...], wo)
        taps = [cw[k : k + 1, pl.ds(c0, C)] for k in range(4)]
        bias = cb[0:1, pl.ds(c0, C)]

        def block(i, carry):
            r0 = i * RB
            p = rows_iota(r0, RB)
            v = bias + jnp.zeros((RB, C), F32)
            full = xpad[pl.ds(r0, RB + 8), :]
            for k in range(4):
                s = 3 - k
                x = full[8 - s : 8 - s + RB]
                if s:
                    x = x * wide(tap_mask(sc, docs, p, s), C)
                v = v + taps[k] * x
            v_o[pl.ds(r0, RB), :] = v
            u_o[pl.ds(r0, RB), :] = (v / (1.0 + jnp.exp(-v))).astype(BF)
            return carry

        lax.fori_loop(0, T // RB, block, 0)
        pt_o[...] = dot_nt(wt[0:XW], u_o[...])

    outs = [((C, D), BF), ((C, 2 * D + LANES), BF)]
    outs += [((T, C), BF)] * 3 + [((T, C), F32), ((XW, T), F32), ((T, C), F32), ((LANES, C), BF), ((8, C), F32)]
    return call(front, outs, 10, 1, [pltpu.VMEM((T + 8, C), F32)])


CHUNK = 128


def at_lane(i, n):
    shape = (CHUNK, n, LANES)
    return lax.broadcasted_iota(jnp.int32, shape, 2) == lax.broadcasted_iota(jnp.int32, shape, 0) + i * CHUNK


def row_totals(hi, lo):
    rows = hi.shape[0] * hi.shape[1]
    both = jnp.concatenate([hi.reshape(rows, LANES).astype(BF), lo.reshape(rows, LANES).astype(BF)], axis=1)
    return dot_nn(both, jnp.ones((2 * LANES, LANES), BF)).reshape(hi.shape)


def lane_sums(ref):
    n = ref.shape[1]

    def chunk(i, tot):
        x = ref[pl.ds(i * CHUNK, CHUNK)]
        hi = x.astype(BF).astype(F32)
        return tot + jnp.sum(jnp.where(at_lane(i, n), row_totals(hi, x - hi), 0.0), axis=0)

    return lax.fori_loop(0, LANES // CHUNK, chunk, jnp.zeros((n, LANES), F32))


def spread(x, out, base):
    n = x.shape[0]
    hi = x.astype(BF).astype(F32)
    lo = x - hi

    def chunk(i, c):
        m = at_lane(i, n)
        out[pl.ds(base + i * CHUNK, CHUNK)] = row_totals(jnp.where(m, hi[None], 0.0), jnp.where(m, lo[None], 0.0))
        return c

    lax.fori_loop(0, LANES // CHUNK, chunk, 0)


def make_carry(T, C, docs, XW, R, N, CT):
    RB = 64
    LT = C // LANES

    def carry(sc, pa, pb, u, z, dg, wt, dtb, alog, pt_o, da_o, du_o, dyin_o, pre_o, ends_o, bs, cs):
        c0 = pl.multiple_of(sc[0], LANES)
        pt = pa[...] + pb[...]
        pt_o[...] = pt
        lin = dot_tn(pt[0:R].astype(BF), wt[XW : XW + R, :])
        pre_o[...] = lin + dtb[0:1, pl.ds(c0, C)]

        def block(i, tot):
            rs = pl.ds(i * RB, RB)
            p = rows_iota(i * RB, RB)
            keep = jnp.ones((RB, LANES), F32)
            for j in range(docs):
                keep = jnp.where(p == sc[1 + j], 0.0, keep)
            x = pre_o[rs, :]
            delta = soft(x)
            d = jnp.where(wide(keep, C) > 0.0, delta, RESET)
            r8 = pl.ds(i * (RB // 8), RB // 8)
            da_o[r8] = d.reshape(RB // 8, 8, C)
            du_o[r8] = (delta * u[rs, :].astype(F32)).reshape(RB // 8, 8, C)
            zf = z[rs, :].astype(F32)
            dyin_o[r8] = (dg[rs, :] * (zf / (1.0 + jnp.exp(-zf)))).reshape(RB // 8, 8, C)
            return tot + jnp.sum(d, axis=0, keepdims=True)

        tot = lax.fori_loop(0, T // RB, block, jnp.zeros((1, C), F32))
        am = [-jnp.exp(alog[:, pl.ds(c0 + l * LANES, LANES)]) for l in range(LT)]
        am2 = [a * LOG2E for a in am]

        def rows(ref, i, j):
            full = ref[i, pl.ds(j, N, stride=0), :]
            return [full[:, l * LANES : (l + 1) * LANES] for l in range(LT)]

        nb = T // LANES

        def outer(k, c):
            bt = pt_o[R_ : R_ + N, pl.ds(pl.multiple_of(k * LANES, LANES), LANES)]
            ct = pt_o[R_ + N : R_ + 2 * N, pl.ds(pl.multiple_of((nb - 1 - k) * LANES, LANES), LANES)]

            spread(bt, bs, 0)
            spread(ct, cs, 0)

            def inner(i, c):
                h, g = c
                h = list(h)
                g = list(g)
                fi = k * (LANES // 8) + i
                ri = T // 8 - 1 - fi
                for j in range(8):
                    bb = bs[i * 8 + j]
                    cc = cs[LANES - 1 - i * 8 - j]
                    df, uf = rows(da_o, fi, j), rows(du_o, fi, j)
                    db, yb = rows(da_o, ri, 7 - j), rows(dyin_o, ri, 7 - j)
                    for l in range(LT):
                        h[l] = jnp.exp2(df[l] * am2[l]) * h[l] + uf[l] * bb
                        g[l] = jnp.exp2(db[l] * am2[l]) * (g[l] + yb[l] * cc)
                return tuple(h), tuple(g)

            return lax.fori_loop(0, LANES // 8, inner, (c[0], c[1]))

        R_ = R
        zero = tuple(jnp.zeros((N, LANES), F32) for _ in range(LT))
        h, g = lax.fori_loop(0, nb, outer, (zero, zero))
        here = sc[1 + docs]
        for d in range(CT):
            for l in range(LT):
                ends_o[d, 0:N, l * LANES : (l + 1) * LANES] = jnp.where((here ^ d) > here, h[l], g[l])
            ends_o[d, N : N + 8, :] = jnp.broadcast_to(tot, (8, C))

    outs = [((XW, T), F32)] + [((T // 8, 8, C), F32)] * 3 + [((T, C), F32)] + [((CT, N + 8, C), F32)]
    return call(carry, outs, 9, 1, [pltpu.VMEM((LANES, N, LANES), F32)] * 2)


def make_scan(T, C, D, docs, XW, R, N, CT):
    RB = 64
    LT = C // LANES
    nb = T // LANES

    def scan(sc, pt, da, du, dyin, pre, u, z, dg, dy, hb, wr, wt, alog, skip, *rest):
        ends = rest[: CT - 1]
        (
            g_o, dz_o, du1_o, dpre_o, dp_o, mix_o, pw_o, pdt_o, vec_o,
            a_s, h_s, y_s, lb_s, dd_s, sb_s, sc_s, bs, cs,
        ) = rest[CT - 1 :]
        c0 = pl.multiple_of(sc[0], LANES)
        am = [-jnp.exp(alog[:, pl.ds(c0 + l * LANES, LANES)]) for l in range(LT)]
        am2 = [a * LOG2E for a in am]
        sl = [slice(l * LANES, (l + 1) * LANES) for l in range(LT)]
        top4 = lax.broadcasted_iota(jnp.int32, (8, LANES), 0) < 4

        def rows(ref, i, j):
            full = ref[i, pl.ds(j, N, stride=0), :]
            return [full[:, sl[l]] for l in range(LT)]

        here = sc[1 + docs]
        hin, gin = [], []
        for l in range(LT):
            for way, got in ((-1, hin), (1, gin)):
                near = jnp.zeros((N, LANES), F32)
                tot = jnp.zeros((1, LANES), F32)
                far = near
                for d in range(1, CT):
                    e = ends[d - 1]
                    near = jnp.where((here ^ d) == here + way, e[0:N, sl[l]], near)
                    tot = jnp.where((here ^ d) == here + way, e[N : N + 1, sl[l]], tot)
                    far = jnp.where((here ^ d) == here + 2 * way, e[0:N, sl[l]], far)
                got.append(near + jnp.exp2(jnp.broadcast_to(tot, (N, LANES)) * am2[l]) * far)
            h_s[0, :, sl[l]] = hin[l]

        def fouter(k, h):
            blk = pl.ds(pl.multiple_of(k * LANES, LANES), LANES)
            spread(pt[R : R + N, blk], bs, k * LANES)
            spread(pt[R + N : R + 2 * N, blk], cs, k * LANES)

            def inner(i, h):
                h = list(h)
                fi = k * (LANES // 8) + i
                for j in range(8):
                    t = fi * 8 + j
                    bb = bs[t]
                    cc = cs[t]
                    dr, ur = rows(da, fi, j), rows(du, fi, j)
                    for l in range(LT):
                        a = jnp.exp2(dr[l] * am2[l])
                        a_s[t, :, sl[l]] = a
                        h[l] = a * h[l] + ur[l] * bb
                        h_s[t + 1, :, sl[l]] = h[l]
                        y_s[fi, j : j + 1, sl[l]] = jnp.sum(h[l] * cc, axis=0, keepdims=True)
                return tuple(h)

            return lax.fori_loop(0, LANES // 8, inner, h)

        lax.fori_loop(0, nb, fouter, tuple(hin))

        def bouter(k, c):
            kb = nb - 1 - k
            blk = pl.ds(pl.multiple_of(kb * LANES, LANES), LANES)
            zero = jnp.zeros((N, LANES), F32)

            def inner(i, c):
                g, ga = c
                g = list(g)
                ga = list(ga)
                l0 = LANES - 1 - i * 8
                fi = kb * (LANES // 8) + LANES // 8 - 1 - i
                for j in range(8):
                    t = kb * LANES + l0 - j
                    jj = 7 - j
                    bb = bs[t]
                    cc = cs[t]
                    sb = zero
                    scc = zero
                    dr, ur, yr = rows(da, fi, jj), rows(du, fi, jj), rows(dyin, fi, jj)
                    for l in range(LT):
                        dyr = yr[l]
                        lam = cc * dyr + g[l]
                        g[l] = a_s[t, :, sl[l]] * lam
                        dal = g[l] * h_s[t, :, sl[l]]
                        pb = lam * bb
                        pd = dal * am[l]
                        pb = pb[0:8] + pb[8:16]
                        pd = pd[0:8] + pd[8:16]
                        both = jnp.where(top4, pb, pd) + pltpu.roll(jnp.where(top4, pd, pb), 4, 0)
                        both = both + pltpu.roll(both, 6, 0)
                        both = both + pltpu.roll(both, 7, 0)
                        lb_s[fi, jj : jj + 1, sl[l]] = both[0:1]
                        dd_s[fi, jj : jj + 1, sl[l]] = both[4:5]
                        ga[l] = ga[l] + dal * dr[l]
                        sb = sb + lam * ur[l]
                        scc = scc + dyr * h_s[t + 1, :, sl[l]]
                    sb_s[l0 - j] = sb
                    sc_s[l0 - j] = scc
                return tuple(g), tuple(ga)

            g, ga = lax.fori_loop(0, LANES // 8, inner, (c[0], c[1]))
            dp_o[R : R + N, blk] = lane_sums(sb_s)
            dp_o[R + N : R + 2 * N, blk] = lane_sums(sc_s)
            return g, ga

        zeros = tuple(jnp.zeros((N, LANES), F32) for _ in range(LT))
        _, ga = lax.fori_loop(0, nb, bouter, (tuple(gin), zeros))
        for l in range(LT):
            vec_o[8 : 8 + N, sl[l]] = am[l] * ga[l]
        skr = skip[0:1, pl.ds(c0, C)]

        def block(i, tot):
            gdt, gsk = tot
            rs = pl.ds(i * RB, RB)
            r8 = pl.ds(i * (RB // 8), RB // 8)
            uf = u[rs, :].astype(F32)
            zf = z[rs, :].astype(F32)
            s = 1.0 / (1.0 + jnp.exp(-zf))
            yin = y_s[r8].reshape(RB, C) + skr * uf
            g_o[rs, :] = (yin * (zf * s)).astype(BF)
            dz_o[rs, :] = (dg[rs, :] * yin * slope_of(zf, s)).astype(BF)
            lb = lb_s[r8].reshape(RB, C)
            dyr = dyin[r8].reshape(RB, C)
            x = pre[rs, :]
            dpre = (lb * uf + dd_s[r8].reshape(RB, C)) / (1.0 + jnp.exp(-x))
            dpre_o[rs, :] = dpre.astype(BF)
            du1_o[rs, :] = dyr * skr + lb * soft(x)
            return gdt + jnp.sum(dpre, axis=0, keepdims=True), gsk + jnp.sum(dyr * uf, axis=0, keepdims=True)

        z1 = jnp.zeros((1, C), F32)
        gdt, gsk = lax.fori_loop(0, T // RB, block, (z1, z1))
        vec_o[5:6, :] = gdt
        vec_o[6:7, :] = gsk
        vec_o[7:8, :] = z1
        vec_o[0:5, :] = jnp.zeros((5, C), F32)
        dp_o[0:R, :] = dot_nt(wt[XW : XW + R, :], dpre_o[...])
        pdt_o[...] = dot_nn(pt[0:R, :].astype(BF), dpre_o[...])
        mix_o[...] = dot_nn(g_o[...], wr[:, D + LANES : 2 * D + LANES]).astype(BF)
        pw_o[:, 0:D] = dot_tn(dz_o[...], hb[...]).astype(BF)
        pw_o[:, D : 2 * D] = dot_tn(g_o[...], dy[...]).astype(BF)

    outs = [((T, C), BF), ((T, C), BF), ((T, C), F32), ((T, C), BF), ((XW, T), F32), ((T, D), BF),
            ((C, 2 * D), BF), ((R, C), F32), ((8 + N, C), F32)]
    scratch = [pltpu.VMEM((T, N, C), F32), pltpu.VMEM((T + 1, N, C), F32)] + [pltpu.VMEM((T // 8, 8, C), F32)] * 3
    scratch += [pltpu.VMEM((LANES, N, LANES), F32)] * 2 + [pltpu.VMEM((T, N, LANES), F32)] * 2
    return call(scan, outs, 14 + CT, 1, scratch)


def make_back(T, C, D, docs, XW, R):
    RB = 64

    def back(sc, da_, db_, du1, v, u, xu, xhalo, wt, cw, vec, pdt, hb, halo, dxu_o, spill_o, pxt_o, vec_o, pad1, pad2, pad3, xpad):
        c0 = pl.multiple_of(sc[0], LANES)
        dpl = (da_[...] + db_[...]).astype(BF)
        pxt_o[:, D : D + LANES] = jnp.concatenate([dot_nn(dpl, u[...]), pdt[...]], axis=0).T.astype(BF)
        dxu_o[...] = du1[...] + dot_tn(dpl, wt[0:XW, :])
        pads = {1: pad1, 2: pad2, 3: pad3}
        xpad[0:8, :] = xhalo[...]
        xpad[8 : 8 + T, :] = xu[...].astype(F32)
        taps = [cw[k : k + 1, pl.ds(c0, C)] for k in range(4)]
        z8 = jnp.zeros((8, C), F32)
        for s in (1, 2, 3):
            pads[s][0:8, :] = z8
            pads[s][8 + T : 16 + T, :] = z8

        def block(i, tot):
            r0 = i * RB
            rs = pl.ds(r0, RB)
            p = rows_iota(r0, RB)
            vf = v[rs, :]
            sg = 1.0 / (1.0 + jnp.exp(-vf))
            dv = dxu_o[rs, :] * slope_of(vf, sg)
            new = [None] * 5
            full = xpad[pl.ds(r0, RB + 8), :]
            new[4] = tot[4] + jnp.sum(dv, axis=0, keepdims=True)
            for k in range(4):
                s = 3 - k
                x = full[8 - s : 8 - s + RB]
                m = dv
                if s:
                    m = dv * wide(tap_mask(sc, docs, p, s), C)
                    pads[s][pl.ds(8 + r0, RB), :] = taps[k] * m
                else:
                    dxu_o[rs, :] = taps[k] * m
                new[k] = tot[k] + jnp.sum(m * x, axis=0, keepdims=True)
            return tuple(new)

        z1 = jnp.zeros((1, C), F32)
        tot = lax.fori_loop(0, T // RB, block, (z1,) * 5)
        vec_o[...] = vec[...]
        for k in range(5):
            vec_o[k : k + 1, :] = tot[k]

        def gather(i, c):
            r0 = i * RB
            rs = pl.ds(r0, RB)
            acc = dxu_o[rs, :]
            for s in (1, 2, 3):
                acc = acc + pads[s][pl.ds(8 + r0, RB + 8), :][s : s + RB]
            dxu_o[rs, :] = acc
            return c

        lax.fori_loop(0, T // RB, gather, 0)
        acc = z8
        for s in (1, 2, 3):
            acc = acc + pads[s][s : s + 8, :]
        spill_o[...] = acc
        own = dot_tn(dxu_o[...].astype(BF), hb[...])
        pxt_o[:, 0:D] = (own + dot_tn(acc.astype(BF), halo[...])).astype(BF)

    outs = [((T, C), F32), ((8, C), F32), ((C, D + LANES), BF), (None, F32)]

    def build(vrows):
        o = outs[:3] + [((vrows, C), F32)]
        return call(back, o, 14, 1, [pltpu.VMEM((T + 16, C), F32)] * 3 + [pltpu.VMEM((T + 8, C), F32)])

    return build


def make_last(T, C, D, Q):
    def last(dxu, spill, dz, wa, wr, mix, x, rt, keep_o, send_o, gain_o):
        low = jnp.concatenate([jnp.zeros((T - 8, C), F32), spill[...]], axis=0)
        dx = (dxu[...] + low).astype(BF)
        dn = dot_nn(dx, wa[...]) + dot_nn(dz[...], wr[:, 0:D])
        xf = x[...].astype(F32)
        inv = lax.rsqrt(jnp.mean(xf * xf, axis=1, keepdims=True) + NORM_EPS)
        gain_o[...] = jnp.sum(dn * xf * inv, axis=0, keepdims=True)
        dnl = dn.astype(BF)
        for e in range(T // Q):
            r = rt[:, e * Q : (e + 1) * Q]
            o = send_o if e % 2 else keep_o
            at = slice((e // 2) * Q, (e // 2 + 1) * Q)
            o[at, 0:D] = dot_tn(r, mix[...]).astype(BF)
            o[at, D : 2 * D] = dot_tn(r, dnl).astype(BF)

    half = T // 2
    outs = [((half, 2 * D), BF), ((half, 2 * D), BF), ((1, D), F32)]
    return call(last, outs, 8, 0)


def flat_slots(k, shift, share, first, here):
    return ((k >> shift) ^ here) * share + first + (k & ((1 << shift) - 1))


def chunk_shape(T, CT, TP):
    share = T // CT
    SR = share // TP
    shift = SR.bit_length() - 1
    assert SR == 1 << shift and T // TP == CT * SR
    return T // TP, share, SR, shift


def make_send(T, D, CT, TP):
    Q, share, SR, shift = chunk_shape(T, CT, TP)

    def send(rsc, perm, x, dy, buf_o, pos_o):
        c = rsc[0]
        tp = rsc[1]
        own = perm[0:1, pl.ds(pl.multiple_of(c * T, LANES), T)].astype(F32)
        r = lax.broadcasted_iota(jnp.int32, (T, T), 0)
        q = lax.broadcasted_iota(jnp.int32, (T, T), 1)
        row = jnp.broadcast_to(own, (T, T))
        col = jnp.broadcast_to(jnp.sum(jnp.where(r == q, row, 0.0), axis=1, keepdims=True), (T, T))
        pos_row = jnp.sum(jnp.where(col < row, 1.0, 0.0), axis=0, keepdims=True)
        k = lax.broadcasted_iota(jnp.int32, (Q, T), 0)
        slot = flat_slots(k, shift, share, SR * tp, c).astype(F32)
        pick = jnp.where(slot == pos_row, 1.0, 0.0).astype(BF)
        buf_o[:, 0:D] = dot_nn(pick, x[...]).astype(BF)
        buf_o[:, D : 2 * D] = dot_nn(pick, dy[...]).astype(BF)
        pos_o[...] = pos_row

    return call(send, [((Q, 2 * D), BF), ((1, T), F32)], 4, 1)


def make_plan(T, CT, TP):
    Q, share, SR, shift = chunk_shape(T, CT, TP)

    def plan(rsc, perm, pos, rt_o, fin_o):
        c = rsc[0]
        tp = rsc[1]
        r = lax.broadcasted_iota(jnp.int32, (T, T), 0)
        q = lax.broadcasted_iota(jnp.int32, (T, T), 1)
        place = r + c * T
        lane = lax.broadcasted_iota(jnp.int32, (T, LANES), 1)
        hot = jnp.zeros((T, LANES), F32)
        for s in range(CT):
            src = jnp.broadcast_to(perm[0:1, s * T : (s + 1) * T], (T, T))
            n = jnp.sum(jnp.where(src == place, 1.0, 0.0), axis=1, keepdims=True)
            hot = jnp.where(lane == s, n, hot)
        below = jnp.where(q < r, 1.0, 0.0).astype(BF)
        count = dot_nn(below, hot.astype(BF))
        rank = jnp.sum(hot * count, axis=1, keepdims=True)
        block = jnp.sum(hot * lane.astype(F32), axis=1, keepdims=True)
        want = block * share + rank
        back = jnp.sum(jnp.where(r == q, jnp.broadcast_to(pos[...], (T, T)), 0.0), axis=1, keepdims=True)
        f = lax.broadcasted_iota(jnp.int32, (T, Q), 1)
        for e in range(TP):
            slot = flat_slots(f, shift, share, SR * (tp ^ e), c).astype(F32)
            rt_o[:, e * Q : (e + 1) * Q] = jnp.where(slot == want, 1.0, 0.0).astype(BF)
            fin_o[:, e * Q : (e + 1) * Q] = jnp.where(slot == back, 1.0, 0.0).astype(BF)

    return call(plan, [((T, T), BF)] * 2, 3, 1)


def make_recv(T, D, TP):
    Q = T // TP

    def recv(rt, gain, *rest):
        parts = rest[:TP]
        x_o, dy_o, hb_o = rest[TP:]
        xa = jnp.zeros((T, D), F32)
        ya = jnp.zeros((T, D), F32)
        for e in range(TP):
            m = rt[:, e * Q : (e + 1) * Q]
            xa = xa + dot_nn(m, parts[e][:, 0:D])
            ya = ya + dot_nn(m, parts[e][:, D : 2 * D])
        x_o[...] = xa.astype(BF)
        dy_o[...] = ya.astype(BF)
        inv = lax.rsqrt(jnp.mean(xa * xa, axis=1, keepdims=True) + NORM_EPS)
        hb_o[...] = (xa * inv * gain[...]).astype(BF)

    return call(recv, [((T, D), BF)] * 3, 2 + TP, 0)


def make_norm_back(Q, D):
    def norm_back(keep, got, far, own, gain, o):
        both = keep[0:Q].astype(F32) + got[0:Q].astype(F32) + far[...].astype(F32)
        xf = own[:, 0:D].astype(F32)
        inv = lax.rsqrt(jnp.mean(xf * xf, axis=1, keepdims=True) + NORM_EPS)
        dn = both[:, D : 2 * D]
        scaled = gain[...] * dn
        mean = jnp.mean(scaled * xf, axis=1, keepdims=True)
        o[:, 0:D] = (xf + both[:, 0:D]).astype(BF)
        o[:, D : 2 * D] = (
            own[:, D : 2 * D].astype(F32) + inv * scaled - xf * (inv * inv * inv) * mean
        ).astype(BF)

    return call(norm_back, [((Q, 2 * D), BF)], 5, 0)


def make_final(T, D, TP):
    Q = T // TP

    def final(fin, *rest):
        out_o, grad_o = rest[TP:]
        a = jnp.zeros((T, D), F32)
        b = jnp.zeros((T, D), F32)
        for e in range(TP):
            m = fin[:, e * Q : (e + 1) * Q]
            a = a + dot_nn(m, rest[e][:, 0:D])
            b = b + dot_nn(m, rest[e][:, D : 2 * D])
        out_o[...] = a.astype(BF)
        grad_o[...] = b.astype(BF)

    return call(final, [((T, D), BF)] * 2, 1 + TP, 0)


def halves(x):
    hi = x.astype(BF)
    return hi, (x - hi.astype(F32)).astype(BF)


def mul3(ah, al, bh, bl):
    return dot_nn(ah, bh) + (dot_nn(ah, bl) + dot_nn(al, bh))


def gram3(parts):
    def rows_of(i, b, n):
        at = slice(i * b, (i + 1) * b)
        tail = slice(i * b, n)
        tot = None
        for h, l in parts:
            one = dot_tn(h[:, at], h[:, tail]) + (dot_tn(h[:, at], l[:, tail]) + dot_tn(l[:, at], h[:, tail]))
            tot = one if tot is None else tot + one
        return tot

    return rows_of


def put_gram(o, parts, n):
    b = n // 3
    rows_of = gram3(parts)
    o[0:b, :] = rows_of(0, b, n)
    o[b : 2 * b, 0 : 2 * b] = rows_of(1, b, n)
    o[b : 2 * b, 2 * b : n] = rows_of(2, b, n)


def momentum_step(gradient, momentum_old):
    momentum_new = MOMENTUM * momentum_old + gradient
    return (momentum_new, gradient + MOMENTUM * momentum_new)


def make_gram_out(rows, D):
    def gram_out(got, mom, g1_o, go_o, mo_o, uo_o, gram_o):
        g1_o[...] = got[:, 0:D]
        g = got[:, D : 2 * D]
        m, u = momentum_step(g, mom[...])
        go_o[...] = g
        mo_o[...] = m
        uo_o[...] = u
        put_gram(gram_o, [halves(u)], D)

    outs = [((rows, D), F32)] * 4 + [((2 * D // 3, D), F32)]
    return call(gram_out, outs, 2, 0)


def make_gram_in(rows, D, XW, R, VR, pack, full):
    b = D // 3
    top = 2 * b

    def gram_in(place, got, g1, mom, xm, dm, vec, go, uo, gi_o, mi_o, gx_o, mx_o, gd_o, md_o, mine_o, away_o, um_o, ua_o, tmp):
        even = (place[1] & 1) == 0
        parts = []
        us = []
        for q in range(2):
            g = got[:, 0:D] if q == 0 else g1[...]
            m, u = momentum_step(g, mom[:, q, :])
            gi_o[:, q, :] = g
            mi_o[:, q, :] = m
            us.append(u)
            parts.append(halves(u))
        put_gram(tmp, parts, D)
        g = got[:, D : D + LANES]
        m, u = momentum_step(g, jnp.concatenate([xm[...], dm[...]], axis=1))
        gx_o[...] = g[:, 0:XW]
        gd_o[...] = g[:, XW : XW + R]
        mx_o[...] = m[:, 0:XW]
        md_o[...] = m[:, XW : XW + R]
        h, l = halves(u)
        small = dot_tn(h, h) + (dot_tn(h, l) + dot_tn(l, h))

        def put_in(buf, ub):
            buf[0:top, :] = tmp[...]
            buf[top : top + VR, :] = vec[...]
            if full > top + VR:
                buf[top + VR : full, :] = jnp.zeros((full - top - VR, D), F32)
            ub[0:rows, :] = us[0]
            ub[rows : 2 * rows, :] = us[1]

        def put_out(buf, ub):
            buf[0:top, :] = go[...]
            buf[top:full, :] = jnp.zeros((full - top, D), F32)
            for k in range(-(-LANES // pack)):
                lo = k * pack
                hi = min(lo + pack, LANES)
                buf[top : top + hi - lo, k * LANES : (k + 1) * LANES] = small[lo:hi]
            ub[0:rows, :] = uo[...]
            ub[rows : 2 * rows, :] = jnp.zeros((rows, D), F32)
            ub[rows : 2 * rows, 0:LANES] = u

        @pl.when(even)
        def _():
            put_in(mine_o, um_o)
            put_out(away_o, ua_o)

        @pl.when(jnp.logical_not(even))
        def _():
            put_out(mine_o, um_o)
            put_in(away_o, ua_o)

    outs = [((rows, 2, D), F32)] * 2
    outs += [((rows, XW), F32)] * 2 + [((rows, R), F32)] * 2 + [((full, D), F32)] * 2 + [((2 * rows, D), F32)] * 2
    return call(gram_in, outs, 9, 1, [pltpu.VMEM((top, D), F32)])


class Polar:
    def __init__(self, n, nbk, cuts, refs):
        self.n, self.nbk, self.cuts = n, nbk, list(cuts)
        self.blocks = n // nbk
        self.ah, self.al, self.qh, self.ql, self.th, self.tl, self.xs, self.acc = refs

    @staticmethod
    def scratch(n, rows):
        return [pltpu.VMEM((n, n), BF)] * 6 + [pltpu.VMEM((rows, n), F32), pltpu.VMEM((n, n), F32)]

    def at(self, b):
        return slice(b * self.nbk, (b + 1) * self.nbk)

    def put(self, i, value, hi_ref, lo_ref):
        h, l = halves(value)
        b = self.nbk
        hi_ref[self.at(i), i * b : self.n] = h
        lo_ref[self.at(i), i * b : self.n] = l
        for j in range(i + 1, self.blocks):
            h, l = halves(value[:, (j - i) * b : (j - i + 1) * b].T)
            hi_ref[self.at(j), self.at(i)] = h
            lo_ref[self.at(j), self.at(i)] = l

    def start(self, tails, upd):
        n, b = self.n, self.nbk
        col = lax.broadcasted_iota(jnp.int32, (1, n), 1)
        edges = [0] + self.cuts
        inv = jnp.zeros((1, n), F32)
        r = lax.broadcasted_iota(jnp.int32, (b, b), 0)
        c = lax.broadcasted_iota(jnp.int32, (b, b), 1)
        for lo, hi in zip(edges[:-1], edges[1:]):
            tot = jnp.zeros((1, 1), F32)
            for k in range(self.blocks):
                inside = (r == c) & (r + k * b >= lo) & (r + k * b < hi)
                d = jnp.sum(jnp.where(inside, tails[k][:, 0:b], 0.0), axis=1, keepdims=True)
                tot = tot + jnp.sum(d, axis=0, keepdims=True)
            inv = jnp.where((col >= lo) & (col < hi), 1.0 / (jnp.sqrt(tot) + 1e-07), inv)
        self.xs[...] = upd * inv
        for i in range(self.blocks):
            g = tails[i]
            if len(self.cuts) > 1:
                r = lax.broadcasted_iota(jnp.int32, g.shape, 0) + i * b
                c = lax.broadcasted_iota(jnp.int32, g.shape, 1) + i * b
                same = jnp.zeros(g.shape, F32)
                for lo, hi in zip(edges[:-1], edges[1:]):
                    same = jnp.where((r >= lo) & (r < hi) & (c >= lo) & (c < hi), 1.0, same)
                g = g * same
            one = inv[:, i * b : n]
            a = g * (one * one)
            self.acc[self.at(i), i * b : n] = a
            self.put(i, a, self.ah, self.al)

    def apply(self):
        for i in range(self.blocks):
            tail = slice(i * self.nbk, self.n)
            a2 = mul3(self.ah[self.at(i), :], self.al[self.at(i), :], self.ah[:, tail], self.al[:, tail])
            r = lax.broadcasted_iota(jnp.int32, a2.shape, 0)
            c = lax.broadcasted_iota(jnp.int32, a2.shape, 1)
            q = jnp.where(r == c, NS_A, 0.0) + (NS_B * self.acc[self.at(i), tail] + NS_C * a2)
            self.put(i, q, self.qh, self.ql)
        h, l = halves(self.xs[...])
        self.xs[...] = mul3(h, l, self.qh[...], self.ql[...])

    def advance(self):
        for src, dst in (((self.ah, self.al), (self.th, self.tl)), ((self.th, self.tl), (self.ah, self.al))):
            for i in range(self.blocks):
                tail = slice(i * self.nbk, self.n)
                a = mul3(src[0][self.at(i), :], src[1][self.at(i), :], self.qh[:, tail], self.ql[:, tail])
                if dst[0] is self.ah:
                    self.acc[self.at(i), tail] = a
                self.put(i, a, *dst)


def unpack_gram(buf, n):
    b = n // 3
    return [buf[0:b, :], buf[b : 2 * b, 0 : 2 * b], buf[b : 2 * b, 2 * b : n]]


def make_muon(D, rows, XW, R, pack, full):
    top = 2 * (D // 3)

    def muon(buf, um, ua, xm_o, xa_o, *refs):
        p = Polar(D, D // 3, (D,), refs[:8])
        s = Polar(LANES, LANES, (XW, XW + R), refs[8:16])
        small = jnp.concatenate(
            [
                buf[top : top + min(pack, LANES - k * pack), k * LANES : (k + 1) * LANES]
                for k in range(-(-LANES // pack))
            ],
            axis=0,
        )
        p.start(unpack_gram(buf, D), jnp.concatenate([um[...], ua[...]], axis=0))
        s.start([small], jnp.concatenate([um[rows:, 0:LANES], ua[rows:, 0:LANES]], axis=0))

        def step(k, c):
            p.apply()
            s.apply()
            p.advance()
            s.advance()
            return c

        lax.fori_loop(0, 4, step, 0)
        p.apply()
        s.apply()
        xm_o[...] = p.xs[0 : 2 * rows, :]
        xa_o[0:rows, :] = p.xs[2 * rows : 3 * rows, :]
        xa_o[rows : 2 * rows, :] = p.xs[3 * rows : 4 * rows, :]
        return s

    def body(place, buf, um, ua, xm_o, xa_o, *refs):
        s = muon(buf, um, ua, xm_o, xa_o, *refs)

        @pl.when((place[1] & 1) == 1)
        def _():
            xm_o[rows : 2 * rows, 0:LANES] = s.xs[0:rows, :]
            xa_o[rows : 2 * rows, 0:LANES] = s.xs[rows : 2 * rows, :]

    body.__name__ = "muon"
    scratch = Polar.scratch(D, 4 * rows) + Polar.scratch(LANES, 2 * rows)
    return call(body, [((2 * rows, D), F32)] * 2, 4, 1, scratch)


def make_finish(rows, D, XW, R, rates):
    def finish(place, xm, xr, wi, wx, wd, wo, oi, ox, od, oo):
        even = (place[1] & 1) == 0
        for q in range(2):
            at = slice(q * rows, (q + 1) * rows)
            oi[:, q, :] = wi[:, q, :] - rates[0] * jnp.where(even, xm[at], xr[at])
        oo[...] = wo[...] - rates[3] * jnp.where(even, xr[0:rows], xm[0:rows])
        s = jnp.where(even, xr[rows:, 0:LANES], xm[rows:, 0:LANES])
        ox[...] = wx[...] - rates[1] * s[:, 0:XW]
        od[...] = wd[...] - rates[2] * s[:, XW : XW + R]

    outs = [((rows, 2, D), F32), ((rows, XW), F32), ((rows, R), F32), ((rows, D), F32)]
    return call(finish, outs, 7, 1)


def make_pack(rows, D, XW, R):
    def pack(wi, wx, wd, wo, a_o, r_o):
        a_o[...] = wi[:, 0, :].astype(BF)
        r_o[:, 0:D] = wi[:, 1, :].astype(BF)
        r_o[:, D : D + LANES] = jnp.concatenate([wx[...], wd[...]], axis=1).astype(BF)
        r_o[:, D + LANES : 2 * D + LANES] = wo[...].astype(BF)

    return call(pack, [((rows, D), BF), ((rows, 2 * D + LANES), BF)], 4, 0)


def shifted(value, axis, by):
    devices = lax.axis_size(axis)
    pairs = [(i, i + by) for i in range(devices) if 0 <= i + by < devices]
    return lax.ppermute(value, axis, pairs)


def swap(value, axis, bit):
    devices = lax.axis_size(axis)
    return lax.ppermute(value, axis, [(i, i ^ bit) for i in range(devices)])


def side(axis, bit):
    return jnp.where((lax.axis_index(axis) & bit) != 0, 1, 0)


def in_order(mine, theirs, axis, bit):
    low = side(axis, bit) == 0
    return jnp.concatenate([jnp.where(low, mine, theirs), jnp.where(low, theirs, mine)], axis=0)


def half_sum(value, axis, bit):
    half = value.shape[0] // 2
    mine = side(axis, bit) * half
    away = lax.dynamic_slice_in_dim(value, half - mine, half)
    kept = lax.dynamic_slice_in_dim(value, mine, half)
    return kept + swap(away, axis, bit)


def half_join(value, axis, bit):
    return in_order(value, swap(value, axis, bit), axis, bit)


def bits_of(axis):
    count = lax.axis_size(axis)
    return [1 << k for k in range(count.bit_length() - 1)]


def sum_rest(value):
    cols = value.shape[1] // 2
    done = []
    for k in range(2):
        part = value[:, k * cols : (k + 1) * cols]
        cut = [("tp", 2), ("fsdp", 1), ("ctx", 1)] if k == 0 else [("fsdp", 1), ("tp", 2), ("ctx", 1)]
        rest = [(a, b) for a in ("tp", "fsdp", "ctx") for b in bits_of(a) if (a, b) not in cut + [("tp", 1)]]
        for axis, bit in cut:
            part = half_sum(part, axis, bit)
        for axis, bit in rest:
            part = part + swap(part, axis, bit)
        for axis, bit in cut[::-1]:
            part = half_join(part, axis, bit)
        done.append(part)
    return jnp.concatenate(done, axis=1)


def to_owners(grads, rows):
    steps = [("fsdp", b) for b in bits_of("fsdp")[::-1]] + [("ctx", b) for b in bits_of("ctx")]
    value = grads
    for axis, bit in steps:
        if axis == "fsdp":
            value = value.reshape(1, 2, value.shape[0] // 2, value.shape[1])
        else:
            value = value.reshape(value.shape[0] // (2 * rows), 2, rows, value.shape[1])
        mine = side(axis, bit)
        away = lax.dynamic_slice_in_dim(value, 1 - mine, 1, 1).astype(BF)
        kept = lax.dynamic_slice_in_dim(value, mine, 1, 1)
        value = kept.astype(F32) + swap(away, axis, bit).astype(F32)
        value = value.reshape(-1, value.shape[3])
    return value


def over_ctx(value):
    count = lax.axis_size("ctx")
    rows = value.shape[0] // count
    parts = [value[d * rows : (d + 1) * rows] for d in range(count)]
    return jnp.concatenate([parts[0]] + [swap(parts[d], "ctx", d) for d in range(1, count)], axis=0)


def doubled(value, axes):
    steps = [(a, b) for a in axes for b in bits_of(a)]
    for axis, bit in steps[:-1]:
        value = jnp.concatenate([value, swap(value, axis, bit)], axis=0)
    return value, swap(value, *steps[-1])


def adam_update(parameters, gradient, moment_one, moment_two, adam_step):
    count = adam_step[0].astype(jnp.float32)
    first_new = BETA_ONE * moment_one + (1.0 - BETA_ONE) * gradient
    second_new = BETA_TWO * moment_two + (1.0 - BETA_TWO) * gradient * gradient
    first_hat = first_new / (1.0 - jnp.power(jnp.float32(BETA_ONE), count))
    second_hat = second_new / (1.0 - jnp.power(jnp.float32(BETA_TWO), count))
    updated = parameters - ADAM_RATE * (
        first_hat / (jnp.sqrt(second_hat) + ADAM_EPS) + DECAY_RATE * parameters
    )
    return (updated, first_new, second_new)


def on_device(
    block_input,
    cotangent,
    route_perm,
    doc_lengths,
    norm_gain,
    in_proj,
    conv_weight,
    conv_bias,
    x_proj,
    dt_proj,
    dt_bias,
    a_log,
    skip_gain,
    out_proj,
    in_momentum,
    x_momentum,
    dt_momentum,
    out_momentum,
    adam_first,
    adam_second,
    adam_step,
):
    ctx_count = lax.axis_size("ctx")
    fsdp_count = lax.axis_size("fsdp")
    tp_count = lax.axis_size("tp")
    owners = fsdp_count * ctx_count
    ctx_index = lax.axis_index("ctx")
    tp_index = lax.axis_index("tp")
    tokens, width = block_input.shape
    stream = tokens * ctx_count
    quarter = tokens // tp_count
    own_rows = in_proj.shape[0]
    channels = own_rows * owners
    inner = conv_bias.shape[0]
    states = a_log.shape[0]
    rank = dt_proj.shape[1]
    xw = x_proj.shape[1]
    lengths = doc_lengths[0]
    docs = lengths.shape[0]
    offsets = jnp.cumsum(lengths) - lengths
    scal = jnp.concatenate(
        [(tp_index * channels)[None], offsets - ctx_index * tokens, ctx_index[None], lax.axis_index("fsdp")[None]]
    ).astype(jnp.int32)
    place = jnp.stack([ctx_index, tp_index]).astype(jnp.int32)
    perm_row = (route_perm % stream).reshape(1, stream)
    gain_row = norm_gain.reshape(1, width)

    w_a, w_r = make_pack(own_rows, width, xw, rank)(in_proj, x_proj, dt_proj, out_proj)
    send, send_pos = make_send(tokens, width, ctx_count, tp_count)(place, perm_row, block_input, cotangent)
    own = over_ctx(send)
    swapped = own_rows % 16 == 0
    if swapped:
        parts_in = doubled(w_a, ("fsdp", "ctx"))
        parts_rest = doubled(w_r, ("ctx", "fsdp"))
    else:
        half = channels // 2
        full_in, full_rest = [lax.all_gather(w, ("fsdp", "ctx"), axis=0, tiled=True) for w in (w_a, w_r)]
        parts_in = (full_in[:half], full_in[half:])
        parts_rest = (full_rest[:half], full_rest[half:])
    route, fin = make_plan(tokens, ctx_count, tp_count)(place, perm_row, send_pos)
    far = swap(own, "tp", 2)
    stream_x, stream_dy, normed = make_recv(tokens, width, tp_count)(
        route, gain_row, own, swap(own, "tp", 1), far, swap(far, "tp", 1)
    )

    halo = shifted(normed[tokens - 8 :], "ctx", 1)
    w_in, w_rest, conv_in, gate_in, conv_act, conv_out, pt_part, d_gated, w_turn, x_halo = make_front(
        tokens, channels, width, docs, xw, rank, ctx_count, fsdp_count, swapped
    )(scal, normed, halo, stream_dy, *parts_in, *parts_rest, conv_weight, conv_bias.reshape(1, inner))
    pt_pair = pt_part + swap(pt_part, "tp", 1)
    pt, dec, drv, d_inner, pre, ends = make_carry(
        tokens, channels, docs, xw, rank, states, ctx_count
    )(scal, pt_pair, swap(pt_pair, "tp", 2), conv_act, gate_in, d_gated, w_turn, dt_bias.reshape(1, inner), a_log)
    ends = [swap(ends[d], "ctx", d) for d in range(1, ctx_count)]
    gate_low, d_gate, du_one, d_pre_low, dp_part, mix_part, grads_one, part_dt, vec_part = make_scan(
        tokens, channels, width, docs, xw, rank, states, ctx_count
    )(
        scal, pt, dec, drv, d_inner, pre, conv_act, gate_in, d_gated, stream_dy, normed, w_rest, w_turn, a_log,
        skip_gain.reshape(1, inner), *ends,
    )

    got_one = to_owners(grads_one, own_rows)
    dp_pair = dp_part + swap(dp_part, "tp", 1)
    d_conv_in, spill, grads_two, vec_chan = make_back(tokens, channels, width, docs, xw, rank)(8 + states)(
        scal, dp_pair, swap(dp_pair, "tp", 2), du_one, conv_out, conv_act, conv_in, x_halo, w_turn, conv_weight,
        vec_part, part_dt, normed, halo,
    )
    got_two = to_owners(grads_two, own_rows)
    keep, away, g_gain = make_last(tokens, channels, width, quarter)(
        d_conv_in, shifted(spill, "ctx", -1), d_gate, w_in, w_rest, mix_part, stream_x, route
    )

    near = swap(away, "tp", 1)
    cross = (keep[quarter:].astype(F32) + near[quarter:].astype(F32)).astype(BF)
    back = make_norm_back(quarter, width)(keep, near, swap(cross, "tp", 2), own, gain_row)[0]
    home = over_ctx(back)
    home_far = swap(home, "tp", 2)
    block_out, input_grad = make_final(tokens, width, tp_count)(
        fin, home, swap(home, "tp", 1), home_far, swap(home_far, "tp", 1)
    )

    kinds = 8 + states
    pack = 24
    vec_wide = lax.dynamic_update_slice(jnp.zeros((kinds, inner), F32), vec_chan, (0, tp_index * channels))
    vec_wide = vec_wide + jnp.pad(g_gain, ((7, kinds - 8), (0, inner - width)))
    vec_rows = kinds * inner // width
    g_one, g_out, mom_out, upd_out, gram_out = make_gram_out(own_rows, width)(got_one, out_momentum)
    top = 2 * (width // 3)
    full = -(-(top + max(vec_rows, pack)) // 64) * 64
    g_in, mom_in, g_x, mom_x, g_dt, mom_dt, gram_mine, gram_away, upd_mine, upd_away = make_gram_in(
        own_rows, width, xw, rank, vec_rows, pack, full
    )(place, got_two, g_one, in_momentum, x_momentum, dt_momentum, vec_wide.reshape(vec_rows, width), gram_out, upd_out)
    gram = sum_rest(gram_mine + swap(gram_away, "tp", 1))
    x_mine, x_away = make_muon(width, own_rows, xw, rank, pack, full)(place, gram, upd_mine, swap(upd_away, "tp", 1))
    rates = [MUON_RATE * 0.2 * math.sqrt(max(a, b)) for a, b in ((2 * inner, width), (inner, xw), (inner, rank), (inner, width))]
    new_in, new_x, new_dt, new_out = make_finish(own_rows, width, xw, rank, rates)(
        place, x_mine, swap(x_away, "tp", 1), in_proj, x_proj, dt_proj, out_proj
    )
    vec_own = gram[top : top + vec_rows]
    vec_sum = jnp.where((tp_index & 1) == 0, vec_own, swap(vec_own, "tp", 1)).reshape(kinds, inner)
    g_alog = vec_sum[8:]
    vec_grads = jnp.concatenate(
        [vec_sum[7, :width], vec_sum[0:4].reshape(-1), vec_sum[4], vec_sum[5], g_alog.reshape(-1), vec_sum[6]]
    )
    vec_params = jnp.concatenate(
        [norm_gain, conv_weight.reshape(-1), conv_bias, dt_bias, a_log.reshape(-1), skip_gain]
    )
    new_vec, first_new, second_new = adam_update(vec_params, vec_grads, adam_first, adam_second, adam_step)
    cut_b = width + 4 * inner
    cut_c = cut_b + inner
    cut_d = cut_c + inner
    cut_e = cut_d + states * inner
    return (
        block_out,
        input_grad,
        vec_sum[7, :width],
        g_in,
        vec_sum[0:4],
        vec_sum[4],
        g_x,
        g_dt,
        vec_sum[5],
        g_alog,
        vec_sum[6],
        g_out,
        new_vec[:width],
        new_in,
        new_vec[width:cut_b].reshape(4, inner),
        new_vec[cut_b:cut_c],
        new_x,
        new_dt,
        new_vec[cut_c:cut_d],
        new_vec[cut_d:cut_e].reshape(states, inner),
        new_vec[cut_e:],
        new_out,
        mom_in,
        mom_x,
        mom_dt,
        mom_out,
        first_new,
        second_new,
    )


def solution(mesh):
    return jax.shard_map(
        on_device,
        mesh=mesh,
        in_specs=(
            P(("fsdp", "ctx"), None),
            P(("fsdp", "ctx"), None),
            P("fsdp"),
            P("fsdp", None),
            P(),
            P(("tp", "fsdp", "ctx"), None, None),
            P(),
            P(),
            P(("tp", "fsdp", "ctx"), None),
            P(("tp", "fsdp", "ctx"), None),
            P(),
            P(),
            P(),
            P(("tp", "fsdp", "ctx"), None),
            P(("tp", "fsdp", "ctx"), None, None),
            P(("tp", "fsdp", "ctx"), None),
            P(("tp", "fsdp", "ctx"), None),
            P(("tp", "fsdp", "ctx"), None),
            P(),
            P(),
            P(),
        ),
        out_specs=(
            P(("fsdp", "ctx"), None),
            P(("fsdp", "ctx"), None),
            P(),
            P(("tp", "fsdp", "ctx"), None, None),
            P(),
            P(),
            P(("tp", "fsdp", "ctx"), None),
            P(("tp", "fsdp", "ctx"), None),
            P(),
            P(),
            P(),
            P(("tp", "fsdp", "ctx"), None),
            P(),
            P(("tp", "fsdp", "ctx"), None, None),
            P(),
            P(),
            P(("tp", "fsdp", "ctx"), None),
            P(("tp", "fsdp", "ctx"), None),
            P(),
            P(),
            P(),
            P(("tp", "fsdp", "ctx"), None),
            P(("tp", "fsdp", "ctx"), None, None),
            P(("tp", "fsdp", "ctx"), None),
            P(("tp", "fsdp", "ctx"), None),
            P(("tp", "fsdp", "ctx"), None),
            P(),
            P(),
        ),
        check_vma=False,
    )
```

```python
import math

import jax
import jax.numpy as jnp
from jax import lax
from jax.experimental import pallas as pl
from jax.experimental.pallas import tpu as pltpu
from jax.sharding import PartitionSpec as P

F32 = jnp.float32
BF = jnp.bfloat16
LANES = 128
RESET = 1e5
LOG2E = 1.4426950408889634
VMEM_LIMIT = 60 * 1024 * 1024
NS_A = 3.4445
NS_B = -4.775
NS_C = 2.0315
MOMENTUM = 0.95
MUON_RATE = 0.1
ADAM_RATE = 0.25
BETA_ONE = 0.9
BETA_TWO = 0.95
ADAM_EPS = 1e-08
DECAY_RATE = 0.01
NORM_EPS = 1e-05


def dot_nn(a, b):
    return lax.dot_general(a, b, (((1,), (0,)), ((), ())), preferred_element_type=F32)


def dot_nt(a, b):
    return lax.dot_general(a, b, (((1,), (1,)), ((), ())), preferred_element_type=F32)


def dot_tn(a, b):
    return lax.dot_general(a, b, (((0,), (0,)), ((), ())), preferred_element_type=F32)


def soft(x):
    return jnp.maximum(x, 0.0) + jnp.log1p(jnp.exp(-jnp.abs(x)))


def slope_of(a, s):
    return s * (1.0 + a * (1.0 - s))


def call(body, outs, n_in, n_smem, scratch=(), flops=10**9):
    specs = [pl.BlockSpec(memory_space=pltpu.SMEM)] * n_smem + [
        pl.BlockSpec(memory_space=pltpu.VMEM)
    ] * (n_in - n_smem)
    return pl.pallas_call(
        body,
        out_shape=[jax.ShapeDtypeStruct(s, d) for s, d in outs],
        in_specs=specs,
        out_specs=[pl.BlockSpec(memory_space=pltpu.VMEM)] * len(outs),
        scratch_shapes=list(scratch),
        compiler_params=pltpu.CompilerParams(vmem_limit_bytes=VMEM_LIMIT),
        name=body.__name__,
    )


def rows_iota(r0, rows):
    return lax.broadcasted_iota(jnp.int32, (rows, LANES), 0) + r0


def tap_mask(sc_ref, docs, p, shift):
    ok = jnp.ones(p.shape, F32)
    for j in range(docs):
        off = sc_ref[1 + j]
        ok = jnp.where((off <= p) & (p < off + shift), 0.0, ok)
    return ok


def wide(mask, width):
    return jnp.concatenate([mask] * (width // LANES), axis=1)


def make_front(T, C, D, docs, XW, R, CT, FS, swapped):
    RB = 64

    def front(sc, hb, halo, dy, a0, a1, r0, r1, cw, cb, wa, wr, xu_o, z_o, u_o, v_o, pt_o, dg_o, wt_o, xh_o, xpad):
        own = C // (CT * FS)
        if swapped:
            z, f = sc[1 + docs], sc[2 + docs]
            for pieces, out in (((a0, a1), wa), ((r0, r1), wr)):
                for e in range(CT * FS):
                    fe, ze = (e % FS, e // FS) if out is wa else (e // CT, e % CT)
                    at = pl.multiple_of(((f ^ fe) * CT + (z ^ ze)) * own, own)
                    k = e * own
                    half = C // 2
                    piece = pieces[k // half]
                    out[pl.ds(at, own), :] = piece[k % half : k % half + own, :]
        else:
            wa[0 : C // 2, :] = a0[...]
            wa[C // 2 : C, :] = a1[...]
            wr[0 : C // 2, :] = r0[...]
            wr[C // 2 : C, :] = r1[...]
        w0 = wa[...]
        w1 = wr[:, 0:D]
        wo = wr[:, D + LANES : 2 * D + LANES]
        wt = wr[:, D : D + LANES].astype(F32).T.astype(BF)
        wt_o[...] = wt
        c0 = pl.multiple_of(sc[0], LANES)
        xh = dot_nt(halo[...], w0).astype(BF).astype(F32)
        xpad[0:8, :] = xh
        xh_o[...] = xh
        xu = dot_nt(hb[...], w0).astype(BF)
        xu_o[...] = xu
        xpad[8 : 8 + T, :] = xu.astype(F32)
        z_o[...] = dot_nt(hb[...], w1).astype(BF)
        dg_o[...] = dot_nt(dy[...], wo)
        taps = [cw[k : k + 1, pl.ds(c0, C)] for k in range(4)]
        bias = cb[0:1, pl.ds(c0, C)]

        def block(i, carry):
            r0 = i * RB
            p = rows_iota(r0, RB)
            v = bias + jnp.zeros((RB, C), F32)
            full = xpad[pl.ds(r0, RB + 8), :]
            for k in range(4):
                s = 3 - k
                x = full[8 - s : 8 - s + RB]
                if s:
                    x = x * wide(tap_mask(sc, docs, p, s), C)
                v = v + taps[k] * x
            v_o[pl.ds(r0, RB), :] = v
            u_o[pl.ds(r0, RB), :] = (v / (1.0 + jnp.exp(-v))).astype(BF)
            return carry

        lax.fori_loop(0, T // RB, block, 0)
        pt_o[...] = dot_nt(wt[0:XW], u_o[...])

    outs = [((C, D), BF), ((C, 2 * D + LANES), BF)]
    outs += [((T, C), BF)] * 3 + [((T, C), F32), ((XW, T), F32), ((T, C), F32), ((LANES, C), BF), ((8, C), F32)]
    return call(front, outs, 10, 1, [pltpu.VMEM((T + 8, C), F32)])


CHUNK = 128


def at_lane(i, n):
    shape = (CHUNK, n, LANES)
    return lax.broadcasted_iota(jnp.int32, shape, 2) == lax.broadcasted_iota(jnp.int32, shape, 0) + i * CHUNK


def row_totals(hi, lo):
    rows = hi.shape[0] * hi.shape[1]
    both = jnp.concatenate([hi.reshape(rows, LANES).astype(BF), lo.reshape(rows, LANES).astype(BF)], axis=1)
    return dot_nn(both, jnp.ones((2 * LANES, LANES), BF)).reshape(hi.shape)


def lane_sums(ref):
    n = ref.shape[1]

    def chunk(i, tot):
        x = ref[pl.ds(i * CHUNK, CHUNK)]
        hi = x.astype(BF).astype(F32)
        return tot + jnp.sum(jnp.where(at_lane(i, n), row_totals(hi, x - hi), 0.0), axis=0)

    return lax.fori_loop(0, LANES // CHUNK, chunk, jnp.zeros((n, LANES), F32))


def spread(x, out, base):
    n = x.shape[0]
    hi = x.astype(BF).astype(F32)
    lo = x - hi

    def chunk(i, c):
        m = at_lane(i, n)
        out[pl.ds(base + i * CHUNK, CHUNK)] = row_totals(jnp.where(m, hi[None], 0.0), jnp.where(m, lo[None], 0.0))
        return c

    lax.fori_loop(0, LANES // CHUNK, chunk, 0)


def make_carry(T, C, docs, XW, R, N, CT):
    RB = 64
    LT = C // LANES

    def carry(sc, pa, pb, u, z, dg, wt, dtb, alog, pt_o, da_o, du_o, dyin_o, pre_o, ends_o, bs, cs):
        c0 = pl.multiple_of(sc[0], LANES)
        pt = pa[...] + pb[...]
        pt_o[...] = pt
        lin = dot_tn(pt[0:R].astype(BF), wt[XW : XW + R, :])
        pre_o[...] = lin + dtb[0:1, pl.ds(c0, C)]

        def block(i, tot):
            rs = pl.ds(i * RB, RB)
            p = rows_iota(i * RB, RB)
            keep = jnp.ones((RB, LANES), F32)
            for j in range(docs):
                keep = jnp.where(p == sc[1 + j], 0.0, keep)
            x = pre_o[rs, :]
            delta = soft(x)
            d = jnp.where(wide(keep, C) > 0.0, delta, RESET)
            r8 = pl.ds(i * (RB // 8), RB // 8)
            da_o[r8] = d.reshape(RB // 8, 8, C)
            du_o[r8] = (delta * u[rs, :].astype(F32)).reshape(RB // 8, 8, C)
            zf = z[rs, :].astype(F32)
            dyin_o[r8] = (dg[rs, :] * (zf / (1.0 + jnp.exp(-zf)))).reshape(RB // 8, 8, C)
            return tot + jnp.sum(d, axis=0, keepdims=True)

        tot = lax.fori_loop(0, T // RB, block, jnp.zeros((1, C), F32))
        am = [-jnp.exp(alog[:, pl.ds(c0 + l * LANES, LANES)]) for l in range(LT)]
        am2 = [a * LOG2E for a in am]

        def rows(ref, i, j):
            full = ref[i, pl.ds(j, N, stride=0), :]
            return [full[:, l * LANES : (l + 1) * LANES] for l in range(LT)]

        nb = T // LANES

        def outer(k, c):
            bt = pt_o[R_ : R_ + N, pl.ds(pl.multiple_of(k * LANES, LANES), LANES)]
            ct = pt_o[R_ + N : R_ + 2 * N, pl.ds(pl.multiple_of((nb - 1 - k) * LANES, LANES), LANES)]

            spread(bt, bs, 0)
            spread(ct, cs, 0)

            def inner(i, c):
                h, g = c
                h = list(h)
                g = list(g)
                fi = k * (LANES // 8) + i
                ri = T // 8 - 1 - fi
                for j in range(8):
                    bb = bs[i * 8 + j]
                    cc = cs[LANES - 1 - i * 8 - j]
                    df, uf = rows(da_o, fi, j), rows(du_o, fi, j)
                    db, yb = rows(da_o, ri, 7 - j), rows(dyin_o, ri, 7 - j)
                    for l in range(LT):
                        h[l] = jnp.exp2(df[l] * am2[l]) * h[l] + uf[l] * bb
                        g[l] = jnp.exp2(db[l] * am2[l]) * (g[l] + yb[l] * cc)
                return tuple(h), tuple(g)

            return lax.fori_loop(0, LANES // 8, inner, (c[0], c[1]))

        R_ = R
        zero = tuple(jnp.zeros((N, LANES), F32) for _ in range(LT))
        h, g = lax.fori_loop(0, nb, outer, (zero, zero))
        here = sc[1 + docs]
        for d in range(CT):
            for l in range(LT):
                ends_o[d, 0:N, l * LANES : (l + 1) * LANES] = jnp.where((here ^ d) > here, h[l], g[l])
            ends_o[d, N : N + 8, :] = jnp.broadcast_to(tot, (8, C))

    outs = [((XW, T), F32)] + [((T // 8, 8, C), F32)] * 3 + [((T, C), F32)] + [((CT, N + 8, C), F32)]
    return call(carry, outs, 9, 1, [pltpu.VMEM((LANES, N, LANES), F32)] * 2)


def make_scan(T, C, D, docs, XW, R, N, CT):
    RB = 64
    LT = C // LANES
    nb = T // LANES

    def scan(sc, pt, da, du, dyin, pre, u, z, dg, dy, hb, wr, wt, alog, skip, *rest):
        ends = rest[: CT - 1]
        (
            g_o, dz_o, du1_o, dpre_o, dp_o, mix_o, pw_o, pdt_o, vec_o,
            a_s, h_s, y_s, lb_s, dd_s, sb_s, sc_s, bs, cs,
        ) = rest[CT - 1 :]
        c0 = pl.multiple_of(sc[0], LANES)
        am = [-jnp.exp(alog[:, pl.ds(c0 + l * LANES, LANES)]) for l in range(LT)]
        am2 = [a * LOG2E for a in am]
        sl = [slice(l * LANES, (l + 1) * LANES) for l in range(LT)]
        top4 = lax.broadcasted_iota(jnp.int32, (8, LANES), 0) < 4

        def rows(ref, i, j):
            full = ref[i, pl.ds(j, N, stride=0), :]
            return [full[:, sl[l]] for l in range(LT)]

        here = sc[1 + docs]
        hin, gin = [], []
        for l in range(LT):
            for way, got in ((-1, hin), (1, gin)):
                near = jnp.zeros((N, LANES), F32)
                tot = jnp.zeros((1, LANES), F32)
                far = near
                for d in range(1, CT):
                    e = ends[d - 1]
                    near = jnp.where((here ^ d) == here + way, e[0:N, sl[l]], near)
                    tot = jnp.where((here ^ d) == here + way, e[N : N + 1, sl[l]], tot)
                    far = jnp.where((here ^ d) == here + 2 * way, e[0:N, sl[l]], far)
                got.append(near + jnp.exp2(jnp.broadcast_to(tot, (N, LANES)) * am2[l]) * far)
            h_s[0, :, sl[l]] = hin[l]

        def fouter(k, h):
            blk = pl.ds(pl.multiple_of(k * LANES, LANES), LANES)
            spread(pt[R : R + N, blk], bs, k * LANES)
            spread(pt[R + N : R + 2 * N, blk], cs, k * LANES)

            def inner(i, h):
                h = list(h)
                fi = k * (LANES // 8) + i
                for j in range(8):
                    t = fi * 8 + j
                    bb = bs[t]
                    cc = cs[t]
                    dr, ur = rows(da, fi, j), rows(du, fi, j)
                    for l in range(LT):
                        a = jnp.exp2(dr[l] * am2[l])
                        a_s[t, :, sl[l]] = a
                        h[l] = a * h[l] + ur[l] * bb
                        h_s[t + 1, :, sl[l]] = h[l]
                        y_s[fi, j : j + 1, sl[l]] = jnp.sum(h[l] * cc, axis=0, keepdims=True)
                return tuple(h)

            return lax.fori_loop(0, LANES // 8, inner, h)

        lax.fori_loop(0, nb, fouter, tuple(hin))

        def bouter(k, c):
            kb = nb - 1 - k
            blk = pl.ds(pl.multiple_of(kb * LANES, LANES), LANES)
            zero = jnp.zeros((N, LANES), F32)

            def inner(i, c):
                g, ga = c
                g = list(g)
                ga = list(ga)
                l0 = LANES - 1 - i * 8
                fi = kb * (LANES // 8) + LANES // 8 - 1 - i
                for j in range(8):
                    t = kb * LANES + l0 - j
                    jj = 7 - j
                    bb = bs[t]
                    cc = cs[t]
                    sb = zero
                    scc = zero
                    dr, ur, yr = rows(da, fi, jj), rows(du, fi, jj), rows(dyin, fi, jj)
                    for l in range(LT):
                        dyr = yr[l]
                        lam = cc * dyr + g[l]
                        g[l] = a_s[t, :, sl[l]] * lam
                        dal = g[l] * h_s[t, :, sl[l]]
                        pb = lam * bb
                        pd = dal * am[l]
                        pb = pb[0:8] + pb[8:16]
                        pd = pd[0:8] + pd[8:16]
                        both = jnp.where(top4, pb, pd) + pltpu.roll(jnp.where(top4, pd, pb), 4, 0)
                        both = both + pltpu.roll(both, 6, 0)
                        both = both + pltpu.roll(both, 7, 0)
                        lb_s[fi, jj : jj + 1, sl[l]] = both[0:1]
                        dd_s[fi, jj : jj + 1, sl[l]] = both[4:5]
                        ga[l] = ga[l] + dal * dr[l]
                        sb = sb + lam * ur[l]
                        scc = scc + dyr * h_s[t + 1, :, sl[l]]
                    sb_s[l0 - j] = sb
                    sc_s[l0 - j] = scc
                return tuple(g), tuple(ga)

            g, ga = lax.fori_loop(0, LANES // 8, inner, (c[0], c[1]))
            dp_o[R : R + N, blk] = lane_sums(sb_s)
            dp_o[R + N : R + 2 * N, blk] = lane_sums(sc_s)
            return g, ga

        zeros = tuple(jnp.zeros((N, LANES), F32) for _ in range(LT))
        _, ga = lax.fori_loop(0, nb, bouter, (tuple(gin), zeros))
        for l in range(LT):
            vec_o[8 : 8 + N, sl[l]] = am[l] * ga[l]
        skr = skip[0:1, pl.ds(c0, C)]

        def block(i, tot):
            gdt, gsk = tot
            rs = pl.ds(i * RB, RB)
            r8 = pl.ds(i * (RB // 8), RB // 8)
            uf = u[rs, :].astype(F32)
            zf = z[rs, :].astype(F32)
            s = 1.0 / (1.0 + jnp.exp(-zf))
            yin = y_s[r8].reshape(RB, C) + skr * uf
            g_o[rs, :] = (yin * (zf * s)).astype(BF)
            dz_o[rs, :] = (dg[rs, :] * yin * slope_of(zf, s)).astype(BF)
            lb = lb_s[r8].reshape(RB, C)
            dyr = dyin[r8].reshape(RB, C)
            x = pre[rs, :]
            dpre = (lb * uf + dd_s[r8].reshape(RB, C)) / (1.0 + jnp.exp(-x))
            dpre_o[rs, :] = dpre.astype(BF)
            du1_o[rs, :] = dyr * skr + lb * soft(x)
            return gdt + jnp.sum(dpre, axis=0, keepdims=True), gsk + jnp.sum(dyr * uf, axis=0, keepdims=True)

        z1 = jnp.zeros((1, C), F32)
        gdt, gsk = lax.fori_loop(0, T // RB, block, (z1, z1))
        vec_o[5:6, :] = gdt
        vec_o[6:7, :] = gsk
        vec_o[7:8, :] = z1
        vec_o[0:5, :] = jnp.zeros((5, C), F32)
        dp_o[0:R, :] = dot_nt(wt[XW : XW + R, :], dpre_o[...])
        pdt_o[...] = dot_nn(pt[0:R, :].astype(BF), dpre_o[...])
        mix_o[...] = dot_nn(g_o[...], wr[:, D + LANES : 2 * D + LANES]).astype(BF)
        pw_o[:, 0:D] = dot_tn(dz_o[...], hb[...]).astype(BF)
        pw_o[:, D : 2 * D] = dot_tn(g_o[...], dy[...]).astype(BF)

    outs = [((T, C), BF), ((T, C), BF), ((T, C), F32), ((T, C), BF), ((XW, T), F32), ((T, D), BF),
            ((C, 2 * D), BF), ((R, C), F32), ((8 + N, C), F32)]
    scratch = [pltpu.VMEM((T, N, C), F32), pltpu.VMEM((T + 1, N, C), F32)] + [pltpu.VMEM((T // 8, 8, C), F32)] * 3
    scratch += [pltpu.VMEM((LANES, N, LANES), F32)] * 2 + [pltpu.VMEM((T, N, LANES), F32)] * 2
    return call(scan, outs, 14 + CT, 1, scratch)


def make_back(T, C, D, docs, XW, R):
    RB = 64

    def back(sc, da_, db_, du1, v, u, xu, xhalo, wt, cw, vec, pdt, hb, halo, dxu_o, spill_o, pxt_o, vec_o, pad1, pad2, pad3, xpad):
        c0 = pl.multiple_of(sc[0], LANES)
        dpl = (da_[...] + db_[...]).astype(BF)
        pxt_o[:, D : D + LANES] = jnp.concatenate([dot_nn(dpl, u[...]), pdt[...]], axis=0).T.astype(BF)
        dxu_o[...] = du1[...] + dot_tn(dpl, wt[0:XW, :])
        pads = {1: pad1, 2: pad2, 3: pad3}
        xpad[0:8, :] = xhalo[...]
        xpad[8 : 8 + T, :] = xu[...].astype(F32)
        taps = [cw[k : k + 1, pl.ds(c0, C)] for k in range(4)]
        z8 = jnp.zeros((8, C), F32)
        for s in (1, 2, 3):
            pads[s][0:8, :] = z8
            pads[s][8 + T : 16 + T, :] = z8

        def block(i, tot):
            r0 = i * RB
            rs = pl.ds(r0, RB)
            p = rows_iota(r0, RB)
            vf = v[rs, :]
            sg = 1.0 / (1.0 + jnp.exp(-vf))
            dv = dxu_o[rs, :] * slope_of(vf, sg)
            new = [None] * 5
            full = xpad[pl.ds(r0, RB + 8), :]
            new[4] = tot[4] + jnp.sum(dv, axis=0, keepdims=True)
            for k in range(4):
                s = 3 - k
                x = full[8 - s : 8 - s + RB]
                m = dv
                if s:
                    m = dv * wide(tap_mask(sc, docs, p, s), C)
                    pads[s][pl.ds(8 + r0, RB), :] = taps[k] * m
                else:
                    dxu_o[rs, :] = taps[k] * m
                new[k] = tot[k] + jnp.sum(m * x, axis=0, keepdims=True)
            return tuple(new)

        z1 = jnp.zeros((1, C), F32)
        tot = lax.fori_loop(0, T // RB, block, (z1,) * 5)
        vec_o[...] = vec[...]
        for k in range(5):
            vec_o[k : k + 1, :] = tot[k]

        def gather(i, c):
            r0 = i * RB
            rs = pl.ds(r0, RB)
            acc = dxu_o[rs, :]
            for s in (1, 2, 3):
                acc = acc + pads[s][pl.ds(8 + r0, RB + 8), :][s : s + RB]
            dxu_o[rs, :] = acc
            return c

        lax.fori_loop(0, T // RB, gather, 0)
        acc = z8
        for s in (1, 2, 3):
            acc = acc + pads[s][s : s + 8, :]
        spill_o[...] = acc
        own = dot_tn(dxu_o[...].astype(BF), hb[...])
        pxt_o[:, 0:D] = (own + dot_tn(acc.astype(BF), halo[...])).astype(BF)

    outs = [((T, C), F32), ((8, C), F32), ((C, D + LANES), BF), (None, F32)]

    def build(vrows):
        o = outs[:3] + [((vrows, C), F32)]
        return call(back, o, 14, 1, [pltpu.VMEM((T + 16, C), F32)] * 3 + [pltpu.VMEM((T + 8, C), F32)])

    return build


def make_last(T, C, D, Q):
    def last(dxu, spill, dz, wa, wr, mix, x, rt, keep_o, send_o, gain_o):
        low = jnp.concatenate([jnp.zeros((T - 8, C), F32), spill[...]], axis=0)
        dx = (dxu[...] + low).astype(BF)
        dn = dot_nn(dx, wa[...]) + dot_nn(dz[...], wr[:, 0:D])
        xf = x[...].astype(F32)
        inv = lax.rsqrt(jnp.mean(xf * xf, axis=1, keepdims=True) + NORM_EPS)
        gain_o[...] = jnp.sum(dn * xf * inv, axis=0, keepdims=True)
        dnl = dn.astype(BF)
        for e in range(T // Q):
            r = rt[:, e * Q : (e + 1) * Q]
            o = send_o if e % 2 else keep_o
            at = slice((e // 2) * Q, (e // 2 + 1) * Q)
            o[at, 0:D] = dot_tn(r, mix[...]).astype(BF)
            o[at, D : 2 * D] = dot_tn(r, dnl).astype(BF)

    half = T // 2
    outs = [((half, 2 * D), BF), ((half, 2 * D), BF), ((1, D), F32)]
    return call(last, outs, 8, 0)


def flat_slots(k, shift, share, first, here):
    return ((k >> shift) ^ here) * share + first + (k & ((1 << shift) - 1))


def chunk_shape(T, CT, TP):
    share = T // CT
    SR = share // TP
    shift = SR.bit_length() - 1
    assert SR == 1 << shift and T // TP == CT * SR
    return T // TP, share, SR, shift


def make_send(T, D, CT, TP):
    Q, share, SR, shift = chunk_shape(T, CT, TP)

    def send(rsc, perm, x, dy, buf_o, pos_o):
        c = rsc[0]
        tp = rsc[1]
        own = perm[0:1, pl.ds(pl.multiple_of(c * T, LANES), T)].astype(F32)
        r = lax.broadcasted_iota(jnp.int32, (T, T), 0)
        q = lax.broadcasted_iota(jnp.int32, (T, T), 1)
        row = jnp.broadcast_to(own, (T, T))
        col = jnp.broadcast_to(jnp.sum(jnp.where(r == q, row, 0.0), axis=1, keepdims=True), (T, T))
        pos_row = jnp.sum(jnp.where(col < row, 1.0, 0.0), axis=0, keepdims=True)
        k = lax.broadcasted_iota(jnp.int32, (Q, T), 0)
        slot = flat_slots(k, shift, share, SR * tp, c).astype(F32)
        pick = jnp.where(slot == pos_row, 1.0, 0.0).astype(BF)
        buf_o[:, 0:D] = dot_nn(pick, x[...]).astype(BF)
        buf_o[:, D : 2 * D] = dot_nn(pick, dy[...]).astype(BF)
        pos_o[...] = pos_row

    return call(send, [((Q, 2 * D), BF), ((1, T), F32)], 4, 1)


def make_plan(T, CT, TP):
    Q, share, SR, shift = chunk_shape(T, CT, TP)

    def plan(rsc, perm, pos, rt_o, fin_o):
        c = rsc[0]
        tp = rsc[1]
        r = lax.broadcasted_iota(jnp.int32, (T, T), 0)
        q = lax.broadcasted_iota(jnp.int32, (T, T), 1)
        place = r + c * T
        lane = lax.broadcasted_iota(jnp.int32, (T, LANES), 1)
        hot = jnp.zeros((T, LANES), F32)
        for s in range(CT):
            src = jnp.broadcast_to(perm[0:1, s * T : (s + 1) * T], (T, T))
            n = jnp.sum(jnp.where(src == place, 1.0, 0.0), axis=1, keepdims=True)
            hot = jnp.where(lane == s, n, hot)
        below = jnp.where(q < r, 1.0, 0.0).astype(BF)
        count = dot_nn(below, hot.astype(BF))
        rank = jnp.sum(hot * count, axis=1, keepdims=True)
        block = jnp.sum(hot * lane.astype(F32), axis=1, keepdims=True)
        want = block * share + rank
        back = jnp.sum(jnp.where(r == q, jnp.broadcast_to(pos[...], (T, T)), 0.0), axis=1, keepdims=True)
        f = lax.broadcasted_iota(jnp.int32, (T, Q), 1)
        for e in range(TP):
            slot = flat_slots(f, shift, share, SR * (tp ^ e), c).astype(F32)
            rt_o[:, e * Q : (e + 1) * Q] = jnp.where(slot == want, 1.0, 0.0).astype(BF)
            fin_o[:, e * Q : (e + 1) * Q] = jnp.where(slot == back, 1.0, 0.0).astype(BF)

    return call(plan, [((T, T), BF)] * 2, 3, 1)


def make_recv(T, D, TP):
    Q = T // TP

    def recv(rt, gain, *rest):
        parts = rest[:TP]
        x_o, dy_o, hb_o = rest[TP:]
        xa = jnp.zeros((T, D), F32)
        ya = jnp.zeros((T, D), F32)
        for e in range(TP):
            m = rt[:, e * Q : (e + 1) * Q]
            xa = xa + dot_nn(m, parts[e][:, 0:D])
            ya = ya + dot_nn(m, parts[e][:, D : 2 * D])
        x_o[...] = xa.astype(BF)
        dy_o[...] = ya.astype(BF)
        inv = lax.rsqrt(jnp.mean(xa * xa, axis=1, keepdims=True) + NORM_EPS)
        hb_o[...] = (xa * inv * gain[...]).astype(BF)

    return call(recv, [((T, D), BF)] * 3, 2 + TP, 0)


def make_norm_back(Q, D):
    def norm_back(keep, got, far, own, gain, o):
        both = keep[0:Q].astype(F32) + got[0:Q].astype(F32) + far[...].astype(F32)
        xf = own[:, 0:D].astype(F32)
        inv = lax.rsqrt(jnp.mean(xf * xf, axis=1, keepdims=True) + NORM_EPS)
        dn = both[:, D : 2 * D]
        scaled = gain[...] * dn
        mean = jnp.mean(scaled * xf, axis=1, keepdims=True)
        o[:, 0:D] = (xf + both[:, 0:D]).astype(BF)
        o[:, D : 2 * D] = (
            own[:, D : 2 * D].astype(F32) + inv * scaled - xf * (inv * inv * inv) * mean
        ).astype(BF)

    return call(norm_back, [((Q, 2 * D), BF)], 5, 0)


def make_final(T, D, TP):
    Q = T // TP

    def final(fin, *rest):
        out_o, grad_o = rest[TP:]
        a = jnp.zeros((T, D), F32)
        b = jnp.zeros((T, D), F32)
        for e in range(TP):
            m = fin[:, e * Q : (e + 1) * Q]
            a = a + dot_nn(m, rest[e][:, 0:D])
            b = b + dot_nn(m, rest[e][:, D : 2 * D])
        out_o[...] = a.astype(BF)
        grad_o[...] = b.astype(BF)

    return call(final, [((T, D), BF)] * 2, 1 + TP, 0)


def halves(x):
    hi = x.astype(BF)
    return hi, (x - hi.astype(F32)).astype(BF)


def mul3(ah, al, bh, bl):
    return dot_nn(ah, bh) + (dot_nn(ah, bl) + dot_nn(al, bh))


def gram3(parts):
    def rows_of(i, b, n):
        at = slice(i * b, (i + 1) * b)
        tail = slice(i * b, n)
        tot = None
        for h, l in parts:
            one = dot_tn(h[:, at], h[:, tail]) + (dot_tn(h[:, at], l[:, tail]) + dot_tn(l[:, at], h[:, tail]))
            tot = one if tot is None else tot + one
        return tot

    return rows_of


def put_gram(o, parts, n):
    b = n // 3
    rows_of = gram3(parts)
    o[0:b, :] = rows_of(0, b, n)
    o[b : 2 * b, 0 : 2 * b] = rows_of(1, b, n)
    o[b : 2 * b, 2 * b : n] = rows_of(2, b, n)


def momentum_step(gradient, momentum_old):
    momentum_new = MOMENTUM * momentum_old + gradient
    return (momentum_new, gradient + MOMENTUM * momentum_new)


def make_gram_out(rows, D):
    def gram_out(got, mom, g1_o, go_o, mo_o, uo_o, gram_o):
        g1_o[...] = got[:, 0:D]
        g = got[:, D : 2 * D]
        m, u = momentum_step(g, mom[...])
        go_o[...] = g
        mo_o[...] = m
        uo_o[...] = u
        put_gram(gram_o, [halves(u)], D)

    outs = [((rows, D), F32)] * 4 + [((2 * D // 3, D), F32)]
    return call(gram_out, outs, 2, 0)


def make_gram_in(rows, D, XW, R, VR, pack, full):
    b = D // 3
    top = 2 * b

    def gram_in(place, got, g1, mom, xm, dm, vec, go, uo, gi_o, mi_o, gx_o, mx_o, gd_o, md_o, mine_o, away_o, um_o, ua_o, tmp):
        even = (place[1] & 1) == 0
        parts = []
        us = []
        for q in range(2):
            g = got[:, 0:D] if q == 0 else g1[...]
            m, u = momentum_step(g, mom[:, q, :])
            gi_o[:, q, :] = g
            mi_o[:, q, :] = m
            us.append(u)
            parts.append(halves(u))
        put_gram(tmp, parts, D)
        g = got[:, D : D + LANES]
        m, u = momentum_step(g, jnp.concatenate([xm[...], dm[...]], axis=1))
        gx_o[...] = g[:, 0:XW]
        gd_o[...] = g[:, XW : XW + R]
        mx_o[...] = m[:, 0:XW]
        md_o[...] = m[:, XW : XW + R]
        h, l = halves(u)
        small = dot_tn(h, h) + (dot_tn(h, l) + dot_tn(l, h))

        def put_in(buf, ub):
            buf[0:top, :] = tmp[...]
            buf[top : top + VR, :] = vec[...]
            if full > top + VR:
                buf[top + VR : full, :] = jnp.zeros((full - top - VR, D), F32)
            ub[0:rows, :] = us[0]
            ub[rows : 2 * rows, :] = us[1]

        def put_out(buf, ub):
            buf[0:top, :] = go[...]
            buf[top:full, :] = jnp.zeros((full - top, D), F32)
            for k in range(-(-LANES // pack)):
                lo = k * pack
                hi = min(lo + pack, LANES)
                buf[top : top + hi - lo, k * LANES : (k + 1) * LANES] = small[lo:hi]
            ub[0:rows, :] = uo[...]
            ub[rows : 2 * rows, :] = jnp.zeros((rows, D), F32)
            ub[rows : 2 * rows, 0:LANES] = u

        @pl.when(even)
        def _():
            put_in(mine_o, um_o)
            put_out(away_o, ua_o)

        @pl.when(jnp.logical_not(even))
        def _():
            put_out(mine_o, um_o)
            put_in(away_o, ua_o)

    outs = [((rows, 2, D), F32)] * 2
    outs += [((rows, XW), F32)] * 2 + [((rows, R), F32)] * 2 + [((full, D), F32)] * 2 + [((2 * rows, D), F32)] * 2
    return call(gram_in, outs, 9, 1, [pltpu.VMEM((top, D), F32)])


class Polar:
    def __init__(self, n, nbk, cuts, refs):
        self.n, self.nbk, self.cuts = n, nbk, list(cuts)
        self.blocks = n // nbk
        self.ah, self.al, self.qh, self.ql, self.th, self.tl, self.xs, self.acc = refs

    @staticmethod
    def scratch(n, rows):
        return [pltpu.VMEM((n, n), BF)] * 6 + [pltpu.VMEM((rows, n), F32), pltpu.VMEM((n, n), F32)]

    def at(self, b):
        return slice(b * self.nbk, (b + 1) * self.nbk)

    def put(self, i, value, hi_ref, lo_ref):
        h, l = halves(value)
        b = self.nbk
        hi_ref[self.at(i), i * b : self.n] = h
        lo_ref[self.at(i), i * b : self.n] = l
        for j in range(i + 1, self.blocks):
            h, l = halves(value[:, (j - i) * b : (j - i + 1) * b].T)
            hi_ref[self.at(j), self.at(i)] = h
            lo_ref[self.at(j), self.at(i)] = l

    def start(self, tails, upd):
        n, b = self.n, self.nbk
        col = lax.broadcasted_iota(jnp.int32, (1, n), 1)
        edges = [0] + self.cuts
        inv = jnp.zeros((1, n), F32)
        r = lax.broadcasted_iota(jnp.int32, (b, b), 0)
        c = lax.broadcasted_iota(jnp.int32, (b, b), 1)
        for lo, hi in zip(edges[:-1], edges[1:]):
            tot = jnp.zeros((1, 1), F32)
            for k in range(self.blocks):
                inside = (r == c) & (r + k * b >= lo) & (r + k * b < hi)
                d = jnp.sum(jnp.where(inside, tails[k][:, 0:b], 0.0), axis=1, keepdims=True)
                tot = tot + jnp.sum(d, axis=0, keepdims=True)
            inv = jnp.where((col >= lo) & (col < hi), 1.0 / (jnp.sqrt(tot) + 1e-07), inv)
        self.xs[...] = upd * inv
        for i in range(self.blocks):
            g = tails[i]
            if len(self.cuts) > 1:
                r = lax.broadcasted_iota(jnp.int32, g.shape, 0) + i * b
                c = lax.broadcasted_iota(jnp.int32, g.shape, 1) + i * b
                same = jnp.zeros(g.shape, F32)
                for lo, hi in zip(edges[:-1], edges[1:]):
                    same = jnp.where((r >= lo) & (r < hi) & (c >= lo) & (c < hi), 1.0, same)
                g = g * same
            one = inv[:, i * b : n]
            a = g * (one * one)
            self.acc[self.at(i), i * b : n] = a
            self.put(i, a, self.ah, self.al)

    def apply(self):
        for i in range(self.blocks):
            tail = slice(i * self.nbk, self.n)
            a2 = mul3(self.ah[self.at(i), :], self.al[self.at(i), :], self.ah[:, tail], self.al[:, tail])
            r = lax.broadcasted_iota(jnp.int32, a2.shape, 0)
            c = lax.broadcasted_iota(jnp.int32, a2.shape, 1)
            q = jnp.where(r == c, NS_A, 0.0) + (NS_B * self.acc[self.at(i), tail] + NS_C * a2)
            self.put(i, q, self.qh, self.ql)
        h, l = halves(self.xs[...])
        self.xs[...] = mul3(h, l, self.qh[...], self.ql[...])

    def advance(self):
        for src, dst in (((self.ah, self.al), (self.th, self.tl)), ((self.th, self.tl), (self.ah, self.al))):
            for i in range(self.blocks):
                tail = slice(i * self.nbk, self.n)
                a = mul3(src[0][self.at(i), :], src[1][self.at(i), :], self.qh[:, tail], self.ql[:, tail])
                if dst[0] is self.ah:
                    self.acc[self.at(i), tail] = a
                self.put(i, a, *dst)


def unpack_gram(buf, n):
    b = n // 3
    return [buf[0:b, :], buf[b : 2 * b, 0 : 2 * b], buf[b : 2 * b, 2 * b : n]]


def make_muon(D, rows, XW, R, pack, full):
    top = 2 * (D // 3)

    def muon(buf, um, ua, xm_o, xa_o, *refs):
        p = Polar(D, D // 3, (D,), refs[:8])
        s = Polar(LANES, LANES, (XW, XW + R), refs[8:16])
        small = jnp.concatenate(
            [
                buf[top : top + min(pack, LANES - k * pack), k * LANES : (k + 1) * LANES]
                for k in range(-(-LANES // pack))
            ],
            axis=0,
        )
        p.start(unpack_gram(buf, D), jnp.concatenate([um[...], ua[...]], axis=0))
        s.start([small], jnp.concatenate([um[rows:, 0:LANES], ua[rows:, 0:LANES]], axis=0))

        def step(k, c):
            p.apply()
            s.apply()
            p.advance()
            s.advance()
            return c

        lax.fori_loop(0, 4, step, 0)
        p.apply()
        s.apply()
        xm_o[...] = p.xs[0 : 2 * rows, :]
        xa_o[0:rows, :] = p.xs[2 * rows : 3 * rows, :]
        xa_o[rows : 2 * rows, :] = p.xs[3 * rows : 4 * rows, :]
        return s

    def body(place, buf, um, ua, xm_o, xa_o, *refs):
        s = muon(buf, um, ua, xm_o, xa_o, *refs)

        @pl.when((place[1] & 1) == 1)
        def _():
            xm_o[rows : 2 * rows, 0:LANES] = s.xs[0:rows, :]
            xa_o[rows : 2 * rows, 0:LANES] = s.xs[rows : 2 * rows, :]

    body.__name__ = "muon"
    scratch = Polar.scratch(D, 4 * rows) + Polar.scratch(LANES, 2 * rows)
    return call(body, [((2 * rows, D), F32)] * 2, 4, 1, scratch)


def make_finish(rows, D, XW, R, rates):
    def finish(place, xm, xr, wi, wx, wd, wo, oi, ox, od, oo):
        even = (place[1] & 1) == 0
        for q in range(2):
            at = slice(q * rows, (q + 1) * rows)
            oi[:, q, :] = wi[:, q, :] - rates[0] * jnp.where(even, xm[at], xr[at])
        oo[...] = wo[...] - rates[3] * jnp.where(even, xr[0:rows], xm[0:rows])
        s = jnp.where(even, xr[rows:, 0:LANES], xm[rows:, 0:LANES])
        ox[...] = wx[...] - rates[1] * s[:, 0:XW]
        od[...] = wd[...] - rates[2] * s[:, XW : XW + R]

    outs = [((rows, 2, D), F32), ((rows, XW), F32), ((rows, R), F32), ((rows, D), F32)]
    return call(finish, outs, 7, 1)


def make_pack(rows, D, XW, R):
    def pack(wi, wx, wd, wo, a_o, r_o):
        a_o[...] = wi[:, 0, :].astype(BF)
        r_o[:, 0:D] = wi[:, 1, :].astype(BF)
        r_o[:, D : D + LANES] = jnp.concatenate([wx[...], wd[...]], axis=1).astype(BF)
        r_o[:, D + LANES : 2 * D + LANES] = wo[...].astype(BF)

    return call(pack, [((rows, D), BF), ((rows, 2 * D + LANES), BF)], 4, 0)


def shifted(value, axis, by):
    devices = lax.axis_size(axis)
    pairs = [(i, i + by) for i in range(devices) if 0 <= i + by < devices]
    return lax.ppermute(value, axis, pairs)


def swap(value, axis, bit):
    devices = lax.axis_size(axis)
    return lax.ppermute(value, axis, [(i, i ^ bit) for i in range(devices)])


def side(axis, bit):
    return jnp.where((lax.axis_index(axis) & bit) != 0, 1, 0)


def in_order(mine, theirs, axis, bit):
    low = side(axis, bit) == 0
    return jnp.concatenate([jnp.where(low, mine, theirs), jnp.where(low, theirs, mine)], axis=0)


def half_sum(value, axis, bit):
    half = value.shape[0] // 2
    mine = side(axis, bit) * half
    away = lax.dynamic_slice_in_dim(value, half - mine, half)
    kept = lax.dynamic_slice_in_dim(value, mine, half)
    return kept + swap(away, axis, bit)


def half_join(value, axis, bit):
    return in_order(value, swap(value, axis, bit), axis, bit)


def bits_of(axis):
    count = lax.axis_size(axis)
    return [1 << k for k in range(count.bit_length() - 1)]


def sum_rest(value):
    cols = value.shape[1] // 2
    done = []
    for k in range(2):
        part = value[:, k * cols : (k + 1) * cols]
        cut = [("tp", 2), ("fsdp", 1), ("ctx", 1)] if k == 0 else [("fsdp", 1), ("tp", 2), ("ctx", 1)]
        rest = [(a, b) for a in ("tp", "fsdp", "ctx") for b in bits_of(a) if (a, b) not in cut + [("tp", 1)]]
        for axis, bit in cut:
            part = half_sum(part, axis, bit)
        for axis, bit in rest:
            part = part + swap(part, axis, bit)
        for axis, bit in cut[::-1]:
            part = half_join(part, axis, bit)
        done.append(part)
    return jnp.concatenate(done, axis=1)


def to_owners(value, rows, axes=("fsdp", "ctx")):
    steps = [(a, b) for a in axes for b in bits_of(a)[:: -1 if a == "fsdp" else 1]]
    for axis, bit in steps:
        if axis == "fsdp":
            value = value.reshape(1, 2, value.shape[0] // 2, value.shape[1])
        else:
            value = value.reshape(value.shape[0] // (2 * rows), 2, rows, value.shape[1])
        mine = side(axis, bit)
        away = lax.dynamic_slice_in_dim(value, 1 - mine, 1, 1).astype(BF)
        kept = lax.dynamic_slice_in_dim(value, mine, 1, 1)
        value = kept.astype(F32) + swap(away, axis, bit).astype(F32)
        value = value.reshape(-1, value.shape[3])
    return value


def over_ctx(value):
    count = lax.axis_size("ctx")
    rows = value.shape[0] // count
    parts = [value[d * rows : (d + 1) * rows] for d in range(count)]
    return jnp.concatenate([parts[0]] + [swap(parts[d], "ctx", d) for d in range(1, count)], axis=0)


def doubled(value, axes):
    steps = [(a, b) for a in axes for b in bits_of(a)]
    for axis, bit in steps[:-1]:
        value = jnp.concatenate([value, swap(value, axis, bit)], axis=0)
    return value, swap(value, *steps[-1])


def adam_update(parameters, gradient, moment_one, moment_two, adam_step):
    count = adam_step[0].astype(jnp.float32)
    first_new = BETA_ONE * moment_one + (1.0 - BETA_ONE) * gradient
    second_new = BETA_TWO * moment_two + (1.0 - BETA_TWO) * gradient * gradient
    first_hat = first_new / (1.0 - jnp.power(jnp.float32(BETA_ONE), count))
    second_hat = second_new / (1.0 - jnp.power(jnp.float32(BETA_TWO), count))
    updated = parameters - ADAM_RATE * (
        first_hat / (jnp.sqrt(second_hat) + ADAM_EPS) + DECAY_RATE * parameters
    )
    return (updated, first_new, second_new)


def on_device(
    block_input,
    cotangent,
    route_perm,
    doc_lengths,
    norm_gain,
    in_proj,
    conv_weight,
    conv_bias,
    x_proj,
    dt_proj,
    dt_bias,
    a_log,
    skip_gain,
    out_proj,
    in_momentum,
    x_momentum,
    dt_momentum,
    out_momentum,
    adam_first,
    adam_second,
    adam_step,
):
    ctx_count = lax.axis_size("ctx")
    fsdp_count = lax.axis_size("fsdp")
    tp_count = lax.axis_size("tp")
    owners = fsdp_count * ctx_count
    ctx_index = lax.axis_index("ctx")
    tp_index = lax.axis_index("tp")
    tokens, width = block_input.shape
    stream = tokens * ctx_count
    quarter = tokens // tp_count
    own_rows = in_proj.shape[0]
    channels = own_rows * owners
    inner = conv_bias.shape[0]
    states = a_log.shape[0]
    rank = dt_proj.shape[1]
    xw = x_proj.shape[1]
    lengths = doc_lengths[0]
    docs = lengths.shape[0]
    offsets = jnp.cumsum(lengths) - lengths
    scal = jnp.concatenate(
        [(tp_index * channels)[None], offsets - ctx_index * tokens, ctx_index[None], lax.axis_index("fsdp")[None]]
    ).astype(jnp.int32)
    place = jnp.stack([ctx_index, tp_index]).astype(jnp.int32)
    perm_row = (route_perm % stream).reshape(1, stream)
    gain_row = norm_gain.reshape(1, width)

    w_a, w_r = make_pack(own_rows, width, xw, rank)(in_proj, x_proj, dt_proj, out_proj)
    send, send_pos = make_send(tokens, width, ctx_count, tp_count)(place, perm_row, block_input, cotangent)
    own = over_ctx(send)
    swapped = own_rows % 16 == 0
    if swapped:
        parts_in = doubled(w_a, ("fsdp", "ctx"))
        parts_rest = doubled(w_r, ("ctx", "fsdp"))
    else:
        half = channels // 2
        full_in, full_rest = [lax.all_gather(w, ("fsdp", "ctx"), axis=0, tiled=True) for w in (w_a, w_r)]
        parts_in = (full_in[:half], full_in[half:])
        parts_rest = (full_rest[:half], full_rest[half:])
    route, fin = make_plan(tokens, ctx_count, tp_count)(place, perm_row, send_pos)
    far = swap(own, "tp", 2)
    stream_x, stream_dy, normed = make_recv(tokens, width, tp_count)(
        route, gain_row, own, swap(own, "tp", 1), far, swap(far, "tp", 1)
    )

    halo = shifted(normed[tokens - 8 :], "ctx", 1)
    w_in, w_rest, conv_in, gate_in, conv_act, conv_out, pt_part, d_gated, w_turn, x_halo = make_front(
        tokens, channels, width, docs, xw, rank, ctx_count, fsdp_count, swapped
    )(scal, normed, halo, stream_dy, *parts_in, *parts_rest, conv_weight, conv_bias.reshape(1, inner))
    pt_pair = pt_part + swap(pt_part, "tp", 1)
    pt, dec, drv, d_inner, pre, ends = make_carry(
        tokens, channels, docs, xw, rank, states, ctx_count
    )(scal, pt_pair, swap(pt_pair, "tp", 2), conv_act, gate_in, d_gated, w_turn, dt_bias.reshape(1, inner), a_log)
    ends = [swap(ends[d], "ctx", d) for d in range(1, ctx_count)]
    gate_low, d_gate, du_one, d_pre_low, dp_part, mix_part, grads_one, part_dt, vec_part = make_scan(
        tokens, channels, width, docs, xw, rank, states, ctx_count
    )(
        scal, pt, dec, drv, d_inner, pre, conv_act, gate_in, d_gated, stream_dy, normed, w_rest, w_turn, a_log,
        skip_gain.reshape(1, inner), *ends,
    )

    got_one = to_owners(grads_one, own_rows)
    dp_pair = dp_part + swap(dp_part, "tp", 1)
    d_conv_in, spill, grads_two, vec_chan = make_back(tokens, channels, width, docs, xw, rank)(8 + states)(
        scal, dp_pair, swap(dp_pair, "tp", 2), du_one, conv_out, conv_act, conv_in, x_halo, w_turn, conv_weight,
        vec_part, part_dt, normed, halo,
    )
    two = to_owners(grads_two, own_rows, ("fsdp",))
    keep, away, g_gain = make_last(tokens, channels, width, quarter)(
        d_conv_in, shifted(spill, "ctx", -1), d_gate, w_in, w_rest, mix_part, stream_x, route
    )

    near = swap(away, "tp", 1)
    cross = (keep[quarter:].astype(F32) + near[quarter:].astype(F32)).astype(BF)
    two, cross = lax.optimization_barrier((two, cross))
    got_two = to_owners(two, own_rows, ("ctx",))
    back = make_norm_back(quarter, width)(keep, near, swap(cross, "tp", 2), own, gain_row)[0]
    got_two, back = lax.optimization_barrier((got_two, back))
    home = over_ctx(back)
    home_far = swap(home, "tp", 2)
    block_out, input_grad = make_final(tokens, width, tp_count)(
        fin, home, swap(home, "tp", 1), home_far, swap(home_far, "tp", 1)
    )

    kinds = 8 + states
    pack = 24
    vec_wide = lax.dynamic_update_slice(jnp.zeros((kinds, inner), F32), vec_chan, (0, tp_index * channels))
    vec_wide = vec_wide + jnp.pad(g_gain, ((7, kinds - 8), (0, inner - width)))
    vec_rows = kinds * inner // width
    g_one, g_out, mom_out, upd_out, gram_out = make_gram_out(own_rows, width)(got_one, out_momentum)
    top = 2 * (width // 3)
    full = -(-(top + max(vec_rows, pack)) // 64) * 64
    g_in, mom_in, g_x, mom_x, g_dt, mom_dt, gram_mine, gram_away, upd_mine, upd_away = make_gram_in(
        own_rows, width, xw, rank, vec_rows, pack, full
    )(place, got_two, g_one, in_momentum, x_momentum, dt_momentum, vec_wide.reshape(vec_rows, width), gram_out, upd_out)
    gram = sum_rest(gram_mine + swap(gram_away, "tp", 1))
    x_mine, x_away = make_muon(width, own_rows, xw, rank, pack, full)(place, gram, upd_mine, swap(upd_away, "tp", 1))
    rates = [MUON_RATE * 0.2 * math.sqrt(max(a, b)) for a, b in ((2 * inner, width), (inner, xw), (inner, rank), (inner, width))]
    new_in, new_x, new_dt, new_out = make_finish(own_rows, width, xw, rank, rates)(
        place, x_mine, swap(x_away, "tp", 1), in_proj, x_proj, dt_proj, out_proj
    )
    vec_own = gram[top : top + vec_rows]
    vec_sum = jnp.where((tp_index & 1) == 0, vec_own, swap(vec_own, "tp", 1)).reshape(kinds, inner)
    g_alog = vec_sum[8:]
    vec_grads = jnp.concatenate(
        [vec_sum[7, :width], vec_sum[0:4].reshape(-1), vec_sum[4], vec_sum[5], g_alog.reshape(-1), vec_sum[6]]
    )
    vec_params = jnp.concatenate(
        [norm_gain, conv_weight.reshape(-1), conv_bias, dt_bias, a_log.reshape(-1), skip_gain]
    )
    new_vec, first_new, second_new = adam_update(vec_params, vec_grads, adam_first, adam_second, adam_step)
    cut_b = width + 4 * inner
    cut_c = cut_b + inner
    cut_d = cut_c + inner
    cut_e = cut_d + states * inner
    return (
        block_out,
        input_grad,
        vec_sum[7, :width],
        g_in,
        vec_sum[0:4],
        vec_sum[4],
        g_x,
        g_dt,
        vec_sum[5],
        g_alog,
        vec_sum[6],
        g_out,
        new_vec[:width],
        new_in,
        new_vec[width:cut_b].reshape(4, inner),
        new_vec[cut_b:cut_c],
        new_x,
        new_dt,
        new_vec[cut_c:cut_d],
        new_vec[cut_d:cut_e].reshape(states, inner),
        new_vec[cut_e:],
        new_out,
        mom_in,
        mom_x,
        mom_dt,
        mom_out,
        first_new,
        second_new,
    )


def solution(mesh):
    return jax.shard_map(
        on_device,
        mesh=mesh,
        in_specs=(
            P(("fsdp", "ctx"), None),
            P(("fsdp", "ctx"), None),
            P("fsdp"),
            P("fsdp", None),
            P(),
            P(("tp", "fsdp", "ctx"), None, None),
            P(),
            P(),
            P(("tp", "fsdp", "ctx"), None),
            P(("tp", "fsdp", "ctx"), None),
            P(),
            P(),
            P(),
            P(("tp", "fsdp", "ctx"), None),
            P(("tp", "fsdp", "ctx"), None, None),
            P(("tp", "fsdp", "ctx"), None),
            P(("tp", "fsdp", "ctx"), None),
            P(("tp", "fsdp", "ctx"), None),
            P(),
            P(),
            P(),
        ),
        out_specs=(
            P(("fsdp", "ctx"), None),
            P(("fsdp", "ctx"), None),
            P(),
            P(("tp", "fsdp", "ctx"), None, None),
            P(),
            P(),
            P(("tp", "fsdp", "ctx"), None),
            P(("tp", "fsdp", "ctx"), None),
            P(),
            P(),
            P(),
            P(("tp", "fsdp", "ctx"), None),
            P(),
            P(("tp", "fsdp", "ctx"), None, None),
            P(),
            P(),
            P(("tp", "fsdp", "ctx"), None),
            P(("tp", "fsdp", "ctx"), None),
            P(),
            P(),
            P(),
            P(("tp", "fsdp", "ctx"), None),
            P(("tp", "fsdp", "ctx"), None, None),
            P(("tp", "fsdp", "ctx"), None),
            P(("tp", "fsdp", "ctx"), None),
            P(("tp", "fsdp", "ctx"), None),
            P(),
            P(),
        ),
        check_vma=False,
    )
```

```python
import math

import jax
import jax.numpy as jnp
from jax import lax
from jax.experimental import pallas as pl
from jax.experimental.pallas import tpu as pltpu
from jax.sharding import PartitionSpec as P

F32 = jnp.float32
BF = jnp.bfloat16
LANES = 128
RESET = 1e5
LOG2E = 1.4426950408889634
VMEM_LIMIT = 60 * 1024 * 1024
NS_A = 3.4445
NS_B = -4.775
NS_C = 2.0315
MOMENTUM = 0.95
MUON_RATE = 0.1
ADAM_RATE = 0.25
BETA_ONE = 0.9
BETA_TWO = 0.95
ADAM_EPS = 1e-08
DECAY_RATE = 0.01
NORM_EPS = 1e-05


def dot_nn(a, b):
    return lax.dot_general(a, b, (((1,), (0,)), ((), ())), preferred_element_type=F32)


def dot_nt(a, b):
    return lax.dot_general(a, b, (((1,), (1,)), ((), ())), preferred_element_type=F32)


def dot_tn(a, b):
    return lax.dot_general(a, b, (((0,), (0,)), ((), ())), preferred_element_type=F32)


def soft(x):
    return jnp.maximum(x, 0.0) + jnp.log1p(jnp.exp(-jnp.abs(x)))


def slope_of(a, s):
    return s * (1.0 + a * (1.0 - s))


def call(body, outs, n_in, n_smem, scratch=(), flops=10**9):
    specs = [pl.BlockSpec(memory_space=pltpu.SMEM)] * n_smem + [
        pl.BlockSpec(memory_space=pltpu.VMEM)
    ] * (n_in - n_smem)
    return pl.pallas_call(
        body,
        out_shape=[jax.ShapeDtypeStruct(s, d) for s, d in outs],
        in_specs=specs,
        out_specs=[pl.BlockSpec(memory_space=pltpu.VMEM)] * len(outs),
        scratch_shapes=list(scratch),
        compiler_params=pltpu.CompilerParams(vmem_limit_bytes=VMEM_LIMIT),
        name=body.__name__,
    )


def rows_iota(r0, rows):
    return lax.broadcasted_iota(jnp.int32, (rows, LANES), 0) + r0


def tap_mask(sc_ref, docs, p, shift):
    ok = jnp.ones(p.shape, F32)
    for j in range(docs):
        off = sc_ref[1 + j]
        ok = jnp.where((off <= p) & (p < off + shift), 0.0, ok)
    return ok


def wide(mask, width):
    return jnp.concatenate([mask] * (width // LANES), axis=1)


def make_front(T, C, D, docs, XW, R, CT, FS, swapped):
    RB = 64

    def front(sc, hb, halo, dy, a0, a1, r0, r1, cw, cb, wa, wr, xu_o, z_o, u_o, v_o, pt_o, dg_o, wt_o, xh_o, xpad):
        own = C // (CT * FS)
        if swapped:
            z, f = sc[1 + docs], sc[2 + docs]
            for pieces, out in (((a0, a1), wa), ((r0, r1), wr)):
                for e in range(CT * FS):
                    fe, ze = (e % FS, e // FS) if out is wa else (e // CT, e % CT)
                    at = pl.multiple_of(((f ^ fe) * CT + (z ^ ze)) * own, own)
                    k = e * own
                    half = C // 2
                    piece = pieces[k // half]
                    out[pl.ds(at, own), :] = piece[k % half : k % half + own, :]
        else:
            wa[0 : C // 2, :] = a0[...]
            wa[C // 2 : C, :] = a1[...]
            wr[0 : C // 2, :] = r0[...]
            wr[C // 2 : C, :] = r1[...]
        w0 = wa[...]
        w1 = wr[:, 0:D]
        wo = wr[:, D + LANES : 2 * D + LANES]
        wt = wr[:, D : D + LANES].astype(F32).T.astype(BF)
        wt_o[...] = wt
        c0 = pl.multiple_of(sc[0], LANES)
        xh = dot_nt(halo[...], w0).astype(BF).astype(F32)
        xpad[0:8, :] = xh
        xh_o[...] = xh
        xu = dot_nt(hb[...], w0).astype(BF)
        xu_o[...] = xu
        xpad[8 : 8 + T, :] = xu.astype(F32)
        z_o[...] = dot_nt(hb[...], w1).astype(BF)
        dg_o[...] = dot_nt(dy[...], wo)
        taps = [cw[k : k + 1, pl.ds(c0, C)] for k in range(4)]
        bias = cb[0:1, pl.ds(c0, C)]

        def block(i, carry):
            r0 = i * RB
            p = rows_iota(r0, RB)
            v = bias + jnp.zeros((RB, C), F32)
            full = xpad[pl.ds(r0, RB + 8), :]
            for k in range(4):
                s = 3 - k
                x = full[8 - s : 8 - s + RB]
                if s:
                    x = x * wide(tap_mask(sc, docs, p, s), C)
                v = v + taps[k] * x
            v_o[pl.ds(r0, RB), :] = v
            u_o[pl.ds(r0, RB), :] = (v / (1.0 + jnp.exp(-v))).astype(BF)
            return carry

        lax.fori_loop(0, T // RB, block, 0)
        pt_o[...] = dot_nt(wt[0:XW], u_o[...])

    outs = [((C, D), BF), ((C, 2 * D + LANES), BF)]
    outs += [((T, C), BF)] * 3 + [((T, C), F32), ((XW, T), F32), ((T, C), F32), ((LANES, C), BF), ((8, C), F32)]
    return call(front, outs, 10, 1, [pltpu.VMEM((T + 8, C), F32)])


CHUNK = 128


def at_lane(i, n):
    shape = (CHUNK, n, LANES)
    return lax.broadcasted_iota(jnp.int32, shape, 2) == lax.broadcasted_iota(jnp.int32, shape, 0) + i * CHUNK


def row_totals(hi, lo):
    rows = hi.shape[0] * hi.shape[1]
    both = jnp.concatenate([hi.reshape(rows, LANES).astype(BF), lo.reshape(rows, LANES).astype(BF)], axis=1)
    return dot_nn(both, jnp.ones((2 * LANES, LANES), BF)).reshape(hi.shape)


def lane_sums(ref):
    n = ref.shape[1]

    def chunk(i, tot):
        x = ref[pl.ds(i * CHUNK, CHUNK)]
        hi = x.astype(BF).astype(F32)
        return tot + jnp.sum(jnp.where(at_lane(i, n), row_totals(hi, x - hi), 0.0), axis=0)

    return lax.fori_loop(0, LANES // CHUNK, chunk, jnp.zeros((n, LANES), F32))


def spread(x, out, base):
    n = x.shape[0]
    hi = x.astype(BF).astype(F32)
    lo = x - hi

    def chunk(i, c):
        m = at_lane(i, n)
        out[pl.ds(base + i * CHUNK, CHUNK)] = row_totals(jnp.where(m, hi[None], 0.0), jnp.where(m, lo[None], 0.0))
        return c

    lax.fori_loop(0, LANES // CHUNK, chunk, 0)


def make_carry(T, C, docs, XW, R, N, CT):
    RB = 64
    LT = C // LANES

    def carry(sc, pa, pb, u, z, dg, wt, dtb, alog, pt_o, da_o, du_o, dyin_o, pre_o, ends_o, bs, cs):
        c0 = pl.multiple_of(sc[0], LANES)
        pt = pa[...] + pb[...]
        pt_o[...] = pt
        lin = dot_tn(pt[0:R].astype(BF), wt[XW : XW + R, :])
        pre_o[...] = lin + dtb[0:1, pl.ds(c0, C)]

        def block(i, tot):
            rs = pl.ds(i * RB, RB)
            p = rows_iota(i * RB, RB)
            keep = jnp.ones((RB, LANES), F32)
            for j in range(docs):
                keep = jnp.where(p == sc[1 + j], 0.0, keep)
            x = pre_o[rs, :]
            delta = soft(x)
            d = jnp.where(wide(keep, C) > 0.0, delta, RESET)
            r8 = pl.ds(i * (RB // 8), RB // 8)
            da_o[r8] = d.reshape(RB // 8, 8, C)
            du_o[r8] = (delta * u[rs, :].astype(F32)).reshape(RB // 8, 8, C)
            zf = z[rs, :].astype(F32)
            dyin_o[r8] = (dg[rs, :] * (zf / (1.0 + jnp.exp(-zf)))).reshape(RB // 8, 8, C)
            return tot + jnp.sum(d, axis=0, keepdims=True)

        tot = lax.fori_loop(0, T // RB, block, jnp.zeros((1, C), F32))
        am = [-jnp.exp(alog[:, pl.ds(c0 + l * LANES, LANES)]) for l in range(LT)]
        am2 = [a * LOG2E for a in am]

        def rows(ref, i, j):
            full = ref[i, pl.ds(j, N, stride=0), :]
            return [full[:, l * LANES : (l + 1) * LANES] for l in range(LT)]

        nb = T // LANES

        def outer(k, c):
            bt = pt_o[R_ : R_ + N, pl.ds(pl.multiple_of(k * LANES, LANES), LANES)]
            ct = pt_o[R_ + N : R_ + 2 * N, pl.ds(pl.multiple_of((nb - 1 - k) * LANES, LANES), LANES)]

            spread(bt, bs, 0)
            spread(ct, cs, 0)

            def inner(i, c):
                h, g = c
                h = list(h)
                g = list(g)
                fi = k * (LANES // 8) + i
                ri = T // 8 - 1 - fi
                for j in range(8):
                    bb = bs[i * 8 + j]
                    cc = cs[LANES - 1 - i * 8 - j]
                    df, uf = rows(da_o, fi, j), rows(du_o, fi, j)
                    db, yb = rows(da_o, ri, 7 - j), rows(dyin_o, ri, 7 - j)
                    for l in range(LT):
                        h[l] = jnp.exp2(df[l] * am2[l]) * h[l] + uf[l] * bb
                        g[l] = jnp.exp2(db[l] * am2[l]) * (g[l] + yb[l] * cc)
                return tuple(h), tuple(g)

            return lax.fori_loop(0, LANES // 8, inner, (c[0], c[1]))

        R_ = R
        zero = tuple(jnp.zeros((N, LANES), F32) for _ in range(LT))
        h, g = lax.fori_loop(0, nb, outer, (zero, zero))
        here = sc[1 + docs]
        for d in range(CT):
            for l in range(LT):
                ends_o[d, 0:N, l * LANES : (l + 1) * LANES] = jnp.where((here ^ d) > here, h[l], g[l])
            ends_o[d, N : N + 8, :] = jnp.broadcast_to(tot, (8, C))

    outs = [((XW, T), F32)] + [((T // 8, 8, C), F32)] * 3 + [((T, C), F32)] + [((CT, N + 8, C), F32)]
    return call(carry, outs, 9, 1, [pltpu.VMEM((LANES, N, LANES), F32)] * 2)


def make_scan(T, C, D, docs, XW, R, N, CT):
    RB = 64
    LT = C // LANES
    nb = T // LANES

    def scan(sc, pt, da, du, dyin, pre, u, z, dg, dy, hb, wr, wt, alog, skip, *rest):
        ends = rest[: CT - 1]
        (
            g_o, dz_o, du1_o, dpre_o, dp_o, mix_o, pw_o, pdt_o, vec_o,
            a_s, h_s, y_s, lb_s, dd_s, sb_s, sc_s, bs, cs,
        ) = rest[CT - 1 :]
        c0 = pl.multiple_of(sc[0], LANES)
        am = [-jnp.exp(alog[:, pl.ds(c0 + l * LANES, LANES)]) for l in range(LT)]
        am2 = [a * LOG2E for a in am]
        sl = [slice(l * LANES, (l + 1) * LANES) for l in range(LT)]
        top4 = lax.broadcasted_iota(jnp.int32, (8, LANES), 0) < 4

        def rows(ref, i, j):
            full = ref[i, pl.ds(j, N, stride=0), :]
            return [full[:, sl[l]] for l in range(LT)]

        here = sc[1 + docs]
        hin, gin = [], []
        for l in range(LT):
            for way, got in ((-1, hin), (1, gin)):
                near = jnp.zeros((N, LANES), F32)
                tot = jnp.zeros((1, LANES), F32)
                far = near
                for d in range(1, CT):
                    e = ends[d - 1]
                    near = jnp.where((here ^ d) == here + way, e[0:N, sl[l]], near)
                    tot = jnp.where((here ^ d) == here + way, e[N : N + 1, sl[l]], tot)
                    far = jnp.where((here ^ d) == here + 2 * way, e[0:N, sl[l]], far)
                got.append(near + jnp.exp2(jnp.broadcast_to(tot, (N, LANES)) * am2[l]) * far)
            h_s[0, :, sl[l]] = hin[l]

        def fouter(k, h):
            blk = pl.ds(pl.multiple_of(k * LANES, LANES), LANES)
            spread(pt[R : R + N, blk], bs, k * LANES)
            spread(pt[R + N : R + 2 * N, blk], cs, k * LANES)

            def inner(i, h):
                h = list(h)
                fi = k * (LANES // 8) + i
                for j in range(8):
                    t = fi * 8 + j
                    bb = bs[t]
                    cc = cs[t]
                    dr, ur = rows(da, fi, j), rows(du, fi, j)
                    for l in range(LT):
                        a = jnp.exp2(dr[l] * am2[l])
                        a_s[t, :, sl[l]] = a
                        h[l] = a * h[l] + ur[l] * bb
                        h_s[t + 1, :, sl[l]] = h[l]
                        y_s[fi, j : j + 1, sl[l]] = jnp.sum(h[l] * cc, axis=0, keepdims=True)
                return tuple(h)

            return lax.fori_loop(0, LANES // 8, inner, h)

        lax.fori_loop(0, nb, fouter, tuple(hin))

        def bouter(k, c):
            kb = nb - 1 - k
            blk = pl.ds(pl.multiple_of(kb * LANES, LANES), LANES)
            zero = jnp.zeros((N, LANES), F32)

            def inner(i, c):
                g, ga = c
                g = list(g)
                ga = list(ga)
                l0 = LANES - 1 - i * 8
                fi = kb * (LANES // 8) + LANES // 8 - 1 - i
                for j in range(8):
                    t = kb * LANES + l0 - j
                    jj = 7 - j
                    bb = bs[t]
                    cc = cs[t]
                    sb = zero
                    scc = zero
                    dr, ur, yr = rows(da, fi, jj), rows(du, fi, jj), rows(dyin, fi, jj)
                    for l in range(LT):
                        dyr = yr[l]
                        lam = cc * dyr + g[l]
                        g[l] = a_s[t, :, sl[l]] * lam
                        dal = g[l] * h_s[t, :, sl[l]]
                        pb = lam * bb
                        pd = dal * am[l]
                        pb = pb[0:8] + pb[8:16]
                        pd = pd[0:8] + pd[8:16]
                        both = jnp.where(top4, pb, pd) + pltpu.roll(jnp.where(top4, pd, pb), 4, 0)
                        both = both + pltpu.roll(both, 6, 0)
                        both = both + pltpu.roll(both, 7, 0)
                        lb_s[fi, jj : jj + 1, sl[l]] = both[0:1]
                        dd_s[fi, jj : jj + 1, sl[l]] = both[4:5]
                        ga[l] = ga[l] + dal * dr[l]
                        sb = sb + lam * ur[l]
                        scc = scc + dyr * h_s[t + 1, :, sl[l]]
                    sb_s[l0 - j] = sb
                    sc_s[l0 - j] = scc
                return tuple(g), tuple(ga)

            g, ga = lax.fori_loop(0, LANES // 8, inner, (c[0], c[1]))
            dp_o[R : R + N, blk] = lane_sums(sb_s)
            dp_o[R + N : R + 2 * N, blk] = lane_sums(sc_s)
            return g, ga

        zeros = tuple(jnp.zeros((N, LANES), F32) for _ in range(LT))
        _, ga = lax.fori_loop(0, nb, bouter, (tuple(gin), zeros))
        for l in range(LT):
            vec_o[8 : 8 + N, sl[l]] = am[l] * ga[l]
        skr = skip[0:1, pl.ds(c0, C)]

        def block(i, tot):
            gdt, gsk = tot
            rs = pl.ds(i * RB, RB)
            r8 = pl.ds(i * (RB // 8), RB // 8)
            uf = u[rs, :].astype(F32)
            zf = z[rs, :].astype(F32)
            s = 1.0 / (1.0 + jnp.exp(-zf))
            yin = y_s[r8].reshape(RB, C) + skr * uf
            g_o[rs, :] = (yin * (zf * s)).astype(BF)
            dz_o[rs, :] = (dg[rs, :] * yin * slope_of(zf, s)).astype(BF)
            lb = lb_s[r8].reshape(RB, C)
            dyr = dyin[r8].reshape(RB, C)
            x = pre[rs, :]
            dpre = (lb * uf + dd_s[r8].reshape(RB, C)) / (1.0 + jnp.exp(-x))
            dpre_o[rs, :] = dpre.astype(BF)
            du1_o[rs, :] = dyr * skr + lb * soft(x)
            return gdt + jnp.sum(dpre, axis=0, keepdims=True), gsk + jnp.sum(dyr * uf, axis=0, keepdims=True)

        z1 = jnp.zeros((1, C), F32)
        gdt, gsk = lax.fori_loop(0, T // RB, block, (z1, z1))
        vec_o[5:6, :] = gdt
        vec_o[6:7, :] = gsk
        vec_o[7:8, :] = z1
        vec_o[0:5, :] = jnp.zeros((5, C), F32)
        dp_o[0:R, :] = dot_nt(wt[XW : XW + R, :], dpre_o[...])
        pdt_o[...] = dot_nn(pt[0:R, :].astype(BF), dpre_o[...])
        mix_o[...] = dot_nn(g_o[...], wr[:, D + LANES : 2 * D + LANES]).astype(BF)
        pw_o[:, 0:D] = dot_tn(dz_o[...], hb[...]).astype(BF)
        pw_o[:, D : 2 * D] = dot_tn(g_o[...], dy[...]).astype(BF)

    outs = [((T, C), BF), ((T, C), BF), ((T, C), F32), ((T, C), BF), ((XW, T), F32), ((T, D), BF),
            ((C, 2 * D), BF), ((R, C), F32), ((8 + N, C), F32)]
    scratch = [pltpu.VMEM((T, N, C), F32), pltpu.VMEM((T + 1, N, C), F32)] + [pltpu.VMEM((T // 8, 8, C), F32)] * 3
    scratch += [pltpu.VMEM((LANES, N, LANES), F32)] * 2 + [pltpu.VMEM((T, N, LANES), F32)] * 2
    return call(scan, outs, 14 + CT, 1, scratch)


def make_back(T, C, D, docs, XW, R):
    RB = 64

    def back(sc, da_, db_, du1, v, u, xu, xhalo, wt, cw, vec, pdt, hb, halo, dxu_o, spill_o, pxt_o, vec_o, pad1, pad2, pad3, xpad):
        c0 = pl.multiple_of(sc[0], LANES)
        dpl = (da_[...] + db_[...]).astype(BF)
        pxt_o[:, D : D + LANES] = jnp.concatenate([dot_nn(dpl, u[...]), pdt[...]], axis=0).T.astype(BF)
        dxu_o[...] = du1[...] + dot_tn(dpl, wt[0:XW, :])
        pads = {1: pad1, 2: pad2, 3: pad3}
        xpad[0:8, :] = xhalo[...]
        xpad[8 : 8 + T, :] = xu[...].astype(F32)
        taps = [cw[k : k + 1, pl.ds(c0, C)] for k in range(4)]
        z8 = jnp.zeros((8, C), F32)
        for s in (1, 2, 3):
            pads[s][0:8, :] = z8
            pads[s][8 + T : 16 + T, :] = z8

        def block(i, tot):
            r0 = i * RB
            rs = pl.ds(r0, RB)
            p = rows_iota(r0, RB)
            vf = v[rs, :]
            sg = 1.0 / (1.0 + jnp.exp(-vf))
            dv = dxu_o[rs, :] * slope_of(vf, sg)
            new = [None] * 5
            full = xpad[pl.ds(r0, RB + 8), :]
            new[4] = tot[4] + jnp.sum(dv, axis=0, keepdims=True)
            for k in range(4):
                s = 3 - k
                x = full[8 - s : 8 - s + RB]
                m = dv
                if s:
                    m = dv * wide(tap_mask(sc, docs, p, s), C)
                    pads[s][pl.ds(8 + r0, RB), :] = taps[k] * m
                else:
                    dxu_o[rs, :] = taps[k] * m
                new[k] = tot[k] + jnp.sum(m * x, axis=0, keepdims=True)
            return tuple(new)

        z1 = jnp.zeros((1, C), F32)
        tot = lax.fori_loop(0, T // RB, block, (z1,) * 5)
        vec_o[...] = vec[...]
        for k in range(5):
            vec_o[k : k + 1, :] = tot[k]

        def gather(i, c):
            r0 = i * RB
            rs = pl.ds(r0, RB)
            acc = dxu_o[rs, :]
            for s in (1, 2, 3):
                acc = acc + pads[s][pl.ds(8 + r0, RB + 8), :][s : s + RB]
            dxu_o[rs, :] = acc
            return c

        lax.fori_loop(0, T // RB, gather, 0)
        acc = z8
        for s in (1, 2, 3):
            acc = acc + pads[s][s : s + 8, :]
        spill_o[...] = acc
        own = dot_tn(dxu_o[...].astype(BF), hb[...])
        pxt_o[:, 0:D] = (own + dot_tn(acc.astype(BF), halo[...])).astype(BF)

    outs = [((T, C), F32), ((8, C), F32), ((C, D + LANES), BF), (None, F32)]

    def build(vrows):
        o = outs[:3] + [((vrows, C), F32)]
        return call(back, o, 14, 1, [pltpu.VMEM((T + 16, C), F32)] * 3 + [pltpu.VMEM((T + 8, C), F32)])

    return build


def make_last(T, C, D, Q):
    def last(dxu, spill, dz, wa, wr, mix, x, rt, keep_o, send_o, gain_o):
        low = jnp.concatenate([jnp.zeros((T - 8, C), F32), spill[...]], axis=0)
        dx = (dxu[...] + low).astype(BF)
        dn = dot_nn(dx, wa[...]) + dot_nn(dz[...], wr[:, 0:D])
        xf = x[...].astype(F32)
        inv = lax.rsqrt(jnp.mean(xf * xf, axis=1, keepdims=True) + NORM_EPS)
        gain_o[...] = jnp.sum(dn * xf * inv, axis=0, keepdims=True)
        dnl = dn.astype(BF)
        for e in range(T // Q):
            r = rt[:, e * Q : (e + 1) * Q]
            o = send_o if e % 2 else keep_o
            at = slice((e // 2) * Q, (e // 2 + 1) * Q)
            o[at, 0:D] = dot_tn(r, mix[...]).astype(BF)
            o[at, D : 2 * D] = dot_tn(r, dnl).astype(BF)

    half = T // 2
    outs = [((half, 2 * D), BF), ((half, 2 * D), BF), ((1, D), F32)]
    return call(last, outs, 8, 0)


def flat_slots(k, shift, share, first, here):
    return ((k >> shift) ^ here) * share + first + (k & ((1 << shift) - 1))


def chunk_shape(T, CT, TP):
    share = T // CT
    SR = share // TP
    shift = SR.bit_length() - 1
    assert SR == 1 << shift and T // TP == CT * SR
    return T // TP, share, SR, shift


def make_send(T, D, CT, TP):
    Q, share, SR, shift = chunk_shape(T, CT, TP)

    def send(rsc, perm, x, dy, buf_o, pos_o):
        c = rsc[0]
        tp = rsc[1]
        own = perm[0:1, pl.ds(pl.multiple_of(c * T, LANES), T)].astype(F32)
        r = lax.broadcasted_iota(jnp.int32, (T, T), 0)
        q = lax.broadcasted_iota(jnp.int32, (T, T), 1)
        row = jnp.broadcast_to(own, (T, T))
        col = jnp.broadcast_to(jnp.sum(jnp.where(r == q, row, 0.0), axis=1, keepdims=True), (T, T))
        pos_row = jnp.sum(jnp.where(col < row, 1.0, 0.0), axis=0, keepdims=True)
        k = lax.broadcasted_iota(jnp.int32, (Q, T), 0)
        slot = flat_slots(k, shift, share, SR * tp, c).astype(F32)
        pick = jnp.where(slot == pos_row, 1.0, 0.0).astype(BF)
        buf_o[:, 0:D] = dot_nn(pick, x[...]).astype(BF)
        buf_o[:, D : 2 * D] = dot_nn(pick, dy[...]).astype(BF)
        pos_o[...] = pos_row

    return call(send, [((Q, 2 * D), BF), ((1, T), F32)], 4, 1)


def make_plan(T, CT, TP):
    Q, share, SR, shift = chunk_shape(T, CT, TP)

    def plan(rsc, perm, pos, rt_o, fin_o):
        c = rsc[0]
        tp = rsc[1]
        r = lax.broadcasted_iota(jnp.int32, (T, T), 0)
        q = lax.broadcasted_iota(jnp.int32, (T, T), 1)
        place = r + c * T
        lane = lax.broadcasted_iota(jnp.int32, (T, LANES), 1)
        hot = jnp.zeros((T, LANES), F32)
        for s in range(CT):
            src = jnp.broadcast_to(perm[0:1, s * T : (s + 1) * T], (T, T))
            n = jnp.sum(jnp.where(src == place, 1.0, 0.0), axis=1, keepdims=True)
            hot = jnp.where(lane == s, n, hot)
        below = jnp.where(q < r, 1.0, 0.0).astype(BF)
        count = dot_nn(below, hot.astype(BF))
        rank = jnp.sum(hot * count, axis=1, keepdims=True)
        block = jnp.sum(hot * lane.astype(F32), axis=1, keepdims=True)
        want = block * share + rank
        back = jnp.sum(jnp.where(r == q, jnp.broadcast_to(pos[...], (T, T)), 0.0), axis=1, keepdims=True)
        f = lax.broadcasted_iota(jnp.int32, (T, Q), 1)
        for e in range(TP):
            slot = flat_slots(f, shift, share, SR * (tp ^ e), c).astype(F32)
            rt_o[:, e * Q : (e + 1) * Q] = jnp.where(slot == want, 1.0, 0.0).astype(BF)
            fin_o[:, e * Q : (e + 1) * Q] = jnp.where(slot == back, 1.0, 0.0).astype(BF)

    return call(plan, [((T, T), BF)] * 2, 3, 1)


def make_recv(T, D, TP):
    Q = T // TP

    def recv(rt, gain, *rest):
        parts = rest[:TP]
        x_o, dy_o, hb_o = rest[TP:]
        xa = jnp.zeros((T, D), F32)
        ya = jnp.zeros((T, D), F32)
        for e in range(TP):
            m = rt[:, e * Q : (e + 1) * Q]
            xa = xa + dot_nn(m, parts[e][:, 0:D])
            ya = ya + dot_nn(m, parts[e][:, D : 2 * D])
        x_o[...] = xa.astype(BF)
        dy_o[...] = ya.astype(BF)
        inv = lax.rsqrt(jnp.mean(xa * xa, axis=1, keepdims=True) + NORM_EPS)
        hb_o[...] = (xa * inv * gain[...]).astype(BF)

    return call(recv, [((T, D), BF)] * 3, 2 + TP, 0)


def make_norm_back(Q, D):
    def norm_back(keep, got, far, own, gain, o):
        both = keep[0:Q].astype(F32) + got[0:Q].astype(F32) + far[...].astype(F32)
        xf = own[:, 0:D].astype(F32)
        inv = lax.rsqrt(jnp.mean(xf * xf, axis=1, keepdims=True) + NORM_EPS)
        dn = both[:, D : 2 * D]
        scaled = gain[...] * dn
        mean = jnp.mean(scaled * xf, axis=1, keepdims=True)
        o[:, 0:D] = (xf + both[:, 0:D]).astype(BF)
        o[:, D : 2 * D] = (
            own[:, D : 2 * D].astype(F32) + inv * scaled - xf * (inv * inv * inv) * mean
        ).astype(BF)

    return call(norm_back, [((Q, 2 * D), BF)], 5, 0)


def make_final(T, D, TP):
    Q = T // TP

    def final(fin, *rest):
        out_o, grad_o = rest[TP:]
        a = jnp.zeros((T, D), F32)
        b = jnp.zeros((T, D), F32)
        for e in range(TP):
            m = fin[:, e * Q : (e + 1) * Q]
            a = a + dot_nn(m, rest[e][:, 0:D])
            b = b + dot_nn(m, rest[e][:, D : 2 * D])
        out_o[...] = a.astype(BF)
        grad_o[...] = b.astype(BF)

    return call(final, [((T, D), BF)] * 2, 1 + TP, 0)


def halves(x):
    hi = x.astype(BF)
    return hi, (x - hi.astype(F32)).astype(BF)


def mul3(ah, al, bh, bl):
    return dot_nn(ah, bh) + (dot_nn(ah, bl) + dot_nn(al, bh))


def gram3(parts):
    def rows_of(i, b, n):
        at = slice(i * b, (i + 1) * b)
        tail = slice(i * b, n)
        tot = None
        for h, l in parts:
            one = dot_tn(h[:, at], h[:, tail]) + (dot_tn(h[:, at], l[:, tail]) + dot_tn(l[:, at], h[:, tail]))
            tot = one if tot is None else tot + one
        return tot

    return rows_of


def put_gram(o, parts, n):
    b = n // 3
    rows_of = gram3(parts)
    o[0:b, :] = rows_of(0, b, n)
    o[b : 2 * b, 0 : 2 * b] = rows_of(1, b, n)
    o[b : 2 * b, 2 * b : n] = rows_of(2, b, n)


def momentum_step(gradient, momentum_old):
    momentum_new = MOMENTUM * momentum_old + gradient
    return (momentum_new, gradient + MOMENTUM * momentum_new)


def make_gram_out(rows, D):
    def gram_out(got, mom, g1_o, go_o, mo_o, uo_o, gram_o):
        g1_o[...] = got[:, 0:D]
        g = got[:, D : 2 * D]
        m, u = momentum_step(g, mom[...])
        go_o[...] = g
        mo_o[...] = m
        uo_o[...] = u
        put_gram(gram_o, [halves(u)], D)

    outs = [((rows, D), F32)] * 4 + [((2 * D // 3, D), F32)]
    return call(gram_out, outs, 2, 0)


def make_gram_in(rows, D, XW, R, VR, pack, full):
    b = D // 3
    top = 2 * b

    def gram_in(place, got, g1, mom, xm, dm, vec, go, uo, gi_o, mi_o, gx_o, mx_o, gd_o, md_o, mine_o, away_o, um_o, ua_o, tmp):
        even = (place[1] & 1) == 0
        parts = []
        us = []
        for q in range(2):
            g = got[:, 0:D] if q == 0 else g1[...]
            m, u = momentum_step(g, mom[:, q, :])
            gi_o[:, q, :] = g
            mi_o[:, q, :] = m
            us.append(u)
            parts.append(halves(u))
        put_gram(tmp, parts, D)
        g = got[:, D : D + LANES]
        m, u = momentum_step(g, jnp.concatenate([xm[...], dm[...]], axis=1))
        gx_o[...] = g[:, 0:XW]
        gd_o[...] = g[:, XW : XW + R]
        mx_o[...] = m[:, 0:XW]
        md_o[...] = m[:, XW : XW + R]
        h, l = halves(u)
        small = dot_tn(h, h) + (dot_tn(h, l) + dot_tn(l, h))

        def put_in(buf, ub):
            buf[0:top, :] = tmp[...]
            buf[top : top + VR, :] = vec[...]
            if full > top + VR:
                buf[top + VR : full, :] = jnp.zeros((full - top - VR, D), F32)
            ub[0:rows, :] = us[0]
            ub[rows : 2 * rows, :] = us[1]

        def put_out(buf, ub):
            buf[0:top, :] = go[...]
            buf[top:full, :] = jnp.zeros((full - top, D), F32)
            for k in range(-(-LANES // pack)):
                lo = k * pack
                hi = min(lo + pack, LANES)
                buf[top : top + hi - lo, k * LANES : (k + 1) * LANES] = small[lo:hi]
            ub[0:rows, :] = uo[...]
            ub[rows : 2 * rows, :] = jnp.zeros((rows, D), F32)
            ub[rows : 2 * rows, 0:LANES] = u

        @pl.when(even)
        def _():
            put_in(mine_o, um_o)
            put_out(away_o, ua_o)

        @pl.when(jnp.logical_not(even))
        def _():
            put_out(mine_o, um_o)
            put_in(away_o, ua_o)

    outs = [((rows, 2, D), F32)] * 2
    outs += [((rows, XW), F32)] * 2 + [((rows, R), F32)] * 2 + [((full, D), F32)] * 2 + [((2 * rows, D), F32)] * 2
    return call(gram_in, outs, 9, 1, [pltpu.VMEM((top, D), F32)])


class Polar:
    def __init__(self, n, nbk, cuts, refs):
        self.n, self.nbk, self.cuts = n, nbk, list(cuts)
        self.blocks = n // nbk
        self.ah, self.al, self.qh, self.ql, self.th, self.tl, self.xs, self.acc = refs

    @staticmethod
    def scratch(n, rows):
        return [pltpu.VMEM((n, n), BF)] * 6 + [pltpu.VMEM((rows, n), F32), pltpu.VMEM((n, n), F32)]

    def at(self, b):
        return slice(b * self.nbk, (b + 1) * self.nbk)

    def put(self, i, value, hi_ref, lo_ref):
        h, l = halves(value)
        b = self.nbk
        hi_ref[self.at(i), i * b : self.n] = h
        lo_ref[self.at(i), i * b : self.n] = l
        for j in range(i + 1, self.blocks):
            h, l = halves(value[:, (j - i) * b : (j - i + 1) * b].T)
            hi_ref[self.at(j), self.at(i)] = h
            lo_ref[self.at(j), self.at(i)] = l

    def start(self, tails, upd):
        n, b = self.n, self.nbk
        col = lax.broadcasted_iota(jnp.int32, (1, n), 1)
        edges = [0] + self.cuts
        inv = jnp.zeros((1, n), F32)
        r = lax.broadcasted_iota(jnp.int32, (b, b), 0)
        c = lax.broadcasted_iota(jnp.int32, (b, b), 1)
        for lo, hi in zip(edges[:-1], edges[1:]):
            tot = jnp.zeros((1, 1), F32)
            for k in range(self.blocks):
                inside = (r == c) & (r + k * b >= lo) & (r + k * b < hi)
                d = jnp.sum(jnp.where(inside, tails[k][:, 0:b], 0.0), axis=1, keepdims=True)
                tot = tot + jnp.sum(d, axis=0, keepdims=True)
            inv = jnp.where((col >= lo) & (col < hi), 1.0 / (jnp.sqrt(tot) + 1e-07), inv)
        self.xs[...] = upd * inv
        for i in range(self.blocks):
            g = tails[i]
            if len(self.cuts) > 1:
                r = lax.broadcasted_iota(jnp.int32, g.shape, 0) + i * b
                c = lax.broadcasted_iota(jnp.int32, g.shape, 1) + i * b
                same = jnp.zeros(g.shape, F32)
                for lo, hi in zip(edges[:-1], edges[1:]):
                    same = jnp.where((r >= lo) & (r < hi) & (c >= lo) & (c < hi), 1.0, same)
                g = g * same
            one = inv[:, i * b : n]
            a = g * (one * one)
            self.acc[self.at(i), i * b : n] = a
            self.put(i, a, self.ah, self.al)

    def factor(self):
        for i in range(self.blocks):
            tail = slice(i * self.nbk, self.n)
            a2 = mul3(self.ah[self.at(i), :], self.al[self.at(i), :], self.ah[:, tail], self.al[:, tail])
            r = lax.broadcasted_iota(jnp.int32, a2.shape, 0)
            c = lax.broadcasted_iota(jnp.int32, a2.shape, 1)
            q = jnp.where(r == c, NS_A, 0.0) + (NS_B * self.acc[self.at(i), tail] + NS_C * a2)
            self.put(i, q, self.qh, self.ql)

    def apply(self):
        self.factor()
        h, l = halves(self.xs[...])
        self.xs[...] = mul3(h, l, self.qh[...], self.ql[...])

    def advance(self):
        self.factor()
        for src, dst in (((self.ah, self.al), (self.th, self.tl)), ((self.th, self.tl), (self.ah, self.al))):
            for i in range(self.blocks):
                tail = slice(i * self.nbk, self.n)
                h, l = src[0][self.at(i), :], src[1][self.at(i), :]
                joined = i == 0 and src[0] is self.ah
                if joined:
                    xh, xl = halves(self.xs[...])
                    h, l = jnp.concatenate([h, xh], axis=0), jnp.concatenate([l, xl], axis=0)
                a = mul3(h, l, self.qh[:, tail], self.ql[:, tail])
                if joined:
                    self.xs[...] = a[self.nbk :]
                    a = a[0 : self.nbk]
                if dst[0] is self.ah:
                    self.acc[self.at(i), tail] = a
                self.put(i, a, *dst)


def unpack_gram(buf, n):
    b = n // 3
    return [buf[0:b, :], buf[b : 2 * b, 0 : 2 * b], buf[b : 2 * b, 2 * b : n]]


def make_muon(D, rows, XW, R, pack, full):
    top = 2 * (D // 3)

    def muon(buf, um, ua, xm_o, xa_o, *refs):
        p = Polar(D, D // 3, (D,), refs[:8])
        s = Polar(LANES, LANES, (XW, XW + R), refs[8:16])
        small = jnp.concatenate(
            [
                buf[top : top + min(pack, LANES - k * pack), k * LANES : (k + 1) * LANES]
                for k in range(-(-LANES // pack))
            ],
            axis=0,
        )
        p.start(unpack_gram(buf, D), jnp.concatenate([um[...], ua[...]], axis=0))
        s.start([small], jnp.concatenate([um[rows:, 0:LANES], ua[rows:, 0:LANES]], axis=0))

        def step(k, c):
            p.advance()
            s.advance()
            return c

        lax.fori_loop(0, 4, step, 0)
        p.apply()
        s.apply()
        xm_o[...] = p.xs[0 : 2 * rows, :]
        xa_o[0:rows, :] = p.xs[2 * rows : 3 * rows, :]
        xa_o[rows : 2 * rows, :] = p.xs[3 * rows : 4 * rows, :]
        return s

    def body(place, buf, um, ua, xm_o, xa_o, *refs):
        s = muon(buf, um, ua, xm_o, xa_o, *refs)

        @pl.when((place[1] & 1) == 1)
        def _():
            xm_o[rows : 2 * rows, 0:LANES] = s.xs[0:rows, :]
            xa_o[rows : 2 * rows, 0:LANES] = s.xs[rows : 2 * rows, :]

    body.__name__ = "muon"
    scratch = Polar.scratch(D, 4 * rows) + Polar.scratch(LANES, 2 * rows)
    return call(body, [((2 * rows, D), F32)] * 2, 4, 1, scratch)


def make_finish(rows, D, XW, R, rates):
    def finish(place, xm, xr, wi, wx, wd, wo, oi, ox, od, oo):
        even = (place[1] & 1) == 0
        for q in range(2):
            at = slice(q * rows, (q + 1) * rows)
            oi[:, q, :] = wi[:, q, :] - rates[0] * jnp.where(even, xm[at], xr[at])
        oo[...] = wo[...] - rates[3] * jnp.where(even, xr[0:rows], xm[0:rows])
        s = jnp.where(even, xr[rows:, 0:LANES], xm[rows:, 0:LANES])
        ox[...] = wx[...] - rates[1] * s[:, 0:XW]
        od[...] = wd[...] - rates[2] * s[:, XW : XW + R]

    outs = [((rows, 2, D), F32), ((rows, XW), F32), ((rows, R), F32), ((rows, D), F32)]
    return call(finish, outs, 7, 1)


def make_pack(rows, D, XW, R):
    def pack(wi, wx, wd, wo, a_o, r_o):
        a_o[...] = wi[:, 0, :].astype(BF)
        r_o[:, 0:D] = wi[:, 1, :].astype(BF)
        r_o[:, D : D + LANES] = jnp.concatenate([wx[...], wd[...]], axis=1).astype(BF)
        r_o[:, D + LANES : 2 * D + LANES] = wo[...].astype(BF)

    return call(pack, [((rows, D), BF), ((rows, 2 * D + LANES), BF)], 4, 0)


def shifted(value, axis, by):
    devices = lax.axis_size(axis)
    pairs = [(i, i + by) for i in range(devices) if 0 <= i + by < devices]
    return lax.ppermute(value, axis, pairs)


def swap(value, axis, bit):
    devices = lax.axis_size(axis)
    return lax.ppermute(value, axis, [(i, i ^ bit) for i in range(devices)])


def side(axis, bit):
    return jnp.where((lax.axis_index(axis) & bit) != 0, 1, 0)


def in_order(mine, theirs, axis, bit):
    low = side(axis, bit) == 0
    return jnp.concatenate([jnp.where(low, mine, theirs), jnp.where(low, theirs, mine)], axis=0)


def half_sum(value, axis, bit):
    half = value.shape[0] // 2
    mine = side(axis, bit) * half
    away = lax.dynamic_slice_in_dim(value, half - mine, half)
    kept = lax.dynamic_slice_in_dim(value, mine, half)
    return kept + swap(away, axis, bit)


def half_join(value, axis, bit):
    return in_order(value, swap(value, axis, bit), axis, bit)


def bits_of(axis):
    count = lax.axis_size(axis)
    return [1 << k for k in range(count.bit_length() - 1)]


def sum_rest(value):
    cols = value.shape[1] // 2
    done = []
    for k in range(2):
        part = value[:, k * cols : (k + 1) * cols]
        cut = [("tp", 2), ("fsdp", 1), ("ctx", 1)] if k == 0 else [("fsdp", 1), ("tp", 2), ("ctx", 1)]
        rest = [(a, b) for a in ("tp", "fsdp", "ctx") for b in bits_of(a) if (a, b) not in cut + [("tp", 1)]]
        for axis, bit in cut:
            part = half_sum(part, axis, bit)
        for axis, bit in rest:
            part = part + swap(part, axis, bit)
        for axis, bit in cut[::-1]:
            part = half_join(part, axis, bit)
        done.append(part)
    return jnp.concatenate(done, axis=1)


def to_owners(value, rows, axes=("fsdp", "ctx")):
    steps = [(a, b) for a in axes for b in bits_of(a)[:: -1 if a == "fsdp" else 1]]
    for axis, bit in steps:
        if axis == "fsdp":
            value = value.reshape(1, 2, value.shape[0] // 2, value.shape[1])
        else:
            value = value.reshape(value.shape[0] // (2 * rows), 2, rows, value.shape[1])
        mine = side(axis, bit)
        away = lax.dynamic_slice_in_dim(value, 1 - mine, 1, 1).astype(BF)
        kept = lax.dynamic_slice_in_dim(value, mine, 1, 1)
        value = kept.astype(F32) + swap(away, axis, bit).astype(F32)
        value = value.reshape(-1, value.shape[3])
    return value


def over_ctx(value):
    count = lax.axis_size("ctx")
    rows = value.shape[0] // count
    parts = [value[d * rows : (d + 1) * rows] for d in range(count)]
    return jnp.concatenate([parts[0]] + [swap(parts[d], "ctx", d) for d in range(1, count)], axis=0)


def doubled(value, axes):
    steps = [(a, b) for a in axes for b in bits_of(a)]
    for axis, bit in steps[:-1]:
        value = jnp.concatenate([value, swap(value, axis, bit)], axis=0)
    return value, swap(value, *steps[-1])


def adam_update(parameters, gradient, moment_one, moment_two, adam_step):
    count = adam_step[0].astype(jnp.float32)
    first_new = BETA_ONE * moment_one + (1.0 - BETA_ONE) * gradient
    second_new = BETA_TWO * moment_two + (1.0 - BETA_TWO) * gradient * gradient
    first_hat = first_new / (1.0 - jnp.power(jnp.float32(BETA_ONE), count))
    second_hat = second_new / (1.0 - jnp.power(jnp.float32(BETA_TWO), count))
    updated = parameters - ADAM_RATE * (
        first_hat / (jnp.sqrt(second_hat) + ADAM_EPS) + DECAY_RATE * parameters
    )
    return (updated, first_new, second_new)


def on_device(
    block_input,
    cotangent,
    route_perm,
    doc_lengths,
    norm_gain,
    in_proj,
    conv_weight,
    conv_bias,
    x_proj,
    dt_proj,
    dt_bias,
    a_log,
    skip_gain,
    out_proj,
    in_momentum,
    x_momentum,
    dt_momentum,
    out_momentum,
    adam_first,
    adam_second,
    adam_step,
):
    ctx_count = lax.axis_size("ctx")
    fsdp_count = lax.axis_size("fsdp")
    tp_count = lax.axis_size("tp")
    owners = fsdp_count * ctx_count
    ctx_index = lax.axis_index("ctx")
    tp_index = lax.axis_index("tp")
    tokens, width = block_input.shape
    stream = tokens * ctx_count
    quarter = tokens // tp_count
    own_rows = in_proj.shape[0]
    channels = own_rows * owners
    inner = conv_bias.shape[0]
    states = a_log.shape[0]
    rank = dt_proj.shape[1]
    xw = x_proj.shape[1]
    lengths = doc_lengths[0]
    docs = lengths.shape[0]
    offsets = jnp.cumsum(lengths) - lengths
    scal = jnp.concatenate(
        [(tp_index * channels)[None], offsets - ctx_index * tokens, ctx_index[None], lax.axis_index("fsdp")[None]]
    ).astype(jnp.int32)
    place = jnp.stack([ctx_index, tp_index]).astype(jnp.int32)
    perm_row = (route_perm % stream).reshape(1, stream)
    gain_row = norm_gain.reshape(1, width)

    w_a, w_r = make_pack(own_rows, width, xw, rank)(in_proj, x_proj, dt_proj, out_proj)
    send, send_pos = make_send(tokens, width, ctx_count, tp_count)(place, perm_row, block_input, cotangent)
    own = over_ctx(send)
    swapped = own_rows % 16 == 0
    if swapped:
        parts_in = doubled(w_a, ("fsdp", "ctx"))
        parts_rest = doubled(w_r, ("ctx", "fsdp"))
    else:
        half = channels // 2
        full_in, full_rest = [lax.all_gather(w, ("fsdp", "ctx"), axis=0, tiled=True) for w in (w_a, w_r)]
        parts_in = (full_in[:half], full_in[half:])
        parts_rest = (full_rest[:half], full_rest[half:])
    route, fin = make_plan(tokens, ctx_count, tp_count)(place, perm_row, send_pos)
    far = swap(own, "tp", 2)
    stream_x, stream_dy, normed = make_recv(tokens, width, tp_count)(
        route, gain_row, own, swap(own, "tp", 1), far, swap(far, "tp", 1)
    )

    halo = shifted(normed[tokens - 8 :], "ctx", 1)
    w_in, w_rest, conv_in, gate_in, conv_act, conv_out, pt_part, d_gated, w_turn, x_halo = make_front(
        tokens, channels, width, docs, xw, rank, ctx_count, fsdp_count, swapped
    )(scal, normed, halo, stream_dy, *parts_in, *parts_rest, conv_weight, conv_bias.reshape(1, inner))
    pt_pair = pt_part + swap(pt_part, "tp", 1)
    pt, dec, drv, d_inner, pre, ends = make_carry(
        tokens, channels, docs, xw, rank, states, ctx_count
    )(scal, pt_pair, swap(pt_pair, "tp", 2), conv_act, gate_in, d_gated, w_turn, dt_bias.reshape(1, inner), a_log)
    ends = [swap(ends[d], "ctx", d) for d in range(1, ctx_count)]
    gate_low, d_gate, du_one, d_pre_low, dp_part, mix_part, grads_one, part_dt, vec_part = make_scan(
        tokens, channels, width, docs, xw, rank, states, ctx_count
    )(
        scal, pt, dec, drv, d_inner, pre, conv_act, gate_in, d_gated, stream_dy, normed, w_rest, w_turn, a_log,
        skip_gain.reshape(1, inner), *ends,
    )

    got_one = to_owners(grads_one, own_rows)
    dp_pair = dp_part + swap(dp_part, "tp", 1)
    d_conv_in, spill, grads_two, vec_chan = make_back(tokens, channels, width, docs, xw, rank)(8 + states)(
        scal, dp_pair, swap(dp_pair, "tp", 2), du_one, conv_out, conv_act, conv_in, x_halo, w_turn, conv_weight,
        vec_part, part_dt, normed, halo,
    )
    two = to_owners(grads_two, own_rows, ("fsdp",))
    keep, away, g_gain = make_last(tokens, channels, width, quarter)(
        d_conv_in, shifted(spill, "ctx", -1), d_gate, w_in, w_rest, mix_part, stream_x, route
    )

    near = swap(away, "tp", 1)
    cross = (keep[quarter:].astype(F32) + near[quarter:].astype(F32)).astype(BF)
    two, cross = lax.optimization_barrier((two, cross))
    got_two = to_owners(two, own_rows, ("ctx",))
    back = make_norm_back(quarter, width)(keep, near, swap(cross, "tp", 2), own, gain_row)[0]
    got_two, back = lax.optimization_barrier((got_two, back))
    home = over_ctx(back)
    home_far = swap(home, "tp", 2)
    block_out, input_grad = make_final(tokens, width, tp_count)(
        fin, home, swap(home, "tp", 1), home_far, swap(home_far, "tp", 1)
    )

    kinds = 8 + states
    pack = 24
    vec_wide = lax.dynamic_update_slice(jnp.zeros((kinds, inner), F32), vec_chan, (0, tp_index * channels))
    vec_wide = vec_wide + jnp.pad(g_gain, ((7, kinds - 8), (0, inner - width)))
    vec_rows = kinds * inner // width
    g_one, g_out, mom_out, upd_out, gram_out = make_gram_out(own_rows, width)(got_one, out_momentum)
    top = 2 * (width // 3)
    full = -(-(top + max(vec_rows, pack)) // 64) * 64
    g_in, mom_in, g_x, mom_x, g_dt, mom_dt, gram_mine, gram_away, upd_mine, upd_away = make_gram_in(
        own_rows, width, xw, rank, vec_rows, pack, full
    )(place, got_two, g_one, in_momentum, x_momentum, dt_momentum, vec_wide.reshape(vec_rows, width), gram_out, upd_out)
    gram = sum_rest(gram_mine + swap(gram_away, "tp", 1))
    x_mine, x_away = make_muon(width, own_rows, xw, rank, pack, full)(place, gram, upd_mine, swap(upd_away, "tp", 1))
    rates = [MUON_RATE * 0.2 * math.sqrt(max(a, b)) for a, b in ((2 * inner, width), (inner, xw), (inner, rank), (inner, width))]
    new_in, new_x, new_dt, new_out = make_finish(own_rows, width, xw, rank, rates)(
        place, x_mine, swap(x_away, "tp", 1), in_proj, x_proj, dt_proj, out_proj
    )
    vec_own = gram[top : top + vec_rows]
    vec_sum = jnp.where((tp_index & 1) == 0, vec_own, swap(vec_own, "tp", 1)).reshape(kinds, inner)
    g_alog = vec_sum[8:]
    vec_grads = jnp.concatenate(
        [vec_sum[7, :width], vec_sum[0:4].reshape(-1), vec_sum[4], vec_sum[5], g_alog.reshape(-1), vec_sum[6]]
    )
    vec_params = jnp.concatenate(
        [norm_gain, conv_weight.reshape(-1), conv_bias, dt_bias, a_log.reshape(-1), skip_gain]
    )
    new_vec, first_new, second_new = adam_update(vec_params, vec_grads, adam_first, adam_second, adam_step)
    cut_b = width + 4 * inner
    cut_c = cut_b + inner
    cut_d = cut_c + inner
    cut_e = cut_d + states * inner
    return (
        block_out,
        input_grad,
        vec_sum[7, :width],
        g_in,
        vec_sum[0:4],
        vec_sum[4],
        g_x,
        g_dt,
        vec_sum[5],
        g_alog,
        vec_sum[6],
        g_out,
        new_vec[:width],
        new_in,
        new_vec[width:cut_b].reshape(4, inner),
        new_vec[cut_b:cut_c],
        new_x,
        new_dt,
        new_vec[cut_c:cut_d],
        new_vec[cut_d:cut_e].reshape(states, inner),
        new_vec[cut_e:],
        new_out,
        mom_in,
        mom_x,
        mom_dt,
        mom_out,
        first_new,
        second_new,
    )


def solution(mesh):
    return jax.shard_map(
        on_device,
        mesh=mesh,
        in_specs=(
            P(("fsdp", "ctx"), None),
            P(("fsdp", "ctx"), None),
            P("fsdp"),
            P("fsdp", None),
            P(),
            P(("tp", "fsdp", "ctx"), None, None),
            P(),
            P(),
            P(("tp", "fsdp", "ctx"), None),
            P(("tp", "fsdp", "ctx"), None),
            P(),
            P(),
            P(),
            P(("tp", "fsdp", "ctx"), None),
            P(("tp", "fsdp", "ctx"), None, None),
            P(("tp", "fsdp", "ctx"), None),
            P(("tp", "fsdp", "ctx"), None),
            P(("tp", "fsdp", "ctx"), None),
            P(),
            P(),
            P(),
        ),
        out_specs=(
            P(("fsdp", "ctx"), None),
            P(("fsdp", "ctx"), None),
            P(),
            P(("tp", "fsdp", "ctx"), None, None),
            P(),
            P(),
            P(("tp", "fsdp", "ctx"), None),
            P(("tp", "fsdp", "ctx"), None),
            P(),
            P(),
            P(),
            P(("tp", "fsdp", "ctx"), None),
            P(),
            P(("tp", "fsdp", "ctx"), None, None),
            P(),
            P(),
            P(("tp", "fsdp", "ctx"), None),
            P(("tp", "fsdp", "ctx"), None),
            P(),
            P(),
            P(),
            P(("tp", "fsdp", "ctx"), None),
            P(("tp", "fsdp", "ctx"), None, None),
            P(("tp", "fsdp", "ctx"), None),
            P(("tp", "fsdp", "ctx"), None),
            P(("tp", "fsdp", "ctx"), None),
            P(),
            P(),
        ),
        check_vma=False,
    )
```
